32 devices in a mesh: seq: 4 (over y, x), dp: 8 (over z, core).
Axes of the slice: x: 2, y: 2, z: 4, core: 2. Of those that a mesh axis runs over, the one named last changes fastest.
Arguments:
- tokens: bfloat16 [8, 2048, 768], P('dp', 'seq'), may hold values from -6 to 6
- doc_start: int32 [8, 2048], P('dp'), may hold values from 0 to 2047, as said below
- cotangent: bfloat16 [8, 2048, 768], P('dp', 'seq'), may hold values from -6 to 6
- norm_one: float32 [768], replicated, may hold values from 0.5 to 1.5
- w_qkv: bfloat16 [768, 2304], replicated, may hold values from -0.21875 to 0.21875
- w_out: bfloat16 [768, 768], replicated, may hold values from -0.875 to 0.875
- norm_two: float32 [768], replicated, may hold values from 0.5 to 1.5
- w_in: bfloat16 [768, 2304], replicated, may hold values from -0.21875 to 0.21875
- w_down: bfloat16 [1152, 768], replicated, may hold values from -0.1875 to 0.1875
Outputs:
- result: bfloat16 [8, 2048, 768], P('dp', 'seq')
- grad_tokens: float32 [8, 2048, 768], P('dp', 'seq')
- grad_norm_one: float32 [768], replicated
- grad_w_qkv: float32 [768, 2304], replicated
- grad_w_out: float32 [768, 768], replicated
- grad_norm_two: float32 [768], replicated
- grad_w_in: float32 [768, 2304], replicated
- grad_w_down: float32 [1152, 768], replicated
The draws below stay inside these ranges and needn't reach their ends.
Inputs may be any that keep to these rules, and one draw needn't show every extreme that they name: Documents are contiguous: doc_start of a token is the place of the first token of its run of equal values, which begins at a place equal to that value; every row begins a document at 0 and ends with a document of one token at place 2048 - 1, and in every row one document starts before 2048 / 8 and runs to place 7 * 256 - 1 or further.
All inputs are finite; a program needn't handle non-finite values.
Results may differ from the reference program's by a relative error of at most 0.013.
Values may be sent and summed in bfloat16 or wider, within the bound.
No kernel may reach another device: no remote copies, remote signals or barrier semaphores. Data moves between devices by JAX's collectives and lax.ppermute only.
A program may use at most 128 MiB of HBM per device.

```python
import jax
import jax.numpy as jnp
from jax import lax

D = 768
HEADS = 12
HEAD_DIM = 64
FF = 1152
SEQLEN = 2048
ROWS = 8


def draw_doc_start(key, part):
    key_first, key_last, key_coin = jax.random.split(jax.random.fold_in(key, 7), 3)
    first_cut = jax.random.randint(key_first, (ROWS, 1), 1, SEQLEN // 8)
    last_cut = jax.random.randint(key_last, (ROWS, 1), 7 * SEQLEN // 8, SEQLEN)
    places = jnp.arange(SEQLEN, dtype=jnp.int32)[None, :]
    coins = jax.random.randint(key_coin, (ROWS, SEQLEN), 0, 24)
    cutting = (coins == 0) & ((places < first_cut) | (places > last_cut))
    cutting = cutting | (places == 0) | (places == first_cut) | (places == last_cut) | (places == SEQLEN - 1)
    return lax.cummax(jnp.where(cutting, places, 0), axis=1).astype(jnp.int32)


def level_of(stream_key, extent, pieces, low, high):
    def one(position, shards_of):
        steps = jax.random.uniform(jax.random.fold_in(jax.random.fold_in(stream_key, 6), position), (shards_of,), jnp.float32, low / len(pieces), high / len(pieces))
        return jnp.repeat(jnp.exp(steps), extent[position] // shards_of).reshape((-1,) + (1,) * (len(extent) - position - 1))

    level = one(*pieces[0])
    for cut in pieces[1:]:
        level = level * one(*cut)
    return level


def centred(key, extent, width, most, pieces=(), kind=jnp.bfloat16):
    values = jax.random.normal(key, extent, jnp.float32) * width
    if len(pieces) > 0:
        values = level_of(key, extent, pieces, -0.22, 0.18) * values
    return jnp.clip(values, min=-most, max=most).astype(kind)


def setup_inputs(seed: int = 0) -> dict:
    streams_of = jax.random.split(jax.random.key(seed), 10)
    return {
        "tokens": centred(streams_of[0], (ROWS, SEQLEN, D), 1.0, 6.0, ((0, 8), (1, 4))),
        "doc_start": draw_doc_start(jax.random.fold_in(streams_of[9], 71), 0),
        "cotangent": centred(streams_of[2], (ROWS, SEQLEN, D), 1.0, 6.0, ((0, 8), (1, 4))),
        "norm_one": jnp.clip(1.0 + 0.1 * jax.random.normal(streams_of[3], (D,), jnp.float32), 0.5, 1.5),
        "w_qkv": centred(streams_of[4], (D, 3 * D), D ** -0.5, 0.21875),
        "w_out": centred(streams_of[5], (D, D), (D // 16) ** -0.5, 0.875),
        "norm_two": jnp.clip(1.0 + 0.1 * jax.random.normal(streams_of[6], (D,), jnp.float32), 0.5, 1.5),
        "w_in": centred(streams_of[7], (D, 2 * FF), D ** -0.5, 0.21875),
        "w_down": centred(streams_of[8], (FF, D), FF ** -0.5, 0.1875),
    }


@jax.custom_vjp
def low(v):
    return lax.optimization_barrier(v.astype(jnp.bfloat16)).astype(jnp.float32)

@jax.custom_vjp
def low_back(v):
    return v

def low_keep(v):
    return (low(v), None)

def low_pass(kept, grad):
    return (grad,)

def back_keep(v):
    return (v, None)

def back_low(kept, grad):
    return (low(grad),)
low.defvjp(low_keep, low_pass)
low_back.defvjp(back_keep, back_low)
EPSILON = 1e-05
ROTARY_BASE = 160000.0
SCORE_SCALE = 0.125
MASKED_SCORE = -1e+30
HIGHEST = lax.Precision.HIGHEST

def layer_norm(values, gain_vec):
    average = lax.optimization_barrier(jnp.mean(values, axis=-1, keepdims=True))
    centered = values - average
    variance = lax.optimization_barrier(jnp.mean(centered * centered, axis=-1, keepdims=True))
    return centered * lax.rsqrt(variance + EPSILON) * gain_vec

def rotary_tables(offset):
    half_dim = HEAD_DIM // 2
    frequency = ROTARY_BASE ** (-(jnp.arange(half_dim, dtype=jnp.float32) * 2.0 / HEAD_DIM))
    angles = offset[:, None] * frequency[None, :]
    return (jnp.cos(angles)[:, None, :], jnp.sin(angles)[:, None, :])

def rotate(values, cosine, sine_table):
    half_dim = values.shape[-1] // 2
    first_half = values[..., :half_dim]
    second_half = values[..., half_dim:]
    return jnp.concatenate([first_half * cosine - second_half * sine_table, second_half * cosine + first_half * sine_table], axis=-1)

def row_forward(hidden, starts, norm_one, w_qkv, w_out, norm_two, w_in, w_down):
    places = jnp.arange(SEQLEN, dtype=jnp.int32)
    offset = (places - starts).astype(jnp.float32)
    cosine, sine_table = rotary_tables(offset)
    normed_one = low(layer_norm(hidden, norm_one))
    projected = low_back(jnp.dot(normed_one, w_qkv, precision=HIGHEST)).reshape(SEQLEN, 3, HEADS, HEAD_DIM)
    queries = low(low_back(rotate(projected[:, 0], cosine, sine_table)))
    key_heads = low(low_back(rotate(projected[:, 1], cosine, sine_table)))
    value_heads = low(low_back(projected[:, 2]))
    block_rows = min(512, SEQLEN)

    def attend_block(block_index):
        row_begin = block_index * block_rows
        query_block = lax.dynamic_slice_in_dim(queries, row_begin, block_rows)
        block_ids = lax.dynamic_slice_in_dim(starts, row_begin, block_rows)
        scores = low_back(jnp.einsum('qhd,khd->hqk', query_block, key_heads, precision=HIGHEST) * SCORE_SCALE)
        allowed = block_ids[:, None] == starts[None, :]
        scores = jnp.where(allowed[None], scores, MASKED_SCORE)
        row_max = lax.optimization_barrier(jnp.max(scores, axis=-1, keepdims=True))
        weight = jnp.exp(scores - row_max)
        probs = low(weight / lax.optimization_barrier(jnp.sum(weight, axis=-1, keepdims=True)))
        return jnp.einsum('hqk,khd->qhd', probs, value_heads, precision=HIGHEST)
    context = lax.map(jax.checkpoint(attend_block), jnp.arange(SEQLEN // block_rows, dtype=jnp.int32))
    context = low(low_back(context.reshape(SEQLEN, D)))
    attended = low_back(jnp.dot(context, w_out, precision=HIGHEST))
    middle = hidden + attended
    normed_two = low(layer_norm(middle, norm_two))
    gate_up = low_back(jnp.dot(normed_two, w_in, precision=HIGHEST))
    inner = low(jax.nn.gelu(gate_up[:, :FF], approximate=False) * gate_up[:, FF:])
    return middle + low_back(jnp.dot(inner, w_down, precision=HIGHEST))

def reference(tokens, doc_start, cotangent, norm_one, w_qkv, w_out, norm_two, w_in, w_down):
    weights = tuple((matrix.astype(jnp.float32) for matrix in (norm_one, w_qkv, w_out, norm_two, w_in, w_down)))

    def row_step(summed, row_inputs):
        hidden, starts, seed_grad = row_inputs

        def forward(row_hidden, *params):
            return row_forward(row_hidden, starts, *params)
        outputs, pullback = jax.vjp(forward, hidden.astype(jnp.float32), *weights)
        gradients = pullback(seed_grad.astype(jnp.float32))
        summed = tuple((left + right for left, right in zip(summed, gradients[1:])))
        return (summed, (outputs.astype(jnp.bfloat16), gradients[0]))
    zero_sums = tuple((jnp.zeros(matrix.shape, jnp.float32) for matrix in weights))
    summed, (result, grad_tokens) = lax.scan(row_step, zero_sums, (tokens, doc_start, cotangent))
    return (result, grad_tokens, summed[0], summed[1], summed[2], summed[3], summed[4], summed[5])
```

```python
import functools

import jax
import jax.numpy as jnp
from jax import lax
from jax.experimental import pallas as pl
from jax.experimental.pallas import tpu as pltpu
from jax.sharding import Mesh
from jax.sharding import PartitionSpec as P

D = 768
HEADS = 12
HEAD_DIM = 64
HALF = HEAD_DIM // 2
FF = 1152
WIDE = 3 * HEAD_DIM

EPSILON = 1e-05
ROTARY_BASE = 160000.0
SCORE_SCALE = 0.125
SCORE_EXP2 = SCORE_SCALE * 1.4426950408889634
MASKED_SCORE = -1e30
KEY_CHUNK = 256
F32 = jnp.float32
BF16 = jnp.bfloat16

dot = functools.partial(jnp.dot, preferred_element_type=F32)


def layer_norm(values, gain_vec):
    average = jnp.mean(values, axis=-1, keepdims=True)
    centered = values - average
    variance = jnp.mean(centered * centered, axis=-1, keepdims=True)
    return centered * lax.rsqrt(variance + EPSILON) * gain_vec


def gelu_gate(gate_part, up_part):
    return jax.nn.gelu(gate_part, approximate=False) * up_part


def project_kernel(hn_ref, w_ref, cos_ref, sin_ref, out_ref):
    part = pl.program_id(0)
    turned = dot(hn_ref[...], w_ref[...]).T
    cosine = jnp.where(part < 2, cos_ref[...], 1.0)
    sine = jnp.where(part < 2, sin_ref[...], 0.0)
    row = pl.multiple_of(part * HEAD_DIM, HEAD_DIM)
    for g in range(out_ref.shape[0]):
        first = turned[g * HEAD_DIM : g * HEAD_DIM + HALF]
        second = turned[g * HEAD_DIM + HALF : (g + 1) * HEAD_DIM]
        out_ref[g, pl.ds(row, HALF), :] = (first * cosine - second * sine).astype(BF16)
        out_ref[g, pl.ds(row + HALF, HALF), :] = (second * cosine + first * sine).astype(BF16)


def project(hn, w_qkv, cosine, sine, piece, groups):
    tokens = hn.shape[0]
    width = groups * HEAD_DIM
    pieces = D // width
    return pl.pallas_call(
        project_kernel,
        grid=(3,),
        in_specs=[
            pl.BlockSpec((tokens, D), lambda i: (0, 0)),
            pl.BlockSpec((D, width), lambda i: (0, i * pieces + piece)),
            pl.BlockSpec((HALF, tokens), lambda i: (0, 0)),
            pl.BlockSpec((HALF, tokens), lambda i: (0, 0)),
        ],
        out_specs=pl.BlockSpec((groups, WIDE, tokens), lambda i: (0, 0, 0)),
        out_shape=jax.ShapeDtypeStruct((groups, WIDE, tokens), BF16),
        compiler_params=pltpu.CompilerParams(vmem_limit_bytes=32 << 20),
        name="project",
    )(hn, w_qkv, cosine, sine)


def mask_scores(scores, chunk, chunks, edge, key_doc, query_doc, query_main):
    if chunk == 0 or chunk == chunks - 1:
        own = key_doc[chunk * KEY_CHUNK : (chunk + 1) * KEY_CHUNK, :]
        return jnp.where(own == query_doc, scores, MASKED_SCORE)
    if edge:
        return jnp.where(query_main, scores, MASKED_SCORE)
    return scores


def forward_kernel(bq, q_ref, kv_ref, kdoc_ref, qdoc_ref, out_ref, lse_ref, key_s, score_s):
    step = pl.program_id(0)
    steps = pl.num_programs(0)
    total = key_s.shape[0]
    chunks = total // KEY_CHUNK
    parts, _, span = kv_ref.shape

    @pl.when(step == 0)
    def _():
        for s in range(parts):
            key_s[s * span : (s + 1) * span, :] = (
                kv_ref[s, HEAD_DIM : 2 * HEAD_DIM, :].astype(F32).T.astype(BF16)
            )

    def run(edge):
        queries = q_ref[0]
        query_doc = qdoc_ref[...]
        query_main = query_doc == kdoc_ref[total // 2 : total // 2 + 1, :]
        top = None
        for c in range(chunks):
            rows = slice(c * KEY_CHUNK, (c + 1) * KEY_CHUNK)
            scores = dot(key_s[rows, :], queries)
            scores = mask_scores(scores, c, chunks, edge, kdoc_ref, query_doc, query_main)
            score_s[rows, :] = scores
            peak = jnp.max(scores.reshape(KEY_CHUNK // 8, 8, bq), axis=0)
            top = peak if top is None else jnp.maximum(top, peak)
        top = jnp.max(top, axis=0, keepdims=True) * SCORE_EXP2
        mass, acc = None, None
        for c in range(chunks):
            rows = slice(c * KEY_CHUNK, (c + 1) * KEY_CHUNK)
            weight = jnp.exp2(score_s[rows, :] * SCORE_EXP2 - top)
            part = jnp.sum(weight.reshape(KEY_CHUNK // 8, 8, bq), axis=0)
            mass = part if mass is None else mass + part
            at = c * KEY_CHUNK % span
            values = kv_ref[c * KEY_CHUNK // span, 2 * HEAD_DIM :, at : at + KEY_CHUNK]
            term = dot(values, weight.astype(BF16))
            acc = term if acc is None else acc + term
        mass = jnp.sum(mass, axis=0, keepdims=True)
        out_ref[0] = (acc / mass).astype(BF16)
        lse_ref[...] = top + jnp.log2(mass)

    at_edge = (step == 0) | (step == steps - 1)
    pl.when(at_edge)(lambda: run(True))
    pl.when(jnp.logical_not(at_edge))(lambda: run(False))


def attend_forward(qkv, key_doc, query_doc, bq):
    parts, _, span = qkv.shape
    total = parts * span
    ratio = span // bq
    return pl.pallas_call(
        functools.partial(forward_kernel, bq),
        grid=(total // bq,),
        in_specs=[
            pl.BlockSpec((1, HEAD_DIM, bq), lambda i: (i // ratio, 0, i % ratio)),
            pl.BlockSpec(qkv.shape, lambda i: (0, 0, 0)),
            pl.BlockSpec((total, 1), lambda i: (0, 0)),
            pl.BlockSpec((1, bq), lambda i: (0, i)),
        ],
        out_specs=[
            pl.BlockSpec((1, HEAD_DIM, bq), lambda i: (i // ratio, 0, i % ratio)),
            pl.BlockSpec((1, bq), lambda i: (0, i)),
        ],
        out_shape=[
            jax.ShapeDtypeStruct((parts, HEAD_DIM, span), BF16),
            jax.ShapeDtypeStruct((1, total), F32),
        ],
        scratch_shapes=[pltpu.VMEM((total, HEAD_DIM), BF16), pltpu.VMEM((total, bq), F32)],
        compiler_params=pltpu.CompilerParams(vmem_limit_bytes=40 << 20),
        cost_estimate=pl.CostEstimate(
            flops=16 * HEAD_DIM * total * total, bytes_accessed=4 << 20, transcendentals=total * total
        ),
        name="attend_forward",
    )(qkv, qkv, key_doc, query_doc)


def backward_kernel(
    bq, q_ref, kv_ref, kdoc_ref, qdoc_ref, do_ref, o_ref, lse_ref, cos_ref, sin_ref,
    grad_ref, key_s, value_s, dk_s, dv_s,
):
    step = pl.program_id(0)
    steps = pl.num_programs(0)
    total = key_s.shape[0]
    chunks = total // KEY_CHUNK
    parts, _, span = kv_ref.shape

    @pl.when(step == 0)
    def _():
        for s in range(parts):
            rows = slice(s * span, (s + 1) * span)
            key_s[rows, :] = kv_ref[s, HEAD_DIM : 2 * HEAD_DIM, :].astype(F32).T.astype(BF16)
            value_s[rows, :] = kv_ref[s, 2 * HEAD_DIM :, :].astype(F32).T.astype(BF16)
        dk_s[...] = jnp.zeros_like(dk_s)
        dv_s[...] = jnp.zeros_like(dv_s)

    def turn_back(grad, cosine, sine):
        first, second = grad[:HALF], grad[HALF:]
        return first * cosine + second * sine, second * cosine - first * sine

    def run(edge):
        queries = q_ref[0]
        upstream = do_ref[0]
        wide_up = upstream.astype(F32)
        centre = jnp.sum(wide_up * o_ref[0].astype(F32), axis=0, keepdims=True)
        query_rows = queries.astype(F32).T.astype(BF16)
        up_rows = wide_up.T.astype(BF16)
        query_doc = qdoc_ref[...]
        query_main = query_doc == kdoc_ref[total // 2 : total // 2 + 1, :]
        lse = lse_ref[...]
        dq = None
        for c in range(chunks):
            rows = slice(c * KEY_CHUNK, (c + 1) * KEY_CHUNK)
            scores = dot(key_s[rows, :], queries)
            scores = mask_scores(scores, c, chunks, edge, kdoc_ref, query_doc, query_main)
            probs = jnp.exp2(scores * SCORE_EXP2 - lse)
            grad_prob = dot(value_s[rows, :], upstream)
            grad_scores = (probs * (grad_prob - centre)).astype(BF16)
            dv_s[rows, :] += dot(probs.astype(BF16), up_rows)
            dk_s[rows, :] += dot(grad_scores, query_rows)
            at = c * KEY_CHUNK % span
            keys = kv_ref[c * KEY_CHUNK // span, HEAD_DIM : 2 * HEAD_DIM, at : at + KEY_CHUNK]
            term = dot(keys, grad_scores)
            dq = term if dq is None else dq + term
        ratio = span // bq
        lanes = pl.ds(pl.multiple_of((step % ratio) * bq, bq), bq)
        here = pl.ds(pl.multiple_of(step * bq, bq), bq)
        one, two = turn_back(dq * SCORE_SCALE, cos_ref[:, here], sin_ref[:, here])
        grad_ref[step // ratio, 0:HALF, lanes] = one.astype(BF16)
        grad_ref[step // ratio, HALF:HEAD_DIM, lanes] = two.astype(BF16)

    at_edge = (step == 0) | (step == steps - 1)
    pl.when(at_edge)(lambda: run(True))
    pl.when(jnp.logical_not(at_edge))(lambda: run(False))

    @pl.when(step == steps - 1)
    def _():
        for s in range(parts):
            rows = slice(s * span, (s + 1) * span)
            one, two = turn_back(dk_s[rows, :].T * SCORE_SCALE, cos_ref[:, rows], sin_ref[:, rows])
            grad_ref[s, HEAD_DIM : HEAD_DIM + HALF, :] = one.astype(BF16)
            grad_ref[s, HEAD_DIM + HALF : 2 * HEAD_DIM, :] = two.astype(BF16)
            grad_ref[s, 2 * HEAD_DIM :, :] = dv_s[rows, :].T.astype(BF16)


def attend_backward(qkv, key_doc, query_doc, upstream, context, lse, cosine, sine, bq):
    parts, _, span = qkv.shape
    total = parts * span
    ratio = span // bq
    block = lambda: pl.BlockSpec((1, HEAD_DIM, bq), lambda i: (i // ratio, 0, i % ratio))
    return pl.pallas_call(
        functools.partial(backward_kernel, bq),
        grid=(total // bq,),
        in_specs=[
            block(),
            pl.BlockSpec(qkv.shape, lambda i: (0, 0, 0)),
            pl.BlockSpec((total, 1), lambda i: (0, 0)),
            pl.BlockSpec((1, bq), lambda i: (0, i)),
            block(),
            block(),
            pl.BlockSpec((1, bq), lambda i: (0, i)),
            pl.BlockSpec((HALF, total), lambda i: (0, 0)),
            pl.BlockSpec((HALF, total), lambda i: (0, 0)),
        ],
        out_specs=pl.BlockSpec(qkv.shape, lambda i: (0, 0, 0)),
        out_shape=jax.ShapeDtypeStruct(qkv.shape, BF16),
        scratch_shapes=[
            pltpu.VMEM((total, HEAD_DIM), BF16),
            pltpu.VMEM((total, HEAD_DIM), BF16),
            pltpu.VMEM((total, HEAD_DIM), F32),
            pltpu.VMEM((total, HEAD_DIM), F32),
        ],
        compiler_params=pltpu.CompilerParams(vmem_limit_bytes=40 << 20),
        cost_estimate=pl.CostEstimate(
            flops=40 * HEAD_DIM * total * total, bytes_accessed=6 << 20, transcendentals=total * total
        ),
        name="attend_backward",
    )(qkv, qkv, key_doc, query_doc, upstream, context, lse, cosine, sine)


def swap_cores(values):
    return lax.ppermute(values, "core", [(0, 1), (1, 0)])


def on_device(tokens, doc_start, cotangent, norm_one, w_qkv, w_out, norm_two, w_in, w_down):
    parts = lax.axis_size("seq")
    rest = lax.axis_size("rest")
    span = tokens.shape[1]
    total = span * parts
    pieces = HEADS // parts
    bq = min(512, span)
    first_token = lax.axis_index("seq") * span
    core = lax.axis_index("core")
    starts = doc_start[0]
    key_doc = starts[:, None]
    query_doc = starts[None, :]

    frequency = ROTARY_BASE ** (-(jnp.arange(HALF, dtype=F32) * 2.0 / HEAD_DIM))
    offset = (jnp.arange(total, dtype=jnp.int32) - starts).astype(F32)
    angles = frequency[:, None] * offset[None, :]
    cosine, sine = jnp.cos(angles), jnp.sin(angles)
    own_cosine = lax.dynamic_slice_in_dim(cosine, first_token, span, axis=1)
    own_sine = lax.dynamic_slice_in_dim(sine, first_token, span, axis=1)

    def exchange(values):
        return lax.all_to_all(values, "seq", split_axis=0, concat_axis=0, tiled=True)

    hidden = tokens[0].astype(F32)
    normed_one, norm_one_back = jax.vjp(lambda u: layer_norm(u, norm_one), hidden)
    hn = normed_one.astype(BF16)
    qkv = [
        exchange(project(hn, w_qkv, own_cosine, own_sine, j, parts)) for j in range(pieces)
    ]
    hn_row = lax.all_gather(hn, "seq")
    contexts, lses, arrived = [], [], []
    for j in range(pieces):
        context, lse = attend_forward(qkv[j], key_doc, query_doc, bq)
        contexts.append(context)
        lses.append(lse)
        arrived.append(exchange(context).reshape(parts * HEAD_DIM, span))
    context_t = jnp.concatenate(arrived, axis=0)

    attended = lax.dot_general(
        context_t, w_out, (((0,), (0,)), ((), ())), preferred_element_type=F32
    )
    middle = hidden + attended
    normed_two, norm_two_back = jax.vjp(lambda u: layer_norm(u, norm_two), middle)
    normed_two_low = normed_two.astype(BF16)
    gate_up = dot(normed_two_low, w_in)
    inner, gelu_back = jax.vjp(gelu_gate, gate_up[:, :FF], gate_up[:, FF:])
    inner_low = inner.astype(BF16)
    result = (middle + dot(inner_low, w_down)).astype(BF16)
    grad_out = cotangent[0]
    grad_w_down = jnp.einsum("tf,td->fd", inner_low, grad_out, preferred_element_type=F32)
    grad_inner = jnp.einsum("td,fd->tf", grad_out, w_down, preferred_element_type=F32)
    grad_gate, grad_up = gelu_back(grad_inner)
    grad_gate_up = jnp.concatenate([grad_gate, grad_up], axis=-1).astype(BF16)
    grad_w_in = jnp.einsum("td,tf->df", normed_two_low, grad_gate_up, preferred_element_type=F32)
    grad_normed_two = jnp.einsum("tf,df->td", grad_gate_up, w_in, preferred_element_type=F32)
    (grad_middle_part,) = norm_two_back(grad_normed_two)
    grad_middle = grad_out.astype(F32) + grad_middle_part
    grad_mid_low = grad_middle.astype(BF16)
    grad_w_out = dot(context_t, grad_mid_low)
    grad_context_t = lax.dot_general(
        w_out, grad_mid_low, (((1,), (1,)), ((), ())), preferred_element_type=F32
    ).astype(BF16)
    upstream = exchange(
        grad_context_t.reshape(pieces, parts, HEAD_DIM, span).transpose(1, 0, 2, 3)
    )

    def halves(wide):
        half = D // 2
        send = jnp.where(core == 0, wide[:, half:], wide[:, :half]).astype(BF16)
        mine = jnp.where(core == 0, wide[:, :half], wide[:, half:])
        return (mine + swap_cores(send).astype(F32)).astype(BF16)

    early = jnp.concatenate(
        [grad_w_in[:, i * D : (i + 1) * D] for i in range(3)] + [grad_w_down, grad_w_out], axis=0
    )
    early_sum = lax.psum_scatter(halves(early), "seq", scatter_dimension=0, tiled=True)
    early_sum = lax.psum_scatter(early_sum, "rest", scatter_dimension=0, tiled=True)

    returned, late = [], []
    for j in range(pieces):
        grads = attend_backward(
            qkv[j], key_doc, query_doc, upstream[:, j], contexts[j], lses[j], cosine, sine, bq
        )
        returned.append(exchange(grads))
        late.append(jnp.einsum("sct,std->cd", grads, hn_row, preferred_element_type=F32))
    late_sum = lax.psum_scatter(
        halves(jnp.concatenate(late, axis=0)), "rest", scatter_dimension=0, tiled=True
    )
    grad_projected_t = (
        jnp.stack(returned)
        .reshape(pieces, parts, 3, HEAD_DIM, span)
        .transpose(2, 0, 1, 3, 4)
        .reshape(3 * D, span)
    )
    grad_normed_one = lax.dot_general(
        grad_projected_t, w_qkv, (((0,), (1,)), ((), ())), preferred_element_type=F32
    )
    (grad_hidden_part,) = norm_one_back(grad_normed_one)
    grad_input = grad_middle + grad_hidden_part

    early_rows = early_sum.shape[0]
    mine = lax.all_gather(jnp.concatenate([early_sum, late_sum], axis=0), ("seq", "rest"))
    other = swap_cores(mine)
    low_lanes = jnp.where(core == 0, mine, other)
    high_lanes = jnp.where(core == 0, other, mine)
    summed = jnp.concatenate([low_lanes, high_lanes], axis=-1).astype(F32)
    early_all = summed[:, :early_rows].reshape(-1, D)
    late_all = (
        summed[:, early_rows:]
        .reshape(parts, pieces, 3, HEAD_DIM, D)
        .transpose(4, 2, 1, 0, 3)
        .reshape(D, 3 * D)
    )
    sum_w_in = jnp.concatenate([early_all[i * D : (i + 1) * D] for i in range(3)], axis=1)
    sum_w_down = early_all[3 * D : 3 * D + FF]
    sum_w_out = early_all[3 * D + FF :]
    sum_norm_one = jnp.sum(late_all * w_qkv.astype(F32), axis=1) / norm_one
    sum_norm_two = jnp.sum(sum_w_in * w_in.astype(F32), axis=1) / norm_two
    return (
        result[None],
        grad_input[None],
        sum_norm_one,
        late_all,
        sum_w_out,
        sum_norm_two,
        sum_w_in,
        sum_w_down,
    )


def solution(mesh):
    parts = mesh.shape["seq"]
    split = Mesh(mesh.devices.reshape(parts, -1, 2), ("seq", "rest", "core"))
    rows = ("rest", "core")
    tokens_at = P(rows, "seq", None)
    return jax.shard_map(
        on_device,
        mesh=split,
        in_specs=(tokens_at, P(rows, None), tokens_at, P(), P(), P(), P(), P(), P()),
        out_specs=(tokens_at, tokens_at, P(), P(), P(), P(), P(), P()),
        check_vma=False,
    )
```

```python
import functools

import jax
import jax.numpy as jnp
from jax import lax
from jax.experimental import pallas as pl
from jax.experimental.pallas import tpu as pltpu
from jax.sharding import Mesh
from jax.sharding import PartitionSpec as P

D = 768
HEADS = 12
HEAD_DIM = 64
HALF = HEAD_DIM // 2
FF = 1152
WIDE = 3 * HEAD_DIM
LANES = D // 2

EPSILON = 1e-05
ROTARY_BASE = 160000.0
SCORE_SCALE = 0.125
SCORE_EXP2 = SCORE_SCALE * 1.4426950408889634
MASKED_SCORE = -1e30
KEY_CHUNK = 256
F32 = jnp.float32
BF16 = jnp.bfloat16

dot = functools.partial(jnp.dot, preferred_element_type=F32)


def cost(flops, moved, transcendentals=0):
    return pl.CostEstimate(flops=flops, bytes_accessed=moved, transcendentals=transcendentals)


def layer_norm(values, gain_vec):
    average = jnp.mean(values, axis=-1, keepdims=True)
    centered = values - average
    variance = jnp.mean(centered * centered, axis=-1, keepdims=True)
    return centered * lax.rsqrt(variance + EPSILON) * gain_vec


def gelu_gate(gate_part, up_part):
    return jax.nn.gelu(gate_part, approximate=False) * up_part


def project_kernel(me_ref, hn_ref, w_ref, cos_ref, sin_ref, out_ref):
    part = pl.program_id(0)
    turned = dot(hn_ref[...], w_ref[...]).T
    cosine = jnp.where(part < 2, cos_ref[...], 1.0)
    sine = jnp.where(part < 2, sin_ref[...], 0.0)
    row = pl.multiple_of(part * HEAD_DIM, HEAD_DIM)
    for g in range(out_ref.shape[0]):
        slot = me_ref[0] ^ g
        first = turned[g * HEAD_DIM : g * HEAD_DIM + HALF]
        second = turned[g * HEAD_DIM + HALF : (g + 1) * HEAD_DIM]
        out_ref[slot, pl.ds(row, HALF), :] = (first * cosine - second * sine).astype(BF16)
        out_ref[slot, pl.ds(row + HALF, HALF), :] = (second * cosine + first * sine).astype(BF16)


def project(me, hn, w_qkv, cosine, sine, piece, groups):
    tokens = hn.shape[0]
    width = groups * HEAD_DIM
    pieces = D // width
    return pl.pallas_call(
        project_kernel,
        grid_spec=pltpu.PrefetchScalarGridSpec(
            num_scalar_prefetch=1,
            grid=(3,),
            in_specs=[
                pl.BlockSpec((tokens, D), lambda i, me: (0, 0)),
                pl.BlockSpec((D, width), lambda i, me: (0, i * pieces + piece)),
                pl.BlockSpec((HALF, tokens), lambda i, me: (0, 0)),
                pl.BlockSpec((HALF, tokens), lambda i, me: (0, 0)),
            ],
            out_specs=pl.BlockSpec((groups, WIDE, tokens), lambda i, me: (0, 0, 0)),
        ),
        out_shape=jax.ShapeDtypeStruct((groups, WIDE, tokens), BF16),
        compiler_params=pltpu.CompilerParams(vmem_limit_bytes=32 << 20),
        cost_estimate=cost(6 * tokens * D * width, 4 << 20),
        name="project",
    )(me, hn, w_qkv, cosine, sine)


def mask_scores(scores, chunk, chunks, edge, key_doc, query_doc, query_main):
    if chunk == 0 or chunk == chunks - 1:
        own = key_doc[chunk * KEY_CHUNK : (chunk + 1) * KEY_CHUNK, :]
        return jnp.where(own == query_doc, scores, MASKED_SCORE)
    if edge:
        return jnp.where(query_main, scores, MASKED_SCORE)
    return scores


def put_in_order(me, slots, qkv_s, key_s, value_s=None):
    span = qkv_s.shape[2]
    for k, ref in enumerate(slots):
        at = me ^ k
        piece = ref[...].reshape(WIDE, span)
        qkv_s[at] = piece
        rows = pl.ds(pl.multiple_of(at * span, span), span)
        key_s[rows, :] = piece[HEAD_DIM : 2 * HEAD_DIM].astype(F32).T.astype(BF16)
        if value_s is not None:
            value_s[rows, :] = piece[2 * HEAD_DIM :].astype(F32).T.astype(BF16)


def slot_specs(slots):
    own = pl.BlockSpec((1,) + slots[0].shape[1:], lambda i, me: (0, 0, 0))
    rest = [pl.BlockSpec(s.shape, lambda i, me: (0, 0)) for s in slots[1:]]
    return [own] + rest


def forward_kernel(bq, parts, me_ref, *refs):
    slots = refs[:parts]
    kdoc_ref, qdoc_ref, out_ref, lse_ref, qkv_s, key_s, score_s = refs[parts:]
    step = pl.program_id(0)
    steps = pl.num_programs(0)
    total = key_s.shape[0]
    chunks = total // KEY_CHUNK
    span = qkv_s.shape[2]
    ratio = span // bq

    @pl.when(step == 0)
    def _():
        put_in_order(me_ref[0], slots, qkv_s, key_s)

    def run(edge):
        lanes = pl.ds(pl.multiple_of((step % ratio) * bq, bq), bq)
        queries = qkv_s[step // ratio, 0:HEAD_DIM, lanes]
        query_doc = qdoc_ref[...]
        query_main = query_doc == kdoc_ref[total // 2 : total // 2 + 1, :]
        top = None
        for c in range(chunks):
            rows = slice(c * KEY_CHUNK, (c + 1) * KEY_CHUNK)
            scores = dot(key_s[rows, :], queries)
            scores = mask_scores(scores, c, chunks, edge, kdoc_ref, query_doc, query_main)
            score_s[rows, :] = scores
            peak = jnp.max(scores.reshape(KEY_CHUNK // 8, 8, bq), axis=0)
            top = peak if top is None else jnp.maximum(top, peak)
        top = jnp.max(top, axis=0, keepdims=True) * SCORE_EXP2
        mass, acc = None, None
        for c in range(chunks):
            rows = slice(c * KEY_CHUNK, (c + 1) * KEY_CHUNK)
            weight = jnp.exp2(score_s[rows, :] * SCORE_EXP2 - top)
            part = jnp.sum(weight.reshape(KEY_CHUNK // 8, 8, bq), axis=0)
            mass = part if mass is None else mass + part
            at = c * KEY_CHUNK % span
            values = qkv_s[c * KEY_CHUNK // span, 2 * HEAD_DIM :, at : at + KEY_CHUNK]
            term = dot(values, weight.astype(BF16))
            acc = term if acc is None else acc + term
        mass = jnp.sum(mass, axis=0, keepdims=True)
        out_ref[0] = (acc / mass).astype(BF16)
        lse_ref[...] = top + jnp.log2(mass)

    at_edge = (step == 0) | (step == steps - 1)
    pl.when(at_edge)(lambda: run(True))
    pl.when(jnp.logical_not(at_edge))(lambda: run(False))


def attend_forward(me, slots, key_doc, query_doc, bq):
    parts, _, span = slots[0].shape
    total = parts * span
    ratio = span // bq
    return pl.pallas_call(
        functools.partial(forward_kernel, bq, parts),
        grid_spec=pltpu.PrefetchScalarGridSpec(
            num_scalar_prefetch=1,
            grid=(total // bq,),
            in_specs=slot_specs(slots)
            + [
                pl.BlockSpec((total, 1), lambda i, me: (0, 0)),
                pl.BlockSpec((1, bq), lambda i, me: (0, i)),
            ],
            out_specs=[
                pl.BlockSpec((1, HEAD_DIM, bq), lambda i, me: (i // ratio, 0, i % ratio)),
                pl.BlockSpec((1, bq), lambda i, me: (0, i)),
            ],
            scratch_shapes=[
                pltpu.VMEM((parts, WIDE, span), BF16),
                pltpu.VMEM((total, HEAD_DIM), BF16),
                pltpu.VMEM((total, bq), F32),
            ],
        ),
        out_shape=[
            jax.ShapeDtypeStruct((parts, HEAD_DIM, span), BF16),
            jax.ShapeDtypeStruct((1, total), F32),
        ],
        compiler_params=pltpu.CompilerParams(vmem_limit_bytes=40 << 20),
        cost_estimate=cost(16 * HEAD_DIM * total * total, 4 << 20, total * total),
        name="attend_forward",
    )(me, *slots, key_doc, query_doc)


def backward_kernel(bq, parts, me_ref, *refs):
    slots = refs[:parts]
    (kdoc_ref, qdoc_ref, do_ref, o_ref, lse_ref, cos_ref, sin_ref, grad_ref,
     qkv_s, key_s, value_s, dk_s, dv_s) = refs[parts:]
    step = pl.program_id(0)
    steps = pl.num_programs(0)
    total = key_s.shape[0]
    chunks = total // KEY_CHUNK
    span = qkv_s.shape[2]
    ratio = span // bq

    @pl.when(step == 0)
    def _():
        put_in_order(me_ref[0], slots, qkv_s, key_s, value_s)
        dk_s[...] = jnp.zeros_like(dk_s)
        dv_s[...] = jnp.zeros_like(dv_s)

    def turn_back(grad, cosine, sine):
        first, second = grad[:HALF], grad[HALF:]
        return first * cosine + second * sine, second * cosine - first * sine

    def run(edge):
        lanes = pl.ds(pl.multiple_of((step % ratio) * bq, bq), bq)
        here = pl.ds(pl.multiple_of(step * bq, bq), bq)
        queries = qkv_s[step // ratio, 0:HEAD_DIM, lanes]
        upstream = do_ref[0, 0]
        wide_up = upstream.astype(F32)
        centre = jnp.sum(wide_up * o_ref[0].astype(F32), axis=0, keepdims=True)
        query_rows = queries.astype(F32).T.astype(BF16)
        up_rows = wide_up.T.astype(BF16)
        query_doc = qdoc_ref[...]
        query_main = query_doc == kdoc_ref[total // 2 : total // 2 + 1, :]
        lse = lse_ref[...]
        dq = None
        for c in range(chunks):
            rows = slice(c * KEY_CHUNK, (c + 1) * KEY_CHUNK)
            scores = dot(key_s[rows, :], queries)
            scores = mask_scores(scores, c, chunks, edge, kdoc_ref, query_doc, query_main)
            probs = jnp.exp2(scores * SCORE_EXP2 - lse)
            grad_prob = dot(value_s[rows, :], upstream)
            grad_scores = (probs * (grad_prob - centre)).astype(BF16)
            dv_s[rows, :] += dot(probs.astype(BF16), up_rows)
            dk_s[rows, :] += dot(grad_scores, query_rows)
            at = c * KEY_CHUNK % span
            keys = qkv_s[c * KEY_CHUNK // span, HEAD_DIM : 2 * HEAD_DIM, at : at + KEY_CHUNK]
            term = dot(keys, grad_scores)
            dq = term if dq is None else dq + term
        one, two = turn_back(dq * SCORE_SCALE, cos_ref[:, here], sin_ref[:, here])
        slot = me_ref[0] ^ (step // ratio)
        grad_ref[slot, 0:HALF, lanes] = one.astype(BF16)
        grad_ref[slot, HALF:HEAD_DIM, lanes] = two.astype(BF16)

    at_edge = (step == 0) | (step == steps - 1)
    pl.when(at_edge)(lambda: run(True))
    pl.when(jnp.logical_not(at_edge))(lambda: run(False))

    @pl.when(step == steps - 1)
    def _():
        for s in range(parts):
            slot = me_ref[0] ^ s
            rows = slice(s * span, (s + 1) * span)
            one, two = turn_back(dk_s[rows, :].T * SCORE_SCALE, cos_ref[:, rows], sin_ref[:, rows])
            grad_ref[slot, HEAD_DIM : HEAD_DIM + HALF, :] = one.astype(BF16)
            grad_ref[slot, HEAD_DIM + HALF : 2 * HEAD_DIM, :] = two.astype(BF16)
            grad_ref[slot, 2 * HEAD_DIM :, :] = dv_s[rows, :].T.astype(BF16)


def attend_backward(me, slots, key_doc, query_doc, upstream, piece, context, lse, cosine, sine, bq):
    parts, _, span = slots[0].shape
    total = parts * span
    ratio = span // bq
    return pl.pallas_call(
        functools.partial(backward_kernel, bq, parts),
        grid_spec=pltpu.PrefetchScalarGridSpec(
            num_scalar_prefetch=1,
            grid=(total // bq,),
            in_specs=slot_specs(slots)
            + [
                pl.BlockSpec((total, 1), lambda i, me: (0, 0)),
                pl.BlockSpec((1, bq), lambda i, me: (0, i)),
                pl.BlockSpec(
                    (1, 1, HEAD_DIM, bq), lambda i, me: (i // ratio, piece, 0, i % ratio)
                ),
                pl.BlockSpec((1, HEAD_DIM, bq), lambda i, me: (i // ratio, 0, i % ratio)),
                pl.BlockSpec((1, bq), lambda i, me: (0, i)),
                pl.BlockSpec((HALF, total), lambda i, me: (0, 0)),
                pl.BlockSpec((HALF, total), lambda i, me: (0, 0)),
            ],
            out_specs=pl.BlockSpec((parts, WIDE, span), lambda i, me: (0, 0, 0)),
            scratch_shapes=[
                pltpu.VMEM((parts, WIDE, span), BF16),
                pltpu.VMEM((total, HEAD_DIM), BF16),
                pltpu.VMEM((total, HEAD_DIM), BF16),
                pltpu.VMEM((total, HEAD_DIM), F32),
                pltpu.VMEM((total, HEAD_DIM), F32),
            ],
        ),
        out_shape=jax.ShapeDtypeStruct((parts, WIDE, span), BF16),
        compiler_params=pltpu.CompilerParams(vmem_limit_bytes=40 << 20),
        cost_estimate=cost(40 * HEAD_DIM * total * total, 6 << 20, total * total),
        name="attend_backward",
    )(me, *slots, key_doc, query_doc, upstream, context, lse, cosine, sine)


def early_grad_kernel(me_ref, n2_ref, gu_ref, inner_ref, cot_ref, ctx_ref, mid_ref, keep_ref, give_ref):
    parts, near = keep_ref.shape[:2]
    rows = D // (2 * parts * near)
    low = me_ref[2] == 0

    def put(first, second, count, at):
        kept = jnp.where(low, first, second).astype(BF16)
        given = jnp.where(low, second, first).astype(BF16)
        for s in range(parts):
            for r in range(near):
                here = slice((s * near + r) * count, (s * near + r + 1) * count)
                slot_s, slot_r = me_ref[0] ^ s, me_ref[1] ^ r
                keep_ref[slot_s, slot_r, at : at + count, :] = kept[here]
                give_ref[slot_s, slot_r, at : at + count, :] = given[here]

    n2_t = n2_ref[...].astype(F32).T.astype(BF16)
    for u in range(2 * FF // LANES):
        block = dot(n2_t, gu_ref[:, u * LANES : (u + 1) * LANES])
        put(block[: D // 2], block[D // 2 :], rows, u * rows)
    inner_t = inner_ref[...].astype(F32).T.astype(BF16)
    down = dot(inner_t, cot_ref[...])
    put(down[:, :LANES], down[:, LANES:], 3 * rows, 6 * rows)
    for u in range(2):
        block = dot(ctx_ref[...], mid_ref[:, u * LANES : (u + 1) * LANES])
        put(block[: D // 2], block[D // 2 :], rows, (9 + u) * rows)


def early_grads(me, n2, gate_up, inner, cotangent, context_t, mid, parts, near):
    rows = D // (2 * parts * near)
    shape = jax.ShapeDtypeStruct((parts, near, 11 * rows, LANES), BF16)
    vmem = pl.BlockSpec(memory_space=pltpu.VMEM)
    return pl.pallas_call(
        early_grad_kernel,
        in_specs=[pl.BlockSpec(memory_space=pltpu.SMEM)] + [vmem] * 6,
        out_specs=[vmem, vmem],
        out_shape=[shape, shape],
        compiler_params=pltpu.CompilerParams(vmem_limit_bytes=44 << 20),
        cost_estimate=cost(2 * n2.shape[0] * 4224 * D, 14 << 20),
        name="early_grads",
    )(me, n2, gate_up, inner, cotangent, context_t, mid)


def late_grad_kernel(pieces, me_ref, *refs):
    grads = refs[:pieces]
    hn_ref, keep_ref, give_ref = refs[pieces:]
    parts = hn_ref.shape[0]
    near = keep_ref.shape[0]
    low = me_ref[2] == 0
    for j, ref in enumerate(grads):
        block = None
        for s in range(parts):
            term = dot(ref[me_ref[0] ^ s], hn_ref[s])
            block = term if block is None else block + term
        for part in range(3):
            head = block[part * HEAD_DIM : (part + 1) * HEAD_DIM]
            first, second = head[:HALF], head[HALF:]
            kept = jnp.where(low, first, second).astype(BF16)
            given = jnp.where(low, second, first).astype(BF16)
            for r in range(near):
                slot = me_ref[1] ^ r
                keep_ref[slot, 3 * j + part] = kept[8 * r : 8 * r + 8]
                give_ref[slot, 3 * j + part] = given[8 * r : 8 * r + 8]


def late_grads(me, grads, hn_row, near):
    pieces = len(grads)
    shape = jax.ShapeDtypeStruct((near, 3 * pieces, 8, D), BF16)
    vmem = pl.BlockSpec(memory_space=pltpu.VMEM)
    return pl.pallas_call(
        functools.partial(late_grad_kernel, pieces),
        in_specs=[pl.BlockSpec(memory_space=pltpu.SMEM)] + [vmem] * (pieces + 1),
        out_specs=[vmem, vmem],
        out_shape=[shape, shape],
        compiler_params=pltpu.CompilerParams(vmem_limit_bytes=32 << 20),
        cost_estimate=cost(2 * 2048 * 576 * D, 6 << 20),
        name="late_grads",
    )(me, *grads, hn_row)


def early_kernel(me_ref, mine_ref, other_ref, w_ref, norm_ref, win_ref, wdown_ref, wout_ref, gain_ref):
    near = mine_ref.shape[1]
    parts = pl.num_programs(0) // 2
    rows = D // (2 * parts * near)

    def run(ref):
        for r in range(near):
            piece = ref[0, me_ref[1] ^ r].astype(F32)
            here = slice(r * rows, (r + 1) * rows)
            wide = jnp.concatenate([piece[rows * u : rows * (u + 1)] for u in range(6)], axis=1)
            win_ref[here, :] = wide
            part = wide * w_ref[here, :].astype(F32)
            gain_ref[here, :] = jnp.sum(part, axis=1, keepdims=True) / norm_ref[here, :]
            wdown_ref[3 * r * rows : 3 * (r + 1) * rows, :] = piece[6 * rows : 9 * rows]
            wout_ref[here, :LANES] = piece[9 * rows : 10 * rows]
            wout_ref[here, LANES:] = piece[10 * rows :]

    ours = (pl.program_id(0) // parts) == me_ref[2]
    pl.when(ours)(lambda: run(mine_ref))
    pl.when(jnp.logical_not(ours))(lambda: run(other_ref))


def assemble_early(me, mine, other, w_in, norm_two):
    parts, near = mine.shape[:2]
    steps = 2 * parts
    rows = D // steps

    def slot(own):
        def index(p, me):
            used = (p // parts == me[2]) == own
            return (jnp.where(used, me[0] ^ (p % parts), 0), 0, 0, 0)

        return pl.BlockSpec((1,) + mine.shape[1:], index)

    return pl.pallas_call(
        early_kernel,
        grid_spec=pltpu.PrefetchScalarGridSpec(
            num_scalar_prefetch=1,
            grid=(steps,),
            in_specs=[
                slot(True),
                slot(False),
                pl.BlockSpec((rows, 2 * FF), lambda p, me: (p, 0)),
                pl.BlockSpec((rows, 1), lambda p, me: (p, 0)),
            ],
            out_specs=[
                pl.BlockSpec((rows, 2 * FF), lambda p, me: (p, 0)),
                pl.BlockSpec((3 * rows, LANES), lambda p, me: (p % parts, p // parts)),
                pl.BlockSpec((rows, D), lambda p, me: (p, 0)),
                pl.BlockSpec((rows, 1), lambda p, me: (p, 0)),
            ],
        ),
        out_shape=[
            jax.ShapeDtypeStruct((D, 2 * FF), F32),
            jax.ShapeDtypeStruct((FF, D), F32),
            jax.ShapeDtypeStruct((D, D), F32),
            jax.ShapeDtypeStruct((D, 1), F32),
        ],
        compiler_params=pltpu.CompilerParams(vmem_limit_bytes=24 << 20),
        cost_estimate=cost(1 << 20, 24 << 20),
        name="assemble_early",
    )(me, mine, other, w_in, norm_two[:, None])


def late_kernel(me_ref, mine_ref, other_ref, w_ref, norm_ref, out_ref, gain_ref, rows_s):
    block = pl.program_id(0)
    groups, near = mine_ref.shape[:2]
    for g in range(groups):
        for r in range(near):
            slot_g, slot_r = me_ref[0] ^ g, me_ref[1] ^ r
            at = pl.multiple_of(g * HEAD_DIM + me_ref[2] * HALF + r * 8, 8)
            rows_s[pl.ds(at, 8), :] = mine_ref[slot_g, slot_r, 0].astype(F32)
            at = pl.multiple_of(g * HEAD_DIM + (1 - me_ref[2]) * HALF + r * 8, 8)
            rows_s[pl.ds(at, 8), :] = other_ref[slot_g, slot_r, 0].astype(F32)
    wide = rows_s[...].T
    out_ref[...] = wide
    part = jnp.sum(wide * w_ref[...].astype(F32), axis=1, keepdims=True) / norm_ref[...]

    @pl.when(block == 0)
    def _():
        gain_ref[...] = part

    @pl.when(block > 0)
    def _():
        gain_ref[...] += part


def assemble_late(me, mine, other, w_qkv, norm_one):
    groups, near, blocks = mine.shape[:3]
    pieces = blocks // 3
    width = groups * HEAD_DIM
    sums = lambda: pl.BlockSpec(
        (groups, near, 1, 8, D), lambda b, me: (0, 0, (b % pieces) * 3 + b // pieces, 0, 0)
    )
    return pl.pallas_call(
        late_kernel,
        grid_spec=pltpu.PrefetchScalarGridSpec(
            num_scalar_prefetch=1,
            grid=(blocks,),
            in_specs=[
                sums(),
                sums(),
                pl.BlockSpec((D, width), lambda b, me: (0, b)),
                pl.BlockSpec((D, 1), lambda b, me: (0, 0)),
            ],
            out_specs=[
                pl.BlockSpec((D, width), lambda b, me: (0, b)),
                pl.BlockSpec((D, 1), lambda b, me: (0, 0)),
            ],
            scratch_shapes=[pltpu.VMEM((width, D), F32)],
        ),
        out_shape=[
            jax.ShapeDtypeStruct((D, 3 * D), F32),
            jax.ShapeDtypeStruct((D, 1), F32),
        ],
        compiler_params=pltpu.CompilerParams(vmem_limit_bytes=24 << 20),
        cost_estimate=cost(1 << 20, 14 << 20),
        name="assemble_late",
    )(me, mine, other, w_qkv, norm_one[:, None])


def input_grad_kernel(parts, pieces, me_ref, *refs):
    pair, last = refs[:parts], refs[parts : 2 * parts]
    w_ref, tok_ref, norm_ref, mid_ref, out_ref, proj_s = refs[2 * parts :]
    span = proj_s.shape[1]
    for k in range(parts):
        group = me_ref[0] ^ k
        for j in range(pieces):
            if j < pieces - 1:
                piece = pair[k][...].reshape(pieces - 1, WIDE, span)[j]
            else:
                piece = last[k][...].reshape(WIDE, span)
            for part in range(3):
                at = part * D + (j * parts + group) * HEAD_DIM
                proj_s[pl.ds(pl.multiple_of(at, HEAD_DIM), HEAD_DIM), :] = piece[
                    part * HEAD_DIM : (part + 1) * HEAD_DIM
                ]
    upstream = dot(w_ref[...], proj_s[...]).T * norm_ref[...]
    values = tok_ref[...].astype(F32)
    centered = values - jnp.mean(values, axis=-1, keepdims=True)
    scale = lax.rsqrt(jnp.mean(centered * centered, axis=-1, keepdims=True) + EPSILON)
    unit = centered * scale
    flat = jnp.mean(upstream, axis=-1, keepdims=True)
    along = jnp.mean(upstream * unit, axis=-1, keepdims=True)
    out_ref[...] = mid_ref[...] + (upstream - flat - unit * along) * scale


def input_grad(me, pair, last, w_qkv, tokens, norm_one, grad_middle):
    parts = len(pair)
    span = tokens.shape[0]
    vmem = pl.BlockSpec(memory_space=pltpu.VMEM)
    return pl.pallas_call(
        functools.partial(input_grad_kernel, parts, 3),
        in_specs=[pl.BlockSpec(memory_space=pltpu.SMEM)] + [vmem] * (2 * parts + 4),
        out_specs=vmem,
        out_shape=jax.ShapeDtypeStruct((span, D), F32),
        scratch_shapes=[pltpu.VMEM((3 * D, span), BF16)],
        compiler_params=pltpu.CompilerParams(vmem_limit_bytes=40 << 20),
        cost_estimate=cost(2 * span * 3 * D * D, 10 << 20),
        name="input_grad",
    )(me, *pair, *last, w_qkv, tokens, norm_one[None, :], grad_middle)


def swap(values, axis, k):
    size = lax.axis_size(axis)
    return lax.ppermute(values, axis, [(i, i ^ k) for i in range(size)])


def add(*terms):
    total = terms[0].astype(F32)
    for term in terms[1:]:
        total += term.astype(F32)
    return total.astype(BF16)


def scatter_seq(slots):
    half = slots.shape[1] // 2
    a, b = slots[:, :half], slots[:, half:]
    from_one = swap(jnp.concatenate([a[1:2], a[3:4]]), "seq", 1)
    from_two = swap(jnp.concatenate([b[2:3], b[3:4]]), "seq", 2)
    a_two = swap(add(a[2], from_one[1]), "seq", 2)
    b_one = swap(add(b[1], from_two[1]), "seq", 1)
    return add(a[0], from_one[0], a_two), add(b[0], from_two[0], b_one)


def gather_seq(values):
    half = values.shape[0] // 2
    one, two = swap(values, "seq", 1), swap(values, "seq", 2)
    first, second = swap(two[:half], "seq", 1), swap(one[half:], "seq", 2)
    return jnp.stack([values, one, two, jnp.concatenate([first, second])])


def scatter_near(slots):
    return add(slots[0], *[swap(slots[k], "near", k) for k in range(1, len(slots))])


def gather_near(values):
    return jnp.stack([values] + [swap(values, "near", k) for k in range(1, lax.axis_size("near"))])


def tie(*values):
    return lax.optimization_barrier(values)


def on_device(tokens, doc_start, cotangent, norm_one, w_qkv, w_out, norm_two, w_in, w_down):
    parts = lax.axis_size("seq")
    near = lax.axis_size("near")
    far = lax.axis_size("far")
    span = tokens.shape[1]
    total = span * parts
    pieces = HEADS // parts
    bq = min(512, span)
    me_seq = lax.axis_index("seq").astype(jnp.int32)
    me = jnp.stack([lax.axis_index(a).astype(jnp.int32) for a in ("seq", "near", "core")])
    first_token = me_seq * span
    starts = doc_start[0]
    key_doc = starts[:, None]
    query_doc = starts[None, :]

    frequency = ROTARY_BASE ** (-(jnp.arange(HALF, dtype=F32) * 2.0 / HEAD_DIM))
    offset = (jnp.arange(total, dtype=jnp.int32) - starts).astype(F32)
    angles = frequency[:, None] * offset[None, :]
    cosine, sine = jnp.cos(angles), jnp.sin(angles)
    own_cosine = lax.dynamic_slice_in_dim(cosine, first_token, span, axis=1)
    own_sine = lax.dynamic_slice_in_dim(sine, first_token, span, axis=1)

    def exchange(values):
        return lax.all_to_all(values, "seq", split_axis=0, concat_axis=0, tiled=True)

    def sum_far(values):
        return lax.psum(values, "far") if far > 1 else values

    hidden = tokens[0].astype(F32)
    hn = layer_norm(hidden, norm_one).astype(BF16)
    qkv = []
    for j in range(pieces):
        sent = project(me, hn, w_qkv, own_cosine, own_sine, j, parts)
        qkv.append([sent] + [swap(sent[k], "seq", k) for k in range(1, parts)])
    hn_row = lax.all_gather(hn, "seq")
    contexts, lses = [], []
    for j in range(pieces):
        context, lse = attend_forward(me, qkv[j], key_doc, query_doc, bq)
        contexts.append(context)
        lses.append(lse)
    arrived = exchange(jnp.stack(contexts, axis=1))
    context_t = arrived.transpose(1, 0, 2, 3).reshape(D, span)

    attended = lax.dot_general(
        context_t, w_out, (((0,), (0,)), ((), ())), preferred_element_type=F32
    )
    middle = hidden + attended
    normed_two, norm_two_back = jax.vjp(lambda u: layer_norm(u, norm_two), middle)
    normed_two_low = normed_two.astype(BF16)
    gate_up = dot(normed_two_low, w_in)
    inner, gelu_back = jax.vjp(gelu_gate, gate_up[:, :FF], gate_up[:, FF:])
    inner_low = inner.astype(BF16)
    grad_out = cotangent[0]
    grad_inner = jnp.einsum("td,fd->tf", grad_out, w_down, preferred_element_type=F32)
    grad_gate, grad_up = gelu_back(grad_inner)
    grad_gate_up = jnp.concatenate([grad_gate, grad_up], axis=-1).astype(BF16)
    grad_normed_two = jnp.einsum("tf,df->td", grad_gate_up, w_in, preferred_element_type=F32)
    (grad_middle_part,) = norm_two_back(grad_normed_two)
    grad_middle = grad_out.astype(F32) + grad_middle_part
    grad_mid_low = grad_middle.astype(BF16)
    grad_context_t = lax.dot_general(
        w_out, grad_mid_low, (((1,), (1,)), ((), ())), preferred_element_type=F32
    ).astype(BF16)
    grad_context_t, inner_low, normed_two_low, hn_row = tie(
        grad_context_t, inner_low, normed_two_low, hn_row
    )
    upstream = exchange(
        grad_context_t.reshape(pieces, parts, HEAD_DIM, span).transpose(1, 0, 2, 3)
    )
    keep, give = early_grads(
        me, normed_two_low, grad_gate_up, inner_low, grad_out, context_t, grad_mid_low, parts, near
    )
    result = (middle + dot(inner_low, w_down)).astype(BF16)
    taken = swap(give, "core", 1)
    taken, upstream = tie(taken, upstream)
    early_a, early_b = scatter_seq(add(keep, taken))

    def backward(j, *inputs):
        return attend_backward(
            me, qkv[j], key_doc, query_doc, upstream, j, contexts[j], lses[j], cosine, sine, bq
        )

    grads = [backward(0), backward(1)]
    grads[1], early_a, early_b, upstream = tie(grads[1], early_a, early_b, upstream)
    own = jnp.stack([grads[0], grads[1]], axis=1)
    pair = [own[0]] + [swap(own[k], "seq", k) for k in range(1, parts)]
    early = scatter_near([early_a[0], early_a[1], early_b[0], early_b[1]])
    grads.append(backward(2))
    grads[2], early, pair = tie(grads[2], early, pair)
    early = gather_near(sum_far(early))
    last = [grads[2][0]] + [swap(grads[2][k], "seq", k) for k in range(1, parts)]

    kept, given = late_grads(me, grads, hn_row, near)
    late = sum_far(scatter_near(add(kept, swap(given, "core", 1))))
    late = gather_near(late)
    grad_input = input_grad(me, pair, last, w_qkv, tokens[0], norm_one, grad_middle)
    early = gather_seq(early)
    late = gather_seq(late)
    sum_w_in, sum_w_down, sum_w_out, sum_norm_two = assemble_early(
        me, early, swap(early, "core", 1), w_in, norm_two
    )
    sum_w_qkv, sum_norm_one = assemble_late(me, late, swap(late, "core", 1), w_qkv, norm_one)
    return (
        result[None],
        grad_input[None],
        sum_norm_one[:, 0],
        sum_w_qkv,
        sum_w_out,
        sum_norm_two[:, 0],
        sum_w_in,
        sum_w_down,
    )


def solution(mesh):
    parts = mesh.shape["seq"]
    near = min(4, mesh.shape["dp"] // 2)
    split = Mesh(mesh.devices.reshape(parts, -1, near, 2), ("seq", "far", "near", "core"))
    rows = ("far", "near", "core")
    tokens_at = P(rows, "seq", None)
    return jax.shard_map(
        on_device,
        mesh=split,
        in_specs=(tokens_at, P(rows, None), tokens_at, P(), P(), P(), P(), P(), P()),
        out_specs=(tokens_at, tokens_at, P(), P(), P(), P(), P(), P()),
        check_vma=False,
    )
```

```python
import functools

import jax
import jax.numpy as jnp
from jax import lax
from jax.experimental import pallas as pl
from jax.experimental.pallas import tpu as pltpu
from jax.sharding import Mesh
from jax.sharding import PartitionSpec as P

D = 768
HEADS = 12
HEAD_DIM = 64
HALF = HEAD_DIM // 2
FF = 1152
WIDE = 3 * HEAD_DIM
LANES = D // 2

EPSILON = 1e-05
ROTARY_BASE = 160000.0
SCORE_SCALE = 0.125
SCORE_EXP2 = SCORE_SCALE * 1.4426950408889634
MASKED_SCORE = -1e30
KEY_CHUNK = 256
F32 = jnp.float32
BF16 = jnp.bfloat16

dot = functools.partial(jnp.dot, preferred_element_type=F32)


def cost(flops, moved, transcendentals=0):
    return pl.CostEstimate(flops=flops, bytes_accessed=moved, transcendentals=transcendentals)


def layer_norm(values, gain_vec):
    average = jnp.mean(values, axis=-1, keepdims=True)
    centered = values - average
    variance = jnp.mean(centered * centered, axis=-1, keepdims=True)
    return centered * lax.rsqrt(variance + EPSILON) * gain_vec


def gelu_gate(gate_part, up_part):
    return jax.nn.gelu(gate_part, approximate=False) * up_part


def project_kernel(me_ref, hn_ref, w_ref, cos_ref, sin_ref, out_ref):
    part = pl.program_id(0)
    turned = dot(hn_ref[...], w_ref[...]).T
    cosine = jnp.where(part < 2, cos_ref[...], 1.0)
    sine = jnp.where(part < 2, sin_ref[...], 0.0)
    row = pl.multiple_of(part * HEAD_DIM, HEAD_DIM)
    for g in range(out_ref.shape[0]):
        slot = me_ref[0] ^ g
        first = turned[g * HEAD_DIM : g * HEAD_DIM + HALF]
        second = turned[g * HEAD_DIM + HALF : (g + 1) * HEAD_DIM]
        out_ref[slot, pl.ds(row, HALF), :] = (first * cosine - second * sine).astype(BF16)
        out_ref[slot, pl.ds(row + HALF, HALF), :] = (second * cosine + first * sine).astype(BF16)


def project(me, hn, w_qkv, cosine, sine, piece, groups):
    tokens = hn.shape[0]
    width = groups * HEAD_DIM
    pieces = D // width
    return pl.pallas_call(
        project_kernel,
        grid_spec=pltpu.PrefetchScalarGridSpec(
            num_scalar_prefetch=1,
            grid=(3,),
            in_specs=[
                pl.BlockSpec((tokens, D), lambda i, me: (0, 0)),
                pl.BlockSpec((D, width), lambda i, me: (0, i * pieces + piece)),
                pl.BlockSpec((HALF, tokens), lambda i, me: (0, 0)),
                pl.BlockSpec((HALF, tokens), lambda i, me: (0, 0)),
            ],
            out_specs=pl.BlockSpec((groups, WIDE, tokens), lambda i, me: (0, 0, 0)),
        ),
        out_shape=jax.ShapeDtypeStruct((groups, WIDE, tokens), BF16),
        compiler_params=pltpu.CompilerParams(vmem_limit_bytes=32 << 20),
        cost_estimate=cost(6 * tokens * D * width, 4 << 20),
        name="project",
    )(me, hn, w_qkv, cosine, sine)


def mask_scores(scores, chunk, chunks, edge, key_doc, query_doc, query_main):
    if chunk == 0 or chunk == chunks - 1:
        own = key_doc[chunk * KEY_CHUNK : (chunk + 1) * KEY_CHUNK, :]
        return jnp.where(own == query_doc, scores, MASKED_SCORE)
    if edge:
        return jnp.where(query_main, scores, MASKED_SCORE)
    return scores


def put_in_order(me, slots, qkv_s, key_s, value_s=None):
    span = qkv_s.shape[2]
    for k, ref in enumerate(slots):
        at = me ^ k
        piece = ref[...].reshape(WIDE, span)
        qkv_s[at] = piece
        rows = pl.ds(pl.multiple_of(at * span, span), span)
        key_s[rows, :] = piece[HEAD_DIM : 2 * HEAD_DIM].astype(F32).T.astype(BF16)
        if value_s is not None:
            value_s[rows, :] = piece[2 * HEAD_DIM :].astype(F32).T.astype(BF16)


def slot_specs(slots):
    own = pl.BlockSpec((1,) + slots[0].shape[1:], lambda i, me: (0, 0, 0))
    rest = [pl.BlockSpec(s.shape, lambda i, me: (0, 0)) for s in slots[1:]]
    return [own] + rest


def forward_kernel(bq, parts, me_ref, *refs):
    slots = refs[:parts]
    kdoc_ref, qdoc_ref, out_ref, lse_ref, qkv_s, key_s, score_s = refs[parts:]
    step = pl.program_id(0)
    steps = pl.num_programs(0)
    total = key_s.shape[0]
    chunks = total // KEY_CHUNK
    span = qkv_s.shape[2]
    ratio = span // bq

    @pl.when(step == 0)
    def _():
        put_in_order(me_ref[0], slots, qkv_s, key_s)

    def run(edge):
        lanes = pl.ds(pl.multiple_of((step % ratio) * bq, bq), bq)
        queries = qkv_s[step // ratio, 0:HEAD_DIM, lanes]
        query_doc = qdoc_ref[...]
        query_main = query_doc == kdoc_ref[total // 2 : total // 2 + 1, :]
        top = None
        for c in range(chunks):
            rows = slice(c * KEY_CHUNK, (c + 1) * KEY_CHUNK)
            scores = dot(key_s[rows, :], queries)
            scores = mask_scores(scores, c, chunks, edge, kdoc_ref, query_doc, query_main)
            score_s[rows, :] = scores
            peak = jnp.max(scores.reshape(KEY_CHUNK // 8, 8, bq), axis=0)
            top = peak if top is None else jnp.maximum(top, peak)
        top = jnp.max(top, axis=0, keepdims=True) * SCORE_EXP2
        mass, acc = None, None
        for c in range(chunks):
            rows = slice(c * KEY_CHUNK, (c + 1) * KEY_CHUNK)
            weight = jnp.exp2(score_s[rows, :] * SCORE_EXP2 - top)
            part = jnp.sum(weight.reshape(KEY_CHUNK // 8, 8, bq), axis=0)
            mass = part if mass is None else mass + part
            at = c * KEY_CHUNK % span
            values = qkv_s[c * KEY_CHUNK // span, 2 * HEAD_DIM :, at : at + KEY_CHUNK]
            term = dot(values, weight.astype(BF16))
            acc = term if acc is None else acc + term
        mass = jnp.sum(mass, axis=0, keepdims=True)
        out_ref[0] = (acc / mass).astype(BF16)
        lse_ref[...] = top + jnp.log2(mass)

    at_edge = (step == 0) | (step == steps - 1)
    pl.when(at_edge)(lambda: run(True))
    pl.when(jnp.logical_not(at_edge))(lambda: run(False))


def attend_forward(me, slots, key_doc, query_doc, bq):
    parts, _, span = slots[0].shape
    total = parts * span
    ratio = span // bq
    return pl.pallas_call(
        functools.partial(forward_kernel, bq, parts),
        grid_spec=pltpu.PrefetchScalarGridSpec(
            num_scalar_prefetch=1,
            grid=(total // bq,),
            in_specs=slot_specs(slots)
            + [
                pl.BlockSpec((total, 1), lambda i, me: (0, 0)),
                pl.BlockSpec((1, bq), lambda i, me: (0, i)),
            ],
            out_specs=[
                pl.BlockSpec((1, HEAD_DIM, bq), lambda i, me: (i // ratio, 0, i % ratio)),
                pl.BlockSpec((1, bq), lambda i, me: (0, i)),
            ],
            scratch_shapes=[
                pltpu.VMEM((parts, WIDE, span), BF16),
                pltpu.VMEM((total, HEAD_DIM), BF16),
                pltpu.VMEM((total, bq), F32),
            ],
        ),
        out_shape=[
            jax.ShapeDtypeStruct((parts, HEAD_DIM, span), BF16),
            jax.ShapeDtypeStruct((1, total), F32),
        ],
        compiler_params=pltpu.CompilerParams(vmem_limit_bytes=40 << 20),
        cost_estimate=cost(16 * HEAD_DIM * total * total, 4 << 20, total * total),
        name="attend_forward",
    )(me, *slots, key_doc, query_doc)


def backward_kernel(bq, parts, me_ref, *refs):
    slots, ups = refs[:parts], refs[parts : 2 * parts]
    (kdoc_ref, qdoc_ref, o_ref, lse_ref, cos_ref, sin_ref, grad_ref,
     qkv_s, key_s, value_s, up_s, dk_s, dv_s) = refs[2 * parts :]
    step = pl.program_id(0)
    steps = pl.num_programs(0)
    total = key_s.shape[0]
    chunks = total // KEY_CHUNK
    span = qkv_s.shape[2]
    ratio = span // bq

    @pl.when(step == 0)
    def _():
        put_in_order(me_ref[0], slots, qkv_s, key_s, value_s)
        for k, ref in enumerate(ups):
            up_s[me_ref[0] ^ k] = ref[...].reshape(HEAD_DIM, span)
        dk_s[...] = jnp.zeros_like(dk_s)
        dv_s[...] = jnp.zeros_like(dv_s)

    def turn_back(grad, cosine, sine):
        first, second = grad[:HALF], grad[HALF:]
        return first * cosine + second * sine, second * cosine - first * sine

    def run(edge):
        lanes = pl.ds(pl.multiple_of((step % ratio) * bq, bq), bq)
        here = pl.ds(pl.multiple_of(step * bq, bq), bq)
        queries = qkv_s[step // ratio, 0:HEAD_DIM, lanes]
        upstream = up_s[step // ratio, :, lanes]
        wide_up = upstream.astype(F32)
        centre = jnp.sum(wide_up * o_ref[0].astype(F32), axis=0, keepdims=True)
        query_rows = queries.astype(F32).T.astype(BF16)
        up_rows = wide_up.T.astype(BF16)
        query_doc = qdoc_ref[...]
        query_main = query_doc == kdoc_ref[total // 2 : total // 2 + 1, :]
        lse = lse_ref[...]
        dq = None
        for c in range(chunks):
            rows = slice(c * KEY_CHUNK, (c + 1) * KEY_CHUNK)
            scores = dot(key_s[rows, :], queries)
            scores = mask_scores(scores, c, chunks, edge, kdoc_ref, query_doc, query_main)
            probs = jnp.exp2(scores * SCORE_EXP2 - lse)
            grad_prob = dot(value_s[rows, :], upstream)
            grad_scores = (probs * (grad_prob - centre)).astype(BF16)
            dv_s[rows, :] += dot(probs.astype(BF16), up_rows)
            dk_s[rows, :] += dot(grad_scores, query_rows)
            at = c * KEY_CHUNK % span
            keys = qkv_s[c * KEY_CHUNK // span, HEAD_DIM : 2 * HEAD_DIM, at : at + KEY_CHUNK]
            term = dot(keys, grad_scores)
            dq = term if dq is None else dq + term
        one, two = turn_back(dq * SCORE_SCALE, cos_ref[:, here], sin_ref[:, here])
        slot = me_ref[0] ^ (step // ratio)
        grad_ref[slot, 0:HALF, lanes] = one.astype(BF16)
        grad_ref[slot, HALF:HEAD_DIM, lanes] = two.astype(BF16)

    at_edge = (step == 0) | (step == steps - 1)
    pl.when(at_edge)(lambda: run(True))
    pl.when(jnp.logical_not(at_edge))(lambda: run(False))

    @pl.when(step == steps - 1)
    def _():
        for s in range(parts):
            slot = me_ref[0] ^ s
            rows = slice(s * span, (s + 1) * span)
            one, two = turn_back(dk_s[rows, :].T * SCORE_SCALE, cos_ref[:, rows], sin_ref[:, rows])
            grad_ref[slot, HEAD_DIM : HEAD_DIM + HALF, :] = one.astype(BF16)
            grad_ref[slot, HEAD_DIM + HALF : 2 * HEAD_DIM, :] = two.astype(BF16)
            grad_ref[slot, 2 * HEAD_DIM :, :] = dv_s[rows, :].T.astype(BF16)


def attend_backward(me, slots, key_doc, query_doc, upstream, piece, context, lse, cosine, sine, bq):
    parts, _, span = slots[0].shape
    total = parts * span
    ratio = span // bq
    return pl.pallas_call(
        functools.partial(backward_kernel, bq, parts),
        grid_spec=pltpu.PrefetchScalarGridSpec(
            num_scalar_prefetch=1,
            grid=(total // bq,),
            in_specs=slot_specs(slots)
            + [pl.BlockSpec((1, 1, HEAD_DIM, span), lambda i, me: (0, piece, 0, 0))]
            + [pl.BlockSpec((1, HEAD_DIM, span), lambda i, me: (piece, 0, 0))] * (parts - 1)
            + [
                pl.BlockSpec((total, 1), lambda i, me: (0, 0)),
                pl.BlockSpec((1, bq), lambda i, me: (0, i)),
                pl.BlockSpec((1, HEAD_DIM, bq), lambda i, me: (i // ratio, 0, i % ratio)),
                pl.BlockSpec((1, bq), lambda i, me: (0, i)),
                pl.BlockSpec((HALF, total), lambda i, me: (0, 0)),
                pl.BlockSpec((HALF, total), lambda i, me: (0, 0)),
            ],
            out_specs=pl.BlockSpec((parts, WIDE, span), lambda i, me: (0, 0, 0)),
            scratch_shapes=[
                pltpu.VMEM((parts, WIDE, span), BF16),
                pltpu.VMEM((total, HEAD_DIM), BF16),
                pltpu.VMEM((total, HEAD_DIM), BF16),
                pltpu.VMEM((parts, HEAD_DIM, span), BF16),
                pltpu.VMEM((total, HEAD_DIM), F32),
                pltpu.VMEM((total, HEAD_DIM), F32),
            ],
        ),
        out_shape=jax.ShapeDtypeStruct((parts, WIDE, span), BF16),
        compiler_params=pltpu.CompilerParams(vmem_limit_bytes=40 << 20),
        cost_estimate=cost(40 * HEAD_DIM * total * total, 6 << 20, total * total),
        name="attend_backward",
    )(me, *slots, *upstream, key_doc, query_doc, context, lse, cosine, sine)


def context_grad_kernel(me_ref, w_ref, mid_ref, out_ref):
    parts, pieces = out_ref.shape[:2]
    grads = lax.dot_general(
        w_ref[...], mid_ref[...], (((1,), (1,)), ((), ())), preferred_element_type=F32
    ).astype(BF16)
    for j in range(pieces):
        for g in range(parts):
            at = (j * parts + g) * HEAD_DIM
            out_ref[me_ref[0] ^ g, j] = grads[at : at + HEAD_DIM]


def context_grad(me, w_out, mid, parts):
    span = mid.shape[0]
    vmem = pl.BlockSpec(memory_space=pltpu.VMEM)
    return pl.pallas_call(
        context_grad_kernel,
        in_specs=[pl.BlockSpec(memory_space=pltpu.SMEM), vmem, vmem],
        out_specs=vmem,
        out_shape=jax.ShapeDtypeStruct((parts, HEADS // parts, HEAD_DIM, span), BF16),
        compiler_params=pltpu.CompilerParams(vmem_limit_bytes=24 << 20),
        cost_estimate=cost(2 * span * D * D, 3 << 20),
        name="context_grad",
    )(me, w_out, mid)


def early_grad_kernel(me_ref, n2_ref, gu_ref, inner_ref, cot_ref, ctx_ref, mid_ref, keep_ref, give_ref):
    parts, near = keep_ref.shape[:2]
    rows = D // (2 * parts * near)
    low = me_ref[2] == 0

    def put(first, second, count, at):
        kept = jnp.where(low, first, second).astype(BF16)
        given = jnp.where(low, second, first).astype(BF16)
        for s in range(parts):
            for r in range(near):
                here = slice((s * near + r) * count, (s * near + r + 1) * count)
                slot_s, slot_r = me_ref[0] ^ s, me_ref[1] ^ r
                keep_ref[slot_s, slot_r, at : at + count, :] = kept[here]
                give_ref[slot_s, slot_r, at : at + count, :] = given[here]

    n2_t = n2_ref[...].astype(F32).T.astype(BF16)
    for u in range(2 * FF // LANES):
        block = dot(n2_t, gu_ref[:, u * LANES : (u + 1) * LANES])
        put(block[: D // 2], block[D // 2 :], rows, u * rows)
    inner_t = inner_ref[...].astype(F32).T.astype(BF16)
    down = dot(inner_t, cot_ref[...])
    put(down[:, :LANES], down[:, LANES:], 3 * rows, 6 * rows)
    for u in range(2):
        block = dot(ctx_ref[...], mid_ref[:, u * LANES : (u + 1) * LANES])
        put(block[: D // 2], block[D // 2 :], rows, (9 + u) * rows)


def early_grads(me, n2, gate_up, inner, cotangent, context_t, mid, parts, near):
    rows = D // (2 * parts * near)
    shape = jax.ShapeDtypeStruct((parts, near, 11 * rows, LANES), BF16)
    operands = (n2, gate_up, inner, cotangent, context_t, mid)
    once = lambda a: pl.BlockSpec(a.shape, lambda i, me: (0,) * len(a.shape))
    return pl.pallas_call(
        early_grad_kernel,
        grid_spec=pltpu.PrefetchScalarGridSpec(
            num_scalar_prefetch=1,
            grid=(1,),
            in_specs=[once(a) for a in operands],
            out_specs=[once(shape), once(shape)],
        ),
        out_shape=[shape, shape],
        compiler_params=pltpu.CompilerParams(vmem_limit_bytes=44 << 20),
        cost_estimate=cost(2 * n2.shape[0] * 4224 * D, 14 << 20),
        name="early_grads",
    )(me, *operands)


def late_grad_kernel(pieces, me_ref, *refs):
    grads = refs[:pieces]
    hn_ref, keep_ref, give_ref = refs[pieces:]
    parts = hn_ref.shape[0]
    near = keep_ref.shape[0]
    low = me_ref[2] == 0
    for j, ref in enumerate(grads):
        block = None
        for s in range(parts):
            term = dot(ref[s], hn_ref[s])
            block = term if block is None else block + term
        for part in range(3):
            head = block[part * HEAD_DIM : (part + 1) * HEAD_DIM]
            first, second = head[:HALF], head[HALF:]
            kept = jnp.where(low, first, second).astype(BF16)
            given = jnp.where(low, second, first).astype(BF16)
            for r in range(near):
                slot = me_ref[1] ^ r
                keep_ref[slot, 3 * j + part] = kept[8 * r : 8 * r + 8]
                give_ref[slot, 3 * j + part] = given[8 * r : 8 * r + 8]


def late_grads(me, grads, hn_row, near):
    pieces = len(grads)
    shape = jax.ShapeDtypeStruct((near, 3 * pieces, 8, D), BF16)
    vmem = pl.BlockSpec(memory_space=pltpu.VMEM)
    return pl.pallas_call(
        functools.partial(late_grad_kernel, pieces),
        in_specs=[pl.BlockSpec(memory_space=pltpu.SMEM)] + [vmem] * (pieces + 1),
        out_specs=[vmem, vmem],
        out_shape=[shape, shape],
        compiler_params=pltpu.CompilerParams(vmem_limit_bytes=32 << 20),
        cost_estimate=cost(2 * 2048 * 576 * D, 6 << 20),
        name="late_grads",
    )(me, *grads, hn_row)


def early_kernel(me_ref, mine_ref, other_ref, w_ref, norm_ref, win_ref, wdown_ref, wout_ref, gain_ref):
    near = mine_ref.shape[1]
    parts = pl.num_programs(0) // 2
    rows = D // (2 * parts * near)

    def run(ref):
        for r in range(near):
            piece = ref[0, me_ref[1] ^ r].astype(F32)
            here = slice(r * rows, (r + 1) * rows)
            wide = jnp.concatenate([piece[rows * u : rows * (u + 1)] for u in range(6)], axis=1)
            win_ref[here, :] = wide
            part = wide * w_ref[here, :].astype(F32)
            gain_ref[here, :] = jnp.sum(part, axis=1, keepdims=True) / norm_ref[here, :]
            wdown_ref[3 * r * rows : 3 * (r + 1) * rows, :] = piece[6 * rows : 9 * rows]
            wout_ref[here, :LANES] = piece[9 * rows : 10 * rows]
            wout_ref[here, LANES:] = piece[10 * rows :]

    ours = (pl.program_id(0) // parts) == me_ref[2]
    pl.when(ours)(lambda: run(mine_ref))
    pl.when(jnp.logical_not(ours))(lambda: run(other_ref))


def assemble_early(me, mine, other, w_in, norm_two):
    parts, near = mine.shape[:2]
    steps = 2 * parts
    rows = D // steps

    def slot(own):
        def index(p, me):
            used = (p // parts == me[2]) == own
            return (jnp.where(used, me[0] ^ (p % parts), 0), 0, 0, 0)

        return pl.BlockSpec((1,) + mine.shape[1:], index)

    return pl.pallas_call(
        early_kernel,
        grid_spec=pltpu.PrefetchScalarGridSpec(
            num_scalar_prefetch=1,
            grid=(steps,),
            in_specs=[
                slot(True),
                slot(False),
                pl.BlockSpec((rows, 2 * FF), lambda p, me: (p, 0)),
                pl.BlockSpec((rows, 1), lambda p, me: (p, 0)),
            ],
            out_specs=[
                pl.BlockSpec((rows, 2 * FF), lambda p, me: (p, 0)),
                pl.BlockSpec((3 * rows, LANES), lambda p, me: (p % parts, p // parts)),
                pl.BlockSpec((rows, D), lambda p, me: (p, 0)),
                pl.BlockSpec((rows, 1), lambda p, me: (p, 0)),
            ],
        ),
        out_shape=[
            jax.ShapeDtypeStruct((D, 2 * FF), F32),
            jax.ShapeDtypeStruct((FF, D), F32),
            jax.ShapeDtypeStruct((D, D), F32),
            jax.ShapeDtypeStruct((D, 1), F32),
        ],
        compiler_params=pltpu.CompilerParams(vmem_limit_bytes=24 << 20),
        cost_estimate=cost(1 << 20, 24 << 20),
        name="assemble_early",
    )(me, mine, other, w_in, norm_two[:, None])


def late_kernel(me_ref, mine_ref, other_ref, w_ref, norm_ref, out_ref, gain_ref, rows_s):
    block = pl.program_id(0)
    groups, near = mine_ref.shape[:2]
    for g in range(groups):
        for r in range(near):
            slot_g, slot_r = me_ref[0] ^ g, me_ref[1] ^ r
            at = pl.multiple_of(g * HEAD_DIM + me_ref[2] * HALF + r * 8, 8)
            rows_s[pl.ds(at, 8), :] = mine_ref[slot_g, slot_r, 0].astype(F32)
            at = pl.multiple_of(g * HEAD_DIM + (1 - me_ref[2]) * HALF + r * 8, 8)
            rows_s[pl.ds(at, 8), :] = other_ref[slot_g, slot_r, 0].astype(F32)
    wide = rows_s[...].T
    out_ref[...] = wide
    part = jnp.sum(wide * w_ref[...].astype(F32), axis=1, keepdims=True) / norm_ref[...]

    @pl.when(block == 0)
    def _():
        gain_ref[...] = part

    @pl.when(block > 0)
    def _():
        gain_ref[...] += part


def assemble_late(me, mine, other, w_qkv, norm_one):
    groups, near, blocks = mine.shape[:3]
    pieces = blocks // 3
    width = groups * HEAD_DIM
    sums = lambda: pl.BlockSpec(
        (groups, near, 1, 8, D), lambda b, me: (0, 0, (b % pieces) * 3 + b // pieces, 0, 0)
    )
    return pl.pallas_call(
        late_kernel,
        grid_spec=pltpu.PrefetchScalarGridSpec(
            num_scalar_prefetch=1,
            grid=(blocks,),
            in_specs=[
                sums(),
                sums(),
                pl.BlockSpec((D, width), lambda b, me: (0, b)),
                pl.BlockSpec((D, 1), lambda b, me: (0, 0)),
            ],
            out_specs=[
                pl.BlockSpec((D, width), lambda b, me: (0, b)),
                pl.BlockSpec((D, 1), lambda b, me: (0, 0)),
            ],
            scratch_shapes=[pltpu.VMEM((width, D), F32)],
        ),
        out_shape=[
            jax.ShapeDtypeStruct((D, 3 * D), F32),
            jax.ShapeDtypeStruct((D, 1), F32),
        ],
        compiler_params=pltpu.CompilerParams(vmem_limit_bytes=24 << 20),
        cost_estimate=cost(1 << 20, 14 << 20),
        name="assemble_late",
    )(me, mine, other, w_qkv, norm_one[:, None])


def input_grad_kernel(parts, pieces, me_ref, *refs):
    pair, last = refs[:parts], refs[parts : 2 * parts]
    w_ref, tok_ref, norm_ref, mid_ref, out_ref, proj_s = refs[2 * parts :]
    span = proj_s.shape[1]
    for k in range(parts):
        group = me_ref[0] ^ k
        for j in range(pieces):
            if j < pieces - 1:
                piece = pair[k][...].reshape(pieces - 1, WIDE, span)[j]
            else:
                piece = last[k][...].reshape(WIDE, span)
            for part in range(3):
                at = part * D + (j * parts + group) * HEAD_DIM
                proj_s[pl.ds(pl.multiple_of(at, HEAD_DIM), HEAD_DIM), :] = piece[
                    part * HEAD_DIM : (part + 1) * HEAD_DIM
                ]
    upstream = dot(w_ref[...], proj_s[...]).T * norm_ref[...]
    values = tok_ref[...].astype(F32)
    centered = values - jnp.mean(values, axis=-1, keepdims=True)
    scale = lax.rsqrt(jnp.mean(centered * centered, axis=-1, keepdims=True) + EPSILON)
    unit = centered * scale
    flat = jnp.mean(upstream, axis=-1, keepdims=True)
    along = jnp.mean(upstream * unit, axis=-1, keepdims=True)
    out_ref[...] = mid_ref[...] + (upstream - flat - unit * along) * scale


def input_grad(me, pair, last, w_qkv, tokens, norm_one, grad_middle):
    parts = len(pair)
    span = tokens.shape[0]
    vmem = pl.BlockSpec(memory_space=pltpu.VMEM)
    return pl.pallas_call(
        functools.partial(input_grad_kernel, parts, 3),
        in_specs=[pl.BlockSpec(memory_space=pltpu.SMEM)] + [vmem] * (2 * parts + 4),
        out_specs=vmem,
        out_shape=jax.ShapeDtypeStruct((span, D), F32),
        scratch_shapes=[pltpu.VMEM((3 * D, span), BF16)],
        compiler_params=pltpu.CompilerParams(vmem_limit_bytes=40 << 20),
        cost_estimate=cost(2 * span * 3 * D * D, 10 << 20),
        name="input_grad",
    )(me, *pair, *last, w_qkv, tokens, norm_one[None, :], grad_middle)


def swap(values, axis, k):
    size = lax.axis_size(axis)
    return lax.ppermute(values, axis, [(i, i ^ k) for i in range(size)])


def add(*terms):
    total = terms[0].astype(F32)
    for term in terms[1:]:
        total += term.astype(F32)
    return total.astype(BF16)


def scatter_near(slots):
    return add(slots[0], *[swap(slots[k], "near", k) for k in range(1, len(slots))])


def gather_near(values):
    return jnp.stack([values] + [swap(values, "near", k) for k in range(1, lax.axis_size("near"))])


def tie(*values):
    return lax.optimization_barrier(values)


def on_device(tokens, doc_start, cotangent, norm_one, w_qkv, w_out, norm_two, w_in, w_down):
    parts = lax.axis_size("seq")
    near = lax.axis_size("near")
    far = lax.axis_size("far")
    span = tokens.shape[1]
    total = span * parts
    pieces = HEADS // parts
    bq = min(512, span)
    me_seq = lax.axis_index("seq").astype(jnp.int32)
    me = jnp.stack([lax.axis_index(a).astype(jnp.int32) for a in ("seq", "near", "core")])
    first_token = me_seq * span
    starts = doc_start[0]
    key_doc = starts[:, None]
    query_doc = starts[None, :]

    frequency = ROTARY_BASE ** (-(jnp.arange(HALF, dtype=F32) * 2.0 / HEAD_DIM))
    offset = (jnp.arange(total, dtype=jnp.int32) - starts).astype(F32)
    angles = frequency[:, None] * offset[None, :]
    cosine, sine = jnp.cos(angles), jnp.sin(angles)
    own_cosine = lax.dynamic_slice_in_dim(cosine, first_token, span, axis=1)
    own_sine = lax.dynamic_slice_in_dim(sine, first_token, span, axis=1)

    def exchange(values):
        return lax.all_to_all(values, "seq", split_axis=0, concat_axis=0, tiled=True)

    def sum_far(values):
        return lax.psum(values, "far") if far > 1 else values

    hidden = tokens[0].astype(F32)
    hn = layer_norm(hidden, norm_one).astype(BF16)
    qkv = []
    for j in range(pieces):
        sent = project(me, hn, w_qkv, own_cosine, own_sine, j, parts)
        qkv.append([sent] + [swap(sent[k], "seq", k) for k in range(1, parts)])
    contexts, lses = [], []
    for j in range(pieces):
        if j == pieces - 1:
            hn_late, qkv[j] = tie(hn, qkv[j])
            hn_near = [swap(hn_late, "seq", 1), swap(hn_late, "seq", 2)]
        context, lse = attend_forward(me, qkv[j], key_doc, query_doc, bq)
        contexts.append(context)
        lses.append(lse)
    arrived = exchange(jnp.stack(contexts, axis=1))
    arrived, hn_near = tie(arrived, hn_near)
    hn_far = [swap(hn_near[1][: span // 2], "seq", 1), swap(hn_near[0][span // 2 :], "seq", 2)]
    context_t = arrived.transpose(1, 0, 2, 3).reshape(D, span)

    attended = lax.dot_general(
        context_t, w_out, (((0,), (0,)), ((), ())), preferred_element_type=F32
    )
    middle = hidden + attended
    normed_two, norm_two_back = jax.vjp(lambda u: layer_norm(u, norm_two), middle)
    normed_two_low = normed_two.astype(BF16)
    gate_up = dot(normed_two_low, w_in)
    inner, gelu_back = jax.vjp(gelu_gate, gate_up[:, :FF], gate_up[:, FF:])
    inner_low = inner.astype(BF16)
    grad_out = cotangent[0]
    grad_inner = jnp.einsum("td,fd->tf", grad_out, w_down, preferred_element_type=F32)
    grad_gate, grad_up = gelu_back(grad_inner)
    grad_gate_up = jnp.concatenate([grad_gate, grad_up], axis=-1).astype(BF16)
    grad_normed_two = jnp.einsum("tf,df->td", grad_gate_up, w_in, preferred_element_type=F32)
    (grad_middle_part,) = norm_two_back(grad_normed_two)
    grad_middle = grad_out.astype(F32) + grad_middle_part
    grad_mid_low = grad_middle.astype(BF16)
    grad_mid_low, hn_far = tie(grad_mid_low, hn_far)
    hn_row = jnp.stack([hn, hn_near[0], hn_near[1], jnp.concatenate(hn_far)])
    sent = context_grad(me, w_out, grad_mid_low, parts)
    sent, inner_low, normed_two_low = tie(sent, inner_low, normed_two_low)
    upstream = [sent] + [swap(sent[k], "seq", k) for k in range(1, parts)]
    keep, give = early_grads(
        me, normed_two_low, grad_gate_up, inner_low, grad_out, context_t, grad_mid_low, parts, near
    )
    result = (middle + dot(inner_low, w_down)).astype(BF16)
    early = add(keep, swap(give, "core", 1))
    early, upstream = tie(early, upstream)

    def backward(j, upstream):
        return attend_backward(
            me, qkv[j], key_doc, query_doc, upstream, j, contexts[j], lses[j], cosine, sine, bq
        )

    half = near // 2
    a, b = early[:, :half], early[:, half:]
    from_one = swap(jnp.concatenate([a[1:2], a[3:4]]), "seq", 1)
    from_two = swap(jnp.concatenate([b[2:3], b[3:4]]), "seq", 2)
    grads = [backward(0, upstream)]
    grads[0], upstream, from_one, from_two = tie(grads[0], upstream, from_one, from_two)
    a_two = swap(add(a[2], from_one[1]), "seq", 2)
    b_one = swap(add(b[1], from_two[1]), "seq", 1)
    grads.append(backward(1, upstream))
    grads, upstream, a_two, b_one = tie(grads, upstream, a_two, b_one)
    own = jnp.stack(grads, axis=1)
    pair = [own[0]] + [swap(own[k], "seq", k) for k in range(1, parts)]
    early = jnp.concatenate([add(a[0], from_one[0], a_two), add(b[0], from_two[0], b_one)])
    early = scatter_near(early)
    grads.append(backward(2, upstream))

    grads, early, pair = tie(grads, early, pair)
    last = [grads[2][0]] + [swap(grads[2][k], "seq", k) for k in range(1, parts)]
    early = gather_near(sum_far(early))
    kept, given = late_grads(me, grads, hn_row, near)
    late = add(kept, swap(given, "core", 1))
    last, early, late = tie(last, early, late)
    one, two = swap(early, "seq", 1), swap(early, "seq", 2)
    late = sum_far(scatter_near(late))
    grad_input = input_grad(me, pair, last, w_qkv, tokens[0], norm_one, grad_middle)
    one, two, late, grad_input = tie(one, two, late, grad_input)
    far_one, far_two = swap(two[: near // 2], "seq", 1), swap(one[near // 2 :], "seq", 2)
    late = gather_near(late)
    far_one, far_two, late = tie(far_one, far_two, late)
    early = jnp.stack([early, one, two, jnp.concatenate([far_one, far_two])])
    early_other = swap(early, "core", 1)
    one, two = swap(late, "seq", 1), swap(late, "seq", 2)
    one, two, early_other = tie(one, two, early_other)
    far_one, far_two = swap(two[: near // 2], "seq", 1), swap(one[near // 2 :], "seq", 2)
    sum_w_in, sum_w_down, sum_w_out, sum_norm_two = assemble_early(
        me, early, early_other, w_in, norm_two
    )
    sum_w_in, far_one, far_two = tie(sum_w_in, far_one, far_two)
    late = jnp.stack([late, one, two, jnp.concatenate([far_one, far_two])])
    sum_w_qkv, sum_norm_one = assemble_late(me, late, swap(late, "core", 1), w_qkv, norm_one)
    return (
        result[None],
        grad_input[None],
        sum_norm_one[:, 0],
        sum_w_qkv,
        sum_w_out,
        sum_norm_two[:, 0],
        sum_w_in,
        sum_w_down,
    )


def solution(mesh):
    parts = mesh.shape["seq"]
    near = min(4, mesh.shape["dp"] // 2)
    split = Mesh(mesh.devices.reshape(parts, -1, near, 2), ("seq", "far", "near", "core"))
    rows = ("far", "near", "core")
    tokens_at = P(rows, "seq", None)
    return jax.shard_map(
        on_device,
        mesh=split,
        in_specs=(tokens_at, P(rows, None), tokens_at, P(), P(), P(), P(), P(), P()),
        out_specs=(tokens_at, tokens_at, P(), P(), P(), P(), P(), P()),
        check_vma=False,
    )
```

```python
import functools

import jax
import jax.numpy as jnp
from jax import lax
from jax.experimental import pallas as pl
from jax.experimental.pallas import tpu as pltpu
from jax.sharding import Mesh
from jax.sharding import PartitionSpec as P

D = 768
HEADS = 12
HEAD_DIM = 64
HALF = HEAD_DIM // 2
FF = 1152
WIDE = 3 * HEAD_DIM
LANES = D // 2

EPSILON = 1e-05
ROTARY_BASE = 160000.0
SCORE_SCALE = 0.125
SCORE_EXP2 = SCORE_SCALE * 1.4426950408889634
MASKED_SCORE = -1e30
KEY_CHUNK = 256
F32 = jnp.float32
BF16 = jnp.bfloat16

dot = functools.partial(jnp.dot, preferred_element_type=F32)


def cost(flops, moved, transcendentals=0):
    return pl.CostEstimate(
        flops=flops, bytes_accessed=moved, transcendentals=0
    )


def norm_kernel(tok_ref, norm_ref, out_ref):
    values = tok_ref[...].astype(F32)
    centered = values - jnp.mean(values, axis=-1, keepdims=True)
    variance = jnp.mean(centered * centered, axis=-1, keepdims=True)
    out_ref[...] = (centered * lax.rsqrt(variance + EPSILON) * norm_ref[...]).astype(BF16)


def first_norm(tokens, norm_one):
    rows = tokens.shape[0] // 2
    return pl.pallas_call(
        norm_kernel,
        grid=(2,),
        in_specs=[
            pl.BlockSpec((rows, D), lambda i: (i, 0)),
            pl.BlockSpec((1, D), lambda i: (0, 0)),
        ],
        out_specs=pl.BlockSpec((rows, D), lambda i: (i, 0)),
        out_shape=jax.ShapeDtypeStruct(tokens.shape, BF16),
        compiler_params=pltpu.CompilerParams(vmem_limit_bytes=8 << 20),
        cost_estimate=cost(1 << 20, 2 << 20),
        name="first_norm",
    )(tokens, norm_one[None, :])


def project_kernel(me_ref, hn_ref, w_ref, cos_ref, sin_ref, out_ref):
    part = pl.program_id(0)
    turned = dot(hn_ref[...], w_ref[...]).T
    cosine = jnp.where(part < 2, cos_ref[...], 1.0)
    sine = jnp.where(part < 2, sin_ref[...], 0.0)
    row = pl.multiple_of(part * HEAD_DIM, HEAD_DIM)
    for g in range(out_ref.shape[0]):
        slot = me_ref[0] ^ g
        first = turned[g * HEAD_DIM : g * HEAD_DIM + HALF]
        second = turned[g * HEAD_DIM + HALF : (g + 1) * HEAD_DIM]
        out_ref[slot, pl.ds(row, HALF), :] = (first * cosine - second * sine).astype(BF16)
        out_ref[slot, pl.ds(row + HALF, HALF), :] = (second * cosine + first * sine).astype(BF16)


def project(me, hn, w_qkv, cosine, sine, piece, groups):
    tokens = hn.shape[0]
    width = groups * HEAD_DIM
    pieces = D // width
    return pl.pallas_call(
        project_kernel,
        grid_spec=pltpu.PrefetchScalarGridSpec(
            num_scalar_prefetch=1,
            grid=(3,),
            in_specs=[
                pl.BlockSpec((tokens, D), lambda i, me: (0, 0)),
                pl.BlockSpec((D, width), lambda i, me: (0, i * pieces + piece)),
                pl.BlockSpec((HALF, tokens), lambda i, me: (0, 0)),
                pl.BlockSpec((HALF, tokens), lambda i, me: (0, 0)),
            ],
            out_specs=pl.BlockSpec((groups, WIDE, tokens), lambda i, me: (0, 0, 0)),
        ),
        out_shape=jax.ShapeDtypeStruct((groups, WIDE, tokens), BF16),
        compiler_params=pltpu.CompilerParams(vmem_limit_bytes=32 << 20),
        cost_estimate=cost(6 * tokens * D * width, 4 << 20),
        name="project",
    )(me, hn, w_qkv, cosine, sine)


def mask_scores(scores, chunk, chunks, edge, key_doc, query_doc, query_main):
    if chunk == 0 or chunk == chunks - 1:
        own = key_doc[chunk * KEY_CHUNK : (chunk + 1) * KEY_CHUNK, :]
        return jnp.where(own == query_doc, scores, MASKED_SCORE)
    if edge:
        return jnp.where(query_main, scores, MASKED_SCORE)
    return scores


def put_in_order(me, slots, qkv_s, key_s, value_s=None):
    span = qkv_s.shape[2]
    for k, ref in enumerate(slots):
        at = me ^ k
        piece = ref[...].reshape(WIDE, span)
        qkv_s[at] = piece
        rows = pl.ds(pl.multiple_of(at * span, span), span)
        key_s[rows, :] = piece[HEAD_DIM : 2 * HEAD_DIM].astype(F32).T.astype(BF16)
        if value_s is not None:
            value_s[rows, :] = piece[2 * HEAD_DIM :].astype(F32).T.astype(BF16)


def slot_specs(slots):
    own = pl.BlockSpec((1,) + slots[0].shape[1:], lambda i, me: (0, 0, 0))
    rest = [pl.BlockSpec(s.shape, lambda i, me: (0, 0)) for s in slots[1:]]
    return [own] + rest


def forward_kernel(bq, parts, me_ref, *refs):
    slots = refs[:parts]
    kdoc_ref, qdoc_ref, out_ref, lse_ref, qkv_s, key_s, score_s = refs[parts:]
    step = pl.program_id(0)
    steps = pl.num_programs(0)
    total = key_s.shape[0]
    chunks = total // KEY_CHUNK
    span = qkv_s.shape[2]
    ratio = span // bq

    @pl.when(step == 0)
    def _():
        put_in_order(me_ref[0], slots, qkv_s, key_s)

    def run(edge):
        lanes = pl.ds(pl.multiple_of((step % ratio) * bq, bq), bq)
        queries = qkv_s[step // ratio, 0:HEAD_DIM, lanes]
        query_doc = qdoc_ref[...]
        query_main = query_doc == kdoc_ref[total // 2 : total // 2 + 1, :]
        top = None
        for c in range(chunks):
            rows = slice(c * KEY_CHUNK, (c + 1) * KEY_CHUNK)
            scores = dot(key_s[rows, :], queries)
            scores = mask_scores(scores, c, chunks, edge, kdoc_ref, query_doc, query_main)
            score_s[rows, :] = scores
            peak = jnp.max(scores.reshape(KEY_CHUNK // 8, 8, bq), axis=0)
            top = peak if top is None else jnp.maximum(top, peak)
        top = jnp.max(top, axis=0, keepdims=True) * SCORE_EXP2
        mass, acc = None, None
        for c in range(chunks):
            rows = slice(c * KEY_CHUNK, (c + 1) * KEY_CHUNK)
            weight = jnp.exp2(score_s[rows, :] * SCORE_EXP2 - top)
            part = jnp.sum(weight.reshape(KEY_CHUNK // 8, 8, bq), axis=0)
            mass = part if mass is None else mass + part
            at = c * KEY_CHUNK % span
            values = qkv_s[c * KEY_CHUNK // span, 2 * HEAD_DIM :, at : at + KEY_CHUNK]
            term = dot(values, weight.astype(BF16))
            acc = term if acc is None else acc + term
        mass = jnp.sum(mass, axis=0, keepdims=True)
        out_ref[0] = (acc / mass).astype(BF16)
        lse_ref[...] = top + jnp.log2(mass)

    at_edge = (step == 0) | (step == steps - 1)
    pl.when(at_edge)(lambda: run(True))
    pl.when(jnp.logical_not(at_edge))(lambda: run(False))


def attend_forward(me, slots, key_doc, query_doc, bq):
    parts, _, span = slots[0].shape
    total = parts * span
    ratio = span // bq
    return pl.pallas_call(
        functools.partial(forward_kernel, bq, parts),
        grid_spec=pltpu.PrefetchScalarGridSpec(
            num_scalar_prefetch=1,
            grid=(total // bq,),
            in_specs=slot_specs(slots)
            + [
                pl.BlockSpec((total, 1), lambda i, me: (0, 0)),
                pl.BlockSpec((1, bq), lambda i, me: (0, i)),
            ],
            out_specs=[
                pl.BlockSpec((1, HEAD_DIM, bq), lambda i, me: (i // ratio ^ me[0], 0, i % ratio)),
                pl.BlockSpec((1, bq), lambda i, me: (0, i)),
            ],
            scratch_shapes=[
                pltpu.VMEM((parts, WIDE, span), BF16),
                pltpu.VMEM((total, HEAD_DIM), BF16),
                pltpu.VMEM((total, bq), F32),
            ],
        ),
        out_shape=[
            jax.ShapeDtypeStruct((parts, HEAD_DIM, span), BF16),
            jax.ShapeDtypeStruct((1, total), F32),
        ],
        compiler_params=pltpu.CompilerParams(vmem_limit_bytes=40 << 20),
        cost_estimate=cost(16 * HEAD_DIM * total * total, 4 << 20, total * total),
        name="attend_forward",
    )(me, *slots, key_doc, query_doc)


def backward_kernel(bq, parts, me_ref, *refs):
    slots, ups = refs[:parts], refs[parts : 2 * parts]
    (kdoc_ref, qdoc_ref, o_ref, lse_ref, cos_ref, sin_ref, grad_ref,
     qkv_s, key_s, value_s, up_s, dk_s, dv_s) = refs[2 * parts :]
    step = pl.program_id(0)
    steps = pl.num_programs(0)
    total = key_s.shape[0]
    chunks = total // KEY_CHUNK
    span = qkv_s.shape[2]
    ratio = span // bq

    @pl.when(step == 0)
    def _():
        put_in_order(me_ref[0], slots, qkv_s, key_s, value_s)
        for k, ref in enumerate(ups):
            up_s[me_ref[0] ^ k] = ref[...].reshape(HEAD_DIM, span)
        dk_s[...] = jnp.zeros_like(dk_s)
        dv_s[...] = jnp.zeros_like(dv_s)

    def turn_back(grad, cosine, sine):
        first, second = grad[:HALF], grad[HALF:]
        return first * cosine + second * sine, second * cosine - first * sine

    def run(edge):
        lanes = pl.ds(pl.multiple_of((step % ratio) * bq, bq), bq)
        here = pl.ds(pl.multiple_of(step * bq, bq), bq)
        queries = qkv_s[step // ratio, 0:HEAD_DIM, lanes]
        upstream = up_s[step // ratio, :, lanes]
        wide_up = upstream.astype(F32)
        centre = jnp.sum(wide_up * o_ref[0].astype(F32), axis=0, keepdims=True)
        query_rows = queries.astype(F32).T.astype(BF16)
        up_rows = wide_up.T.astype(BF16)
        query_doc = qdoc_ref[...]
        query_main = query_doc == kdoc_ref[total // 2 : total // 2 + 1, :]
        lse = lse_ref[...]
        dq = None
        for c in range(chunks):
            rows = slice(c * KEY_CHUNK, (c + 1) * KEY_CHUNK)
            scores = dot(key_s[rows, :], queries)
            scores = mask_scores(scores, c, chunks, edge, kdoc_ref, query_doc, query_main)
            probs = jnp.exp2(scores * SCORE_EXP2 - lse)
            grad_prob = dot(value_s[rows, :], upstream)
            grad_scores = (probs * (grad_prob - centre)).astype(BF16)
            dv_s[rows, :] += dot(probs.astype(BF16), up_rows)
            dk_s[rows, :] += dot(grad_scores, query_rows)
            at = c * KEY_CHUNK % span
            keys = qkv_s[c * KEY_CHUNK // span, HEAD_DIM : 2 * HEAD_DIM, at : at + KEY_CHUNK]
            term = dot(keys, grad_scores)
            dq = term if dq is None else dq + term
        one, two = turn_back(dq * SCORE_SCALE, cos_ref[:, here], sin_ref[:, here])
        slot = me_ref[0] ^ (step // ratio)
        grad_ref[slot, 0:HALF, lanes] = one.astype(BF16)
        grad_ref[slot, HALF:HEAD_DIM, lanes] = two.astype(BF16)

    at_edge = (step == 0) | (step == steps - 1)
    pl.when(at_edge)(lambda: run(True))
    pl.when(jnp.logical_not(at_edge))(lambda: run(False))

    @pl.when(step == steps - 1)
    def _():
        for s in range(parts):
            slot = me_ref[0] ^ s
            rows = slice(s * span, (s + 1) * span)
            one, two = turn_back(dk_s[rows, :].T * SCORE_SCALE, cos_ref[:, rows], sin_ref[:, rows])
            grad_ref[slot, HEAD_DIM : HEAD_DIM + HALF, :] = one.astype(BF16)
            grad_ref[slot, HEAD_DIM + HALF : 2 * HEAD_DIM, :] = two.astype(BF16)
            grad_ref[slot, 2 * HEAD_DIM :, :] = dv_s[rows, :].T.astype(BF16)


def attend_backward(me, slots, key_doc, query_doc, upstream, piece, context, lse, cosine, sine, bq):
    parts, _, span = slots[0].shape
    total = parts * span
    ratio = span // bq
    return pl.pallas_call(
        functools.partial(backward_kernel, bq, parts),
        grid_spec=pltpu.PrefetchScalarGridSpec(
            num_scalar_prefetch=1,
            grid=(total // bq,),
            in_specs=slot_specs(slots)
            + [pl.BlockSpec((1, HEAD_DIM, span), lambda i, me: (piece, 0, 0))] * parts
            + [
                pl.BlockSpec((total, 1), lambda i, me: (0, 0)),
                pl.BlockSpec((1, bq), lambda i, me: (0, i)),
                pl.BlockSpec((1, HEAD_DIM, bq), lambda i, me: (i // ratio ^ me[0], 0, i % ratio)),
                pl.BlockSpec((1, bq), lambda i, me: (0, i)),
                pl.BlockSpec((HALF, total), lambda i, me: (0, 0)),
                pl.BlockSpec((HALF, total), lambda i, me: (0, 0)),
            ],
            out_specs=pl.BlockSpec((parts, WIDE, span), lambda i, me: (0, 0, 0)),
            scratch_shapes=[
                pltpu.VMEM((parts, WIDE, span), BF16),
                pltpu.VMEM((total, HEAD_DIM), BF16),
                pltpu.VMEM((total, HEAD_DIM), BF16),
                pltpu.VMEM((parts, HEAD_DIM, span), BF16),
                pltpu.VMEM((total, HEAD_DIM), F32),
                pltpu.VMEM((total, HEAD_DIM), F32),
            ],
        ),
        out_shape=jax.ShapeDtypeStruct((parts, WIDE, span), BF16),
        compiler_params=pltpu.CompilerParams(vmem_limit_bytes=40 << 20),
        cost_estimate=cost(40 * HEAD_DIM * total * total, 6 << 20, total * total),
        name="attend_backward",
    )(me, *slots, *upstream, key_doc, query_doc, context, lse, cosine, sine)


def dot_rows(a, b):
    return lax.dot_general(a, b, (((1,), (1,)), ((), ())), preferred_element_type=F32)


def middle_kernel(parts, me_ref, *refs):
    slots = refs[:parts]
    (tok_ref, cot_ref, wout_ref, norm_ref, win_ref, wdown_ref,
     ctx_ref, n2_ref, gu_ref, inner_ref, low_ref, mid_ref, result_ref) = refs[parts : parts + 13]
    outs, down_s = refs[parts + 13 : -1], refs[-1]
    pieces = slots[0].shape[0]

    def rows_of(j, k):
        at = (j * parts + (me_ref[0] ^ k)) * HEAD_DIM
        return pl.ds(pl.multiple_of(at, HEAD_DIM), HEAD_DIM)

    for k, ref in enumerate(slots):
        for j in range(pieces):
            ctx_ref[rows_of(j, k), :] = ref[j]
    context = ctx_ref[...].astype(F32).T.astype(BF16)
    middle = tok_ref[...].astype(F32) + dot(context, wout_ref[...])
    centered = middle - jnp.mean(middle, axis=-1, keepdims=True)
    scale = lax.rsqrt(jnp.mean(centered * centered, axis=-1, keepdims=True) + EPSILON)
    unit = centered * scale
    normed = (unit * norm_ref[...]).astype(BF16)
    n2_ref[...] = normed
    cotangent = cot_ref[...]
    for c in range(FF // LANES):
        cols = slice(c * LANES, (c + 1) * LANES)
        high = slice(FF + c * LANES, FF + (c + 1) * LANES)
        gate = dot(normed, win_ref[:, cols])
        up = dot(normed, win_ref[:, high])
        grad_inner = dot_rows(cotangent, wdown_ref[cols, :])
        share = 0.5 + 0.5 * lax.erf(gate * 0.7071067811865476)
        slope = share + gate * (0.3989422804014327 * jnp.exp(-0.5 * gate * gate))
        gelu = gate * share
        inner_ref[:, cols] = (gelu * up).astype(BF16)
        gu_ref[:, cols] = (slope * up * grad_inner).astype(BF16)
        gu_ref[:, high] = (gelu * grad_inner).astype(BF16)
    upstream = dot_rows(gu_ref[...], win_ref[...]) * norm_ref[...]
    flat = jnp.mean(upstream, axis=-1, keepdims=True)
    along = jnp.mean(upstream * unit, axis=-1, keepdims=True)
    grad_middle = cotangent.astype(F32) + (upstream - flat - unit * along) * scale
    mid_ref[...] = grad_middle
    low = grad_middle.astype(BF16)
    low_ref[...] = low
    down_s[...] = dot_rows(wout_ref[...], low).astype(BF16)
    for k, ref in enumerate(outs):
        for j in range(pieces):
            ref[j] = down_s[rows_of(j, k), :]
    result_ref[...] = (middle + dot(inner_ref[...], wdown_ref[...])).astype(BF16)


def middle_part(me, slots, tokens, cotangent, w_out, norm_two, w_in, w_down):
    parts, span = len(slots), tokens.shape[0]
    vmem = pl.BlockSpec(memory_space=pltpu.VMEM)
    like = lambda shape, kind=BF16: jax.ShapeDtypeStruct(shape, kind)
    out_shape = [
        like((D, span)),
        like((span, D)),
        like((span, 2 * FF)),
        like((span, FF)),
        like((span, D)),
        like((span, D), F32),
        like((span, D)),
    ] + [like(slots[0].shape)] * parts
    return pl.pallas_call(
        functools.partial(middle_kernel, parts),
        in_specs=[pl.BlockSpec(memory_space=pltpu.SMEM)] + [vmem] * (parts + 6),
        out_specs=[vmem] * len(out_shape),
        out_shape=out_shape,
        scratch_shapes=[pltpu.VMEM((D, span), BF16)],
        compiler_params=pltpu.CompilerParams(vmem_limit_bytes=50 << 20),
        cost_estimate=cost(2 * span * D * (2 * D + 5 * FF + 2 * FF), 20 << 20),
        name="middle_part",
    )(me, *slots, tokens, cotangent, w_out, norm_two[None, :], w_in, w_down)


def early_grad_kernel(at_ref, n2_ref, gu_ref, inner_ref, cot_ref, ctx_ref, mid_ref, keep_ref, give_ref):
    pieces = keep_ref.shape[0]
    rows = D // (2 * pieces)
    low = at_ref[0] == 0

    def put(first, second, count, at):
        kept = jnp.where(low, first, second).astype(BF16)
        given = jnp.where(low, second, first).astype(BF16)
        for p in range(pieces):
            here = slice(p * count, (p + 1) * count)
            place = at_ref[1 + p]
            keep_ref[place, at : at + count, :] = kept[here]
            give_ref[place, at : at + count, :] = given[here]

    n2_t = n2_ref[...].astype(F32).T.astype(BF16)
    for u in range(2 * FF // LANES):
        block = dot(n2_t, gu_ref[:, u * LANES : (u + 1) * LANES])
        put(block[: D // 2], block[D // 2 :], rows, u * rows)
    inner_t = inner_ref[...].astype(F32).T.astype(BF16)
    down = dot(inner_t, cot_ref[...])
    put(down[:, :LANES], down[:, LANES:], 3 * rows, 6 * rows)
    for u in range(2):
        block = dot(ctx_ref[...], mid_ref[:, u * LANES : (u + 1) * LANES])
        put(block[: D // 2], block[D // 2 :], rows, (9 + u) * rows)


def early_places(me, parts, near):
    half = near // 2
    first = [(k, q) for k in (1, 3) for q in range(half)]
    second = [(k, q) for k in (2, 3) for q in range(half, near)]
    kept = [(k, q) for k in (0, 2) for q in range(half)]
    kept += [(k, q) for k in (0, 1) for q in range(half, near)]
    order = {slot: i for i, slot in enumerate(first + second + kept)}
    table = jnp.array([order[k, q] for k in range(parts) for q in range(near)], jnp.int32)
    piece = jnp.arange(parts * near, dtype=jnp.int32)
    return jnp.concatenate([me[2:], table[piece ^ (me[0] * near + me[1])]])


def early_grads(me, n2, gate_up, inner, cotangent, context_t, mid, parts, near):
    rows = D // (2 * parts * near)
    shape = jax.ShapeDtypeStruct((parts * near, 11 * rows, LANES), BF16)
    operands = (n2, gate_up, inner, cotangent, context_t, mid)
    once = lambda a: pl.BlockSpec(a.shape, lambda i, at: (0,) * len(a.shape))
    return pl.pallas_call(
        early_grad_kernel,
        grid_spec=pltpu.PrefetchScalarGridSpec(
            num_scalar_prefetch=1,
            grid=(1,),
            in_specs=[once(a) for a in operands],
            out_specs=[once(shape), once(shape)],
        ),
        out_shape=[shape, shape],
        compiler_params=pltpu.CompilerParams(vmem_limit_bytes=44 << 20),
        cost_estimate=cost(2 * n2.shape[0] * 4224 * D, 14 << 20),
        name="early_grads",
    )(early_places(me, parts, near), *operands)


def late_grad_kernel(pieces, me_ref, *refs):
    grads = refs[:pieces]
    hn_ref, keep_ref, give_ref = refs[pieces:]
    parts = hn_ref.shape[0]
    near = keep_ref.shape[0]
    low = me_ref[2] == 0
    for j, ref in enumerate(grads):
        block = None
        for s in range(parts):
            term = dot(ref[s], hn_ref[s])
            block = term if block is None else block + term
        for part in range(3):
            head = block[part * HEAD_DIM : (part + 1) * HEAD_DIM]
            first, second = head[:HALF], head[HALF:]
            kept = jnp.where(low, first, second).astype(BF16)
            given = jnp.where(low, second, first).astype(BF16)
            for r in range(near):
                slot = me_ref[1] ^ r
                keep_ref[slot, 3 * j + part] = kept[8 * r : 8 * r + 8]
                give_ref[slot, 3 * j + part] = given[8 * r : 8 * r + 8]


def late_grads(me, grads, hn_row, near):
    pieces = len(grads)
    shape = jax.ShapeDtypeStruct((near, 3 * pieces, 8, D), BF16)
    vmem = pl.BlockSpec(memory_space=pltpu.VMEM)
    return pl.pallas_call(
        functools.partial(late_grad_kernel, pieces),
        in_specs=[pl.BlockSpec(memory_space=pltpu.SMEM)] + [vmem] * (pieces + 1),
        out_specs=[vmem, vmem],
        out_shape=[shape, shape],
        compiler_params=pltpu.CompilerParams(vmem_limit_bytes=32 << 20),
        cost_estimate=cost(2 * 2048 * 576 * D, 6 << 20),
        name="late_grads",
    )(me, *grads, hn_row)


def fold_lanes(wide):
    total = wide[:, :128]
    for i in range(1, wide.shape[1] // 128):
        total += wide[:, 128 * i : 128 * (i + 1)]
    return total


def early_kernel(
    me_ref, mine_ref, other_ref, w_ref, norm_ref, win_ref, wdown_ref, wout_ref, gain_ref, part_s
):
    near = mine_ref.shape[1]
    step = pl.program_id(0)
    steps = pl.num_programs(0)
    parts = steps // 2
    rows = D // (steps * near)

    def run(ref):
        for r in range(near):
            piece = ref[0, me_ref[1] ^ r].astype(F32)
            here = slice(r * rows, (r + 1) * rows)
            wide = jnp.concatenate([piece[rows * u : rows * (u + 1)] for u in range(6)], axis=1)
            win_ref[here, :] = wide
            at = pl.multiple_of((step * near + r) * rows, rows)
            part_s[pl.ds(at, rows), :] = fold_lanes(wide * w_ref[here, :].astype(F32))
            wdown_ref[3 * r * rows : 3 * (r + 1) * rows, :] = piece[6 * rows : 9 * rows]
            wout_ref[here, :LANES] = piece[9 * rows : 10 * rows]
            wout_ref[here, LANES:] = piece[10 * rows :]

    ours = (step // parts) == me_ref[2]
    pl.when(ours)(lambda: run(mine_ref))
    pl.when(jnp.logical_not(ours))(lambda: run(other_ref))

    @pl.when(step == steps - 1)
    def _():
        gain_ref[...] = jnp.sum(part_s[...].T, axis=0, keepdims=True) / norm_ref[...]


def assemble_early(me, mine, other, w_in, norm_two):
    parts, near = mine.shape[:2]
    steps = 2 * parts
    rows = D // steps

    def slot(own):
        def index(p, me):
            used = (p // parts == me[2]) == own
            return (jnp.where(used, me[0] ^ (p % parts), 0), 0, 0, 0)

        return pl.BlockSpec((1,) + mine.shape[1:], index)

    return pl.pallas_call(
        early_kernel,
        grid_spec=pltpu.PrefetchScalarGridSpec(
            num_scalar_prefetch=1,
            grid=(steps,),
            in_specs=[
                slot(True),
                slot(False),
                pl.BlockSpec((rows, 2 * FF), lambda p, me: (p, 0)),
                pl.BlockSpec((1, D), lambda p, me: (0, 0)),
            ],
            out_specs=[
                pl.BlockSpec((rows, 2 * FF), lambda p, me: (p, 0)),
                pl.BlockSpec((3 * rows, LANES), lambda p, me: (p % parts, p // parts)),
                pl.BlockSpec((rows, D), lambda p, me: (p, 0)),
                pl.BlockSpec((1, D), lambda p, me: (0, 0)),
            ],
            scratch_shapes=[pltpu.VMEM((D, 128), F32)],
        ),
        out_shape=[
            jax.ShapeDtypeStruct((D, 2 * FF), F32),
            jax.ShapeDtypeStruct((FF, D), F32),
            jax.ShapeDtypeStruct((D, D), F32),
            jax.ShapeDtypeStruct((1, D), F32),
        ],
        compiler_params=pltpu.CompilerParams(vmem_limit_bytes=24 << 20),
        cost_estimate=cost(1 << 20, 24 << 20),
        name="assemble_early",
    )(me, mine, other, w_in, norm_two[None, :])


def late_kernel(me_ref, *refs):
    mine, other = refs[:5], refs[5:10]
    w_ref, norm_ref, out_ref, gain_ref, rows_s, part_s, unit_s = refs[10:]
    block = pl.program_id(0)
    near = mine[0].shape[0]
    pieces = mine[0].shape[1] // 3
    low = me_ref[2] == 0
    row = (block % pieces) * 3 + block // pieces

    @pl.when(block == 0)
    def _():
        ones = lax.broadcasted_iota(jnp.int32, unit_s.shape, 0) == lax.broadcasted_iota(
            jnp.int32, unit_s.shape, 1
        )
        unit_s[...] = ones.astype(F32).astype(BF16)

    for k in range(4):
        for q in range(near):
            which = k if k < 3 else 3 + q // (near // 2)
            place = q if k < 3 else q % (near // 2)
            kept, swapped = mine[which][place, row], other[which][place, row]
            at = (me_ref[0] ^ k) * HEAD_DIM + (me_ref[1] ^ q) * 8
            lower = jnp.where(low, kept.astype(F32), swapped.astype(F32))
            upper = jnp.where(low, swapped.astype(F32), kept.astype(F32))
            rows_s[pl.ds(pl.multiple_of(at, 8), 8), :] = lower
            rows_s[pl.ds(pl.multiple_of(at + HALF, 8), 8), :] = upper
    wide = lax.dot_general(
        unit_s[...], rows_s[...].astype(BF16), (((1,), (1,)), ((), ())), preferred_element_type=F32
    )
    out_ref[...] = wide
    part = fold_lanes(wide * w_ref[...].astype(F32))

    @pl.when(block == 0)
    def _():
        part_s[...] = part

    @pl.when(block > 0)
    def _():
        part_s[...] += part

    @pl.when(block == pl.num_programs(0) - 1)
    def _():
        gain_ref[...] = jnp.sum(part_s[...].T, axis=0, keepdims=True) / norm_ref[...]


def assemble_late(me, mine, other, w_qkv, norm_one):
    groups, blocks = 4, mine[0].shape[1]
    pieces = blocks // 3
    width = groups * HEAD_DIM
    sums = [pl.BlockSpec(v.shape, lambda b, me: (0, 0, 0, 0)) for v in mine]
    return pl.pallas_call(
        late_kernel,
        grid_spec=pltpu.PrefetchScalarGridSpec(
            num_scalar_prefetch=1,
            grid=(blocks,),
            in_specs=sums
            + sums
            + [
                pl.BlockSpec((D, width), lambda b, me: (0, b)),
                pl.BlockSpec((1, D), lambda b, me: (0, 0)),
            ],
            out_specs=[
                pl.BlockSpec((D, width), lambda b, me: (0, b)),
                pl.BlockSpec((1, D), lambda b, me: (0, 0)),
            ],
            scratch_shapes=[
                pltpu.VMEM((width, D), F32),
                pltpu.VMEM((D, 128), F32),
                pltpu.VMEM((D, D), BF16),
            ],
        ),
        out_shape=[
            jax.ShapeDtypeStruct((D, 3 * D), F32),
            jax.ShapeDtypeStruct((1, D), F32),
        ],
        compiler_params=pltpu.CompilerParams(vmem_limit_bytes=60 << 20),
        cost_estimate=cost(1 << 20, 14 << 20),
        name="assemble_late",
    )(me, *mine, *other, w_qkv, norm_one[None, :])


def input_grad_kernel(parts, pieces, me_ref, *refs):
    pair, last = refs[:parts], refs[parts : 2 * parts]
    w_ref, tok_ref, norm_ref, mid_ref, out_ref, proj_s = refs[2 * parts :]
    span = proj_s.shape[1]
    for k in range(parts):
        group = me_ref[0] ^ k
        for j in range(pieces):
            if j < pieces - 1:
                piece = pair[k][...].reshape(pieces - 1, WIDE, span)[j]
            else:
                piece = last[k][...].reshape(WIDE, span)
            for part in range(3):
                at = part * D + (j * parts + group) * HEAD_DIM
                proj_s[pl.ds(pl.multiple_of(at, HEAD_DIM), HEAD_DIM), :] = piece[
                    part * HEAD_DIM : (part + 1) * HEAD_DIM
                ]
    upstream = dot(w_ref[...], proj_s[...]).T * norm_ref[...]
    values = tok_ref[...].astype(F32)
    centered = values - jnp.mean(values, axis=-1, keepdims=True)
    scale = lax.rsqrt(jnp.mean(centered * centered, axis=-1, keepdims=True) + EPSILON)
    unit = centered * scale
    flat = jnp.mean(upstream, axis=-1, keepdims=True)
    along = jnp.mean(upstream * unit, axis=-1, keepdims=True)
    out_ref[...] = mid_ref[...] + (upstream - flat - unit * along) * scale


def input_grad(me, pair, last, w_qkv, tokens, norm_one, grad_middle):
    parts = len(pair)
    span = tokens.shape[0]
    vmem = pl.BlockSpec(memory_space=pltpu.VMEM)
    return pl.pallas_call(
        functools.partial(input_grad_kernel, parts, 3),
        in_specs=[pl.BlockSpec(memory_space=pltpu.SMEM)] + [vmem] * (2 * parts + 4),
        out_specs=vmem,
        out_shape=jax.ShapeDtypeStruct((span, D), F32),
        scratch_shapes=[pltpu.VMEM((3 * D, span), BF16)],
        compiler_params=pltpu.CompilerParams(vmem_limit_bytes=40 << 20),
        cost_estimate=cost(2 * span * 3 * D * D, 10 << 20),
        name="input_grad",
    )(me, *pair, *last, w_qkv, tokens, norm_one[None, :], grad_middle)


def swap(values, axis, k):
    size = lax.axis_size(axis)
    return lax.ppermute(values, axis, [(i, i ^ k) for i in range(size)])


def add(*terms):
    total = terms[0].astype(F32)
    for term in terms[1:]:
        total += term.astype(F32)
    return total.astype(BF16)


def scatter_near(slots):
    return add(slots[0], *[swap(slots[k], "near", k) for k in range(1, len(slots))])


def gather_near(values):
    return jnp.stack([values] + [swap(values, "near", k) for k in range(1, lax.axis_size("near"))])


def tie(*values):
    return lax.optimization_barrier(values)


def on_device(tokens, doc_start, cotangent, norm_one, w_qkv, w_out, norm_two, w_in, w_down):
    parts = lax.axis_size("seq")
    near = lax.axis_size("near")
    far = lax.axis_size("far")
    span = tokens.shape[1]
    total = span * parts
    pieces = HEADS // parts
    bq = min(512, span)
    me_seq = lax.axis_index("seq").astype(jnp.int32)
    me = jnp.stack([lax.axis_index(a).astype(jnp.int32) for a in ("seq", "near", "core")])
    first_token = me_seq * span
    starts = doc_start[0]
    key_doc = starts[:, None]
    query_doc = starts[None, :]

    frequency = ROTARY_BASE ** (-(jnp.arange(HALF, dtype=F32) * 2.0 / HEAD_DIM))
    offset = (jnp.arange(total, dtype=jnp.int32) - starts).astype(F32)
    angles = frequency[:, None] * offset[None, :]
    cosine, sine = jnp.cos(angles), jnp.sin(angles)
    own_cosine = lax.dynamic_slice_in_dim(cosine, first_token, span, axis=1)
    own_sine = lax.dynamic_slice_in_dim(sine, first_token, span, axis=1)

    def sum_far(values):
        return lax.psum(values, "far") if far > 1 else values

    hn = first_norm(tokens[0], norm_one)
    qkv = []
    for j in range(pieces):
        sent = project(me, hn, w_qkv, own_cosine, own_sine, j, parts)
        qkv.append([sent] + [swap(sent[k], "seq", k) for k in range(1, parts)])
    contexts, lses = [], []
    for j in range(pieces):
        if j == pieces - 1:
            hn_late, qkv[j] = tie(hn, qkv[j])
            hn_near = [swap(hn_late, "seq", 1), swap(hn_late, "seq", 2)]
        context, lse = attend_forward(me, qkv[j], key_doc, query_doc, bq)
        contexts.append(context)
        lses.append(lse)
    arrived = [jnp.stack([c[k] for c in contexts]) for k in range(parts)]
    arrived[1:] = [swap(arrived[k], "seq", k) for k in range(1, parts)]
    arrived, hn_near = tie(arrived, hn_near)
    hn_far = [swap(hn_near[1][: span // 2], "seq", 1), swap(hn_near[0][span // 2 :], "seq", 2)]
    outs = middle_part(me, arrived, tokens[0], cotangent[0], w_out, norm_two, w_in, w_down)
    outs, hn_far = tie(outs, hn_far)
    context_t, normed_two, grad_gate_up, inner, grad_mid_low, grad_middle, result = outs[:7]
    hn_row = jnp.stack([hn, hn_near[0], hn_near[1], jnp.concatenate(hn_far)])
    upstream = [outs[7]] + [swap(outs[7 + k], "seq", k) for k in range(1, parts)]
    keep, give = early_grads(
        me, normed_two, grad_gate_up, inner, cotangent[0], context_t, grad_mid_low, parts, near
    )
    taken = swap(give, "core", 1)
    half = near // 2
    at = [2 * half, 4 * half, 5 * half, 6 * half, 7 * half, 8 * half]
    send_one = add(keep[: at[0]], taken[: at[0]])
    send_two = add(keep[at[0] : at[1]], taken[at[0] : at[1]])
    early = add(keep[at[1] :], taken[at[1] :])
    a_own, a_two, b_own, b_one = (early[i * half : (i + 1) * half] for i in range(4))
    send_one, send_two, early, upstream = tie(send_one, send_two, early, upstream)

    def backward(j, upstream):
        return attend_backward(
            me, qkv[j], key_doc, query_doc, upstream, j, contexts[j], lses[j], cosine, sine, bq
        )

    from_one, from_two = swap(send_one, "seq", 1), swap(send_two, "seq", 2)
    grads = [backward(0, upstream)]
    grads[0], upstream, from_one, from_two = tie(grads[0], upstream, from_one, from_two)
    by_two = swap(add(a_two, from_one[half:]), "seq", 2)
    by_one = swap(add(b_one, from_two[half:]), "seq", 1)
    grads.append(backward(1, upstream))
    grads, upstream, by_two, by_one = tie(grads, upstream, by_two, by_one)
    own = jnp.stack(grads, axis=1)
    pair = [own[0]] + [swap(own[k], "seq", k) for k in range(1, parts)]
    early = [add(a_own[i], from_one[i], by_two[i]) for i in range(half)]
    early += [add(b_own[i], from_two[i], by_one[i]) for i in range(half)]
    early = scatter_near(early)
    grads.append(backward(2, upstream))

    kept, given = late_grads(me, grads, hn_row, near)
    grads, early, pair, kept, given = tie(grads, early, pair, kept, given)
    last = [grads[2][0]] + [swap(grads[2][k], "seq", k) for k in range(1, parts)]
    early = sum_far(early)
    slots = [early, swap(early, "near", 1), swap(early, "near", 2), swap(early, "near", 3)]
    late = add(kept, swap(given, "core", 1))
    last, slots, late = tie(last, slots, late)
    early = jnp.stack(slots)
    one, two = swap(early, "seq", 1), swap(early, "seq", 2)
    late = sum_far(scatter_near(late))
    grad_input = input_grad(me, pair, last, w_qkv, tokens[0], norm_one, grad_middle)
    one, two, late, grad_input = tie(one, two, late, grad_input)
    far_one, far_two = swap(two[: near // 2], "seq", 1), swap(one[near // 2 :], "seq", 2)
    late = gather_near(late)
    far_one, far_two, late = tie(far_one, far_two, late)
    early = jnp.stack([early, one, two, jnp.concatenate([far_one, far_two])])
    early_other = swap(early, "core", 1)
    one, two = swap(late, "seq", 1), swap(late, "seq", 2)
    one, two, early_other = tie(one, two, early_other)
    far = [swap(two[: near // 2], "seq", 1), swap(one[near // 2 :], "seq", 2)]
    mine = [late, one, two]
    other = [swap(v, "core", 1) for v in mine]
    sum_w_in, sum_w_down, sum_w_out, sum_norm_two = assemble_early(
        me, early, early_other, w_in, norm_two
    )
    sum_w_in, far, other = tie(sum_w_in, far, other)
    mine += far
    other += [swap(v, "core", 1) for v in far]
    sum_w_qkv, sum_norm_one = assemble_late(me, mine, other, w_qkv, norm_one)
    return (
        result[None],
        grad_input[None],
        sum_norm_one[0],
        sum_w_qkv,
        sum_w_out,
        sum_norm_two[0],
        sum_w_in,
        sum_w_down,
    )


def solution(mesh):
    parts = mesh.shape["seq"]
    near = min(4, mesh.shape["dp"] // 2)
    split = Mesh(mesh.devices.reshape(parts, -1, near, 2), ("seq", "far", "near", "core"))
    rows = ("far", "near", "core")
    tokens_at = P(rows, "seq", None)
    return jax.shard_map(
        on_device,
        mesh=split,
        in_specs=(tokens_at, P(rows, None), tokens_at, P(), P(), P(), P(), P(), P()),
        out_specs=(tokens_at, tokens_at, P(), P(), P(), P(), P(), P()),
        check_vma=False,
    )
```

```python
import functools

import jax
import jax.numpy as jnp
from jax import lax
from jax.experimental import pallas as pl
from jax.experimental.pallas import tpu as pltpu
from jax.sharding import Mesh
from jax.sharding import PartitionSpec as P

D = 768
HEADS = 12
HEAD_DIM = 64
HALF = HEAD_DIM // 2
FF = 1152
WIDE = 3 * HEAD_DIM
LANES = D // 2

EPSILON = 1e-05
ROTARY_BASE = 160000.0
SCORE_SCALE = 0.125
SCORE_EXP2 = SCORE_SCALE * 1.4426950408889634
MASKED_SCORE = -1e30
KEY_CHUNK = 256
F32 = jnp.float32
BF16 = jnp.bfloat16

dot = functools.partial(jnp.dot, preferred_element_type=F32)


def cost(flops, moved, transcendentals=0):
    return pl.CostEstimate(
        flops=flops, bytes_accessed=moved, transcendentals=0
    )


def norm_kernel(tok_ref, norm_ref, out_ref):
    values = tok_ref[...].astype(F32)
    centered = values - jnp.mean(values, axis=-1, keepdims=True)
    variance = jnp.mean(centered * centered, axis=-1, keepdims=True)
    out_ref[...] = (centered * lax.rsqrt(variance + EPSILON) * norm_ref[...]).astype(BF16)


def first_norm(tokens, norm_one):
    rows = tokens.shape[0] // 2
    return pl.pallas_call(
        norm_kernel,
        grid=(2,),
        in_specs=[
            pl.BlockSpec((rows, D), lambda i: (i, 0)),
            pl.BlockSpec((1, D), lambda i: (0, 0)),
        ],
        out_specs=pl.BlockSpec((rows, D), lambda i: (i, 0)),
        out_shape=jax.ShapeDtypeStruct(tokens.shape, BF16),
        compiler_params=pltpu.CompilerParams(vmem_limit_bytes=6 << 20),
        cost_estimate=cost(1 << 20, 2 << 20),
        name="first_norm",
    )(tokens, norm_one[None, :])


def project_kernel(me_ref, hn_ref, w_ref, cos_ref, sin_ref, out_ref):
    part = pl.program_id(0)
    turned = dot(hn_ref[...], w_ref[...]).T
    cosine = jnp.where(part < 2, cos_ref[...], 1.0)
    sine = jnp.where(part < 2, sin_ref[...], 0.0)
    row = pl.multiple_of(part * HEAD_DIM, HEAD_DIM)
    for g in range(out_ref.shape[0]):
        slot = me_ref[0] ^ g
        first = turned[g * HEAD_DIM : g * HEAD_DIM + HALF]
        second = turned[g * HEAD_DIM + HALF : (g + 1) * HEAD_DIM]
        out_ref[slot, pl.ds(row, HALF), :] = (first * cosine - second * sine).astype(BF16)
        out_ref[slot, pl.ds(row + HALF, HALF), :] = (second * cosine + first * sine).astype(BF16)


def project(me, hn, w_qkv, cosine, sine, piece, groups):
    tokens = hn.shape[0]
    width = groups * HEAD_DIM
    pieces = D // width
    return pl.pallas_call(
        project_kernel,
        grid_spec=pltpu.PrefetchScalarGridSpec(
            num_scalar_prefetch=1,
            grid=(3,),
            in_specs=[
                pl.BlockSpec((tokens, D), lambda i, me: (0, 0)),
                pl.BlockSpec((D, width), lambda i, me: (0, i * pieces + piece)),
                pl.BlockSpec((HALF, tokens), lambda i, me: (0, 0)),
                pl.BlockSpec((HALF, tokens), lambda i, me: (0, 0)),
            ],
            out_specs=pl.BlockSpec((groups, WIDE, tokens), lambda i, me: (0, 0, 0)),
        ),
        out_shape=jax.ShapeDtypeStruct((groups, WIDE, tokens), BF16),
        compiler_params=pltpu.CompilerParams(vmem_limit_bytes=32 << 20),
        cost_estimate=cost(6 * tokens * D * width, 4 << 20),
        name="project",
    )(me, hn, w_qkv, cosine, sine)


def mask_scores(scores, chunk, chunks, edge, key_doc, query_doc, query_main):
    if chunk == 0 or chunk == chunks - 1:
        own = key_doc[chunk * KEY_CHUNK : (chunk + 1) * KEY_CHUNK, :]
        return jnp.where(own == query_doc, scores, MASKED_SCORE)
    if edge:
        return jnp.where(query_main, scores, MASKED_SCORE)
    return scores


def put_in_order(me, slots, qkv_s, key_s, value_s=None):
    span = qkv_s.shape[2]
    for k, ref in enumerate(slots):
        at = me ^ k
        piece = ref[...].reshape(WIDE, span)
        qkv_s[at] = piece
        rows = pl.ds(pl.multiple_of(at * span, span), span)
        key_s[rows, :] = piece[HEAD_DIM : 2 * HEAD_DIM].astype(F32).T.astype(BF16)
        if value_s is not None:
            value_s[rows, :] = piece[2 * HEAD_DIM :].astype(F32).T.astype(BF16)


def slot_specs(slots):
    own = pl.BlockSpec((1,) + slots[0].shape[1:], lambda i, me: (0, 0, 0))
    rest = [pl.BlockSpec(s.shape, lambda i, me: (0, 0)) for s in slots[1:]]
    return [own] + rest


def forward_kernel(bq, parts, me_ref, *refs):
    slots = refs[:parts]
    kdoc_ref, qdoc_ref, out_ref, lse_ref, qkv_s, key_s, score_s = refs[parts:]
    step = pl.program_id(0)
    steps = pl.num_programs(0)
    total = key_s.shape[0]
    chunks = total // KEY_CHUNK
    span = qkv_s.shape[2]
    ratio = span // bq

    @pl.when(step == 0)
    def _():
        put_in_order(me_ref[0], slots, qkv_s, key_s)

    def run(edge):
        lanes = pl.ds(pl.multiple_of((step % ratio) * bq, bq), bq)
        queries = qkv_s[step // ratio, 0:HEAD_DIM, lanes]
        query_doc = qdoc_ref[...]
        query_main = query_doc == kdoc_ref[total // 2 : total // 2 + 1, :]
        top = None
        for c in range(chunks):
            rows = slice(c * KEY_CHUNK, (c + 1) * KEY_CHUNK)
            scores = dot(key_s[rows, :], queries)
            scores = mask_scores(scores, c, chunks, edge, kdoc_ref, query_doc, query_main)
            score_s[rows, :] = scores
            peak = jnp.max(scores.reshape(KEY_CHUNK // 8, 8, bq), axis=0)
            top = peak if top is None else jnp.maximum(top, peak)
        top = jnp.max(top, axis=0, keepdims=True) * SCORE_EXP2
        mass, acc = None, None
        for c in range(chunks):
            rows = slice(c * KEY_CHUNK, (c + 1) * KEY_CHUNK)
            weight = jnp.exp2(score_s[rows, :] * SCORE_EXP2 - top)
            part = jnp.sum(weight.reshape(KEY_CHUNK // 8, 8, bq), axis=0)
            mass = part if mass is None else mass + part
            at = c * KEY_CHUNK % span
            values = qkv_s[c * KEY_CHUNK // span, 2 * HEAD_DIM :, at : at + KEY_CHUNK]
            term = dot(values, weight.astype(BF16))
            acc = term if acc is None else acc + term
        mass = jnp.sum(mass, axis=0, keepdims=True)
        out_ref[0] = (acc / mass).astype(BF16)
        lse_ref[...] = top + jnp.log2(mass)

    at_edge = (step == 0) | (step == steps - 1)
    pl.when(at_edge)(lambda: run(True))
    pl.when(jnp.logical_not(at_edge))(lambda: run(False))


def attend_forward(me, slots, key_doc, query_doc, bq):
    parts, _, span = slots[0].shape
    total = parts * span
    ratio = span // bq
    return pl.pallas_call(
        functools.partial(forward_kernel, bq, parts),
        grid_spec=pltpu.PrefetchScalarGridSpec(
            num_scalar_prefetch=1,
            grid=(total // bq,),
            in_specs=slot_specs(slots)
            + [
                pl.BlockSpec((total, 1), lambda i, me: (0, 0)),
                pl.BlockSpec((1, bq), lambda i, me: (0, i)),
            ],
            out_specs=[
                pl.BlockSpec((1, HEAD_DIM, bq), lambda i, me: (i // ratio ^ me[0], 0, i % ratio)),
                pl.BlockSpec((1, bq), lambda i, me: (0, i)),
            ],
            scratch_shapes=[
                pltpu.VMEM((parts, WIDE, span), BF16),
                pltpu.VMEM((total, HEAD_DIM), BF16),
                pltpu.VMEM((total, bq), F32),
            ],
        ),
        out_shape=[
            jax.ShapeDtypeStruct((parts, HEAD_DIM, span), BF16),
            jax.ShapeDtypeStruct((1, total), F32),
        ],
        compiler_params=pltpu.CompilerParams(vmem_limit_bytes=40 << 20),
        cost_estimate=cost(16 * HEAD_DIM * total * total, 4 << 20, total * total),
        name="attend_forward",
    )(me, *slots, key_doc, query_doc)


def backward_kernel(bq, parts, turn, me_ref, *refs):
    slots, ups = refs[:parts], refs[parts : 2 * parts]
    (kdoc_ref, qdoc_ref, o_ref, lse_ref, cos_ref, sin_ref, grad_ref,
     qkv_s, key_s, value_s, up_s, dk_s, dv_s) = refs[2 * parts :]
    step = pl.program_id(0)
    steps = pl.num_programs(0)
    total = key_s.shape[0]
    chunks = total // KEY_CHUNK
    span = qkv_s.shape[2]
    ratio = span // bq

    @pl.when(step == 0)
    def _():
        put_in_order(me_ref[0], slots, qkv_s, key_s, value_s)
        for k, ref in enumerate(ups):
            up_s[me_ref[0] ^ k] = ref[...].reshape(HEAD_DIM, span)
        dk_s[...] = jnp.zeros_like(dk_s)
        dv_s[...] = jnp.zeros_like(dv_s)

    def turn_back(grad, cosine, sine):
        first, second = grad[:HALF], grad[HALF:]
        return first * cosine + second * sine, second * cosine - first * sine

    def run(edge):
        lanes = pl.ds(pl.multiple_of((step % ratio) * bq, bq), bq)
        here = pl.ds(pl.multiple_of(step * bq, bq), bq)
        queries = qkv_s[step // ratio, 0:HEAD_DIM, lanes]
        upstream = up_s[step // ratio, :, lanes]
        wide_up = upstream.astype(F32)
        centre = jnp.sum(wide_up * o_ref[0].astype(F32), axis=0, keepdims=True)
        query_rows = queries.astype(F32).T.astype(BF16)
        up_rows = wide_up.T.astype(BF16)
        query_doc = qdoc_ref[...]
        query_main = query_doc == kdoc_ref[total // 2 : total // 2 + 1, :]
        lse = lse_ref[...]
        dq = None
        for c in range(chunks):
            rows = slice(c * KEY_CHUNK, (c + 1) * KEY_CHUNK)
            scores = dot(key_s[rows, :], queries)
            scores = mask_scores(scores, c, chunks, edge, kdoc_ref, query_doc, query_main)
            probs = jnp.exp2(scores * SCORE_EXP2 - lse)
            grad_prob = dot(value_s[rows, :], upstream)
            grad_scores = (probs * (grad_prob - centre)).astype(BF16)
            dv_s[rows, :] += dot(probs.astype(BF16), up_rows)
            dk_s[rows, :] += dot(grad_scores, query_rows)
            at = c * KEY_CHUNK % span
            keys = qkv_s[c * KEY_CHUNK // span, HEAD_DIM : 2 * HEAD_DIM, at : at + KEY_CHUNK]
            term = dot(keys, grad_scores)
            dq = term if dq is None else dq + term
        one, two = turn_back(dq * SCORE_SCALE, cos_ref[:, here], sin_ref[:, here])
        slot = (me_ref[0] if turn else 0) ^ (step // ratio)
        grad_ref[slot, 0:HALF, lanes] = one.astype(BF16)
        grad_ref[slot, HALF:HEAD_DIM, lanes] = two.astype(BF16)

    at_edge = (step == 0) | (step == steps - 1)
    pl.when(at_edge)(lambda: run(True))
    pl.when(jnp.logical_not(at_edge))(lambda: run(False))

    @pl.when(step == steps - 1)
    def _():
        for s in range(parts):
            slot = (me_ref[0] if turn else 0) ^ s
            rows = slice(s * span, (s + 1) * span)
            one, two = turn_back(dk_s[rows, :].T * SCORE_SCALE, cos_ref[:, rows], sin_ref[:, rows])
            grad_ref[slot, HEAD_DIM : HEAD_DIM + HALF, :] = one.astype(BF16)
            grad_ref[slot, HEAD_DIM + HALF : 2 * HEAD_DIM, :] = two.astype(BF16)
            grad_ref[slot, 2 * HEAD_DIM :, :] = dv_s[rows, :].T.astype(BF16)


def attend_backward(
    me, slots, key_doc, query_doc, upstream, piece, context, lse, cosine, sine, bq, turn
):
    parts, _, span = slots[0].shape
    total = parts * span
    ratio = span // bq
    return pl.pallas_call(
        functools.partial(backward_kernel, bq, parts, turn),
        grid_spec=pltpu.PrefetchScalarGridSpec(
            num_scalar_prefetch=1,
            grid=(total // bq,),
            in_specs=slot_specs(slots)
            + [pl.BlockSpec((1, HEAD_DIM, span), lambda i, me: (piece, 0, 0))] * parts
            + [
                pl.BlockSpec((total, 1), lambda i, me: (0, 0)),
                pl.BlockSpec((1, bq), lambda i, me: (0, i)),
                pl.BlockSpec((1, HEAD_DIM, bq), lambda i, me: (i // ratio ^ me[0], 0, i % ratio)),
                pl.BlockSpec((1, bq), lambda i, me: (0, i)),
                pl.BlockSpec((HALF, total), lambda i, me: (0, 0)),
                pl.BlockSpec((HALF, total), lambda i, me: (0, 0)),
            ],
            out_specs=pl.BlockSpec((parts, WIDE, span), lambda i, me: (0, 0, 0)),
            scratch_shapes=[
                pltpu.VMEM((parts, WIDE, span), BF16),
                pltpu.VMEM((total, HEAD_DIM), BF16),
                pltpu.VMEM((total, HEAD_DIM), BF16),
                pltpu.VMEM((parts, HEAD_DIM, span), BF16),
                pltpu.VMEM((total, HEAD_DIM), F32),
                pltpu.VMEM((total, HEAD_DIM), F32),
            ],
        ),
        out_shape=jax.ShapeDtypeStruct((parts, WIDE, span), BF16),
        compiler_params=pltpu.CompilerParams(vmem_limit_bytes=40 << 20),
        cost_estimate=cost(40 * HEAD_DIM * total * total, 6 << 20, total * total),
        name="attend_backward",
    )(me, *slots, *upstream, key_doc, query_doc, context, lse, cosine, sine)


def dot_rows(a, b):
    return lax.dot_general(a, b, (((1,), (1,)), ((), ())), preferred_element_type=F32)


def middle_kernel(parts, me_ref, *refs):
    slots = refs[:parts]
    (tok_ref, cot_ref, wout_ref, norm_ref, win_ref, wdown_ref,
     ctx_ref, n2_ref, gu_ref, inner_ref, low_ref, mid_ref, result_ref) = refs[parts : parts + 13]
    outs, down_s = refs[parts + 13 : -1], refs[-1]
    pieces = slots[0].shape[0]

    def rows_of(j, k):
        at = (j * parts + (me_ref[0] ^ k)) * HEAD_DIM
        return pl.ds(pl.multiple_of(at, HEAD_DIM), HEAD_DIM)

    for k, ref in enumerate(slots):
        for j in range(pieces):
            ctx_ref[rows_of(j, k), :] = ref[j]
    context = ctx_ref[...].astype(F32).T.astype(BF16)
    middle = tok_ref[...].astype(F32) + dot(context, wout_ref[...])
    centered = middle - jnp.mean(middle, axis=-1, keepdims=True)
    scale = lax.rsqrt(jnp.mean(centered * centered, axis=-1, keepdims=True) + EPSILON)
    unit = centered * scale
    normed = (unit * norm_ref[...]).astype(BF16)
    n2_ref[...] = normed
    cotangent = cot_ref[...]
    for c in range(FF // LANES):
        cols = slice(c * LANES, (c + 1) * LANES)
        high = slice(FF + c * LANES, FF + (c + 1) * LANES)
        gate = dot(normed, win_ref[:, cols])
        up = dot(normed, win_ref[:, high])
        grad_inner = dot_rows(cotangent, wdown_ref[cols, :])
        share = 0.5 + 0.5 * lax.erf(gate * 0.7071067811865476)
        slope = share + gate * (0.3989422804014327 * jnp.exp(-0.5 * gate * gate))
        gelu = gate * share
        inner_ref[:, cols] = (gelu * up).astype(BF16)
        gu_ref[:, cols] = (slope * up * grad_inner).astype(BF16)
        gu_ref[:, high] = (gelu * grad_inner).astype(BF16)
    upstream = dot_rows(gu_ref[...], win_ref[...]) * norm_ref[...]
    flat = jnp.mean(upstream, axis=-1, keepdims=True)
    along = jnp.mean(upstream * unit, axis=-1, keepdims=True)
    grad_middle = cotangent.astype(F32) + (upstream - flat - unit * along) * scale
    mid_ref[...] = grad_middle
    low = grad_middle.astype(BF16)
    low_ref[...] = low
    down_s[...] = dot_rows(wout_ref[...], low).astype(BF16)
    for k, ref in enumerate(outs):
        for j in range(pieces):
            ref[j] = down_s[rows_of(j, k), :]
    result_ref[...] = (middle + dot(inner_ref[...], wdown_ref[...])).astype(BF16)


def middle_part(me, slots, tokens, cotangent, w_out, norm_two, w_in, w_down):
    parts, span = len(slots), tokens.shape[0]
    vmem = pl.BlockSpec(memory_space=pltpu.VMEM)
    like = lambda shape, kind=BF16: jax.ShapeDtypeStruct(shape, kind)
    out_shape = [
        like((D, span)),
        like((span, D)),
        like((span, 2 * FF)),
        like((span, FF)),
        like((span, D)),
        like((span, D), F32),
        like((span, D)),
    ] + [like(slots[0].shape)] * parts
    return pl.pallas_call(
        functools.partial(middle_kernel, parts),
        in_specs=[pl.BlockSpec(memory_space=pltpu.SMEM)] + [vmem] * (parts + 6),
        out_specs=[vmem] * len(out_shape),
        out_shape=out_shape,
        scratch_shapes=[pltpu.VMEM((D, span), BF16)],
        compiler_params=pltpu.CompilerParams(vmem_limit_bytes=18 << 20),
        cost_estimate=cost(2 * span * D * (2 * D + 5 * FF + 2 * FF), 20 << 20),
        name="middle_part",
    )(me, *slots, tokens, cotangent, w_out, norm_two[None, :], w_in, w_down)


def early_grad_kernel(at_ref, n2_ref, gu_ref, inner_ref, cot_ref, ctx_ref, mid_ref, keep_ref, give_ref):
    pieces = keep_ref.shape[0]
    rows = D // (2 * pieces)
    low = at_ref[0] == 0

    def put(first, second, count, at):
        kept = jnp.where(low, first, second).astype(BF16)
        given = jnp.where(low, second, first).astype(BF16)
        for p in range(pieces):
            here = slice(p * count, (p + 1) * count)
            place = at_ref[1 + p]
            keep_ref[place, at : at + count, :] = kept[here]
            give_ref[place, at : at + count, :] = given[here]

    n2_t = n2_ref[...].astype(F32).T.astype(BF16)
    for u in range(2 * FF // LANES):
        block = dot(n2_t, gu_ref[:, u * LANES : (u + 1) * LANES])
        put(block[: D // 2], block[D // 2 :], rows, u * rows)
    inner_t = inner_ref[...].astype(F32).T.astype(BF16)
    down = dot(inner_t, cot_ref[...])
    put(down[:, :LANES], down[:, LANES:], 3 * rows, 6 * rows)
    for u in range(2):
        block = dot(ctx_ref[...], mid_ref[:, u * LANES : (u + 1) * LANES])
        put(block[: D // 2], block[D // 2 :], rows, (9 + u) * rows)


def early_places(me, parts, near):
    half = near // 2
    first = [(k, q) for k in (1, 3) for q in range(half)]
    second = [(k, q) for k in (2, 3) for q in range(half, near)]
    kept = [(k, q) for k in (0, 2) for q in range(half)]
    kept += [(k, q) for k in (0, 1) for q in range(half, near)]
    order = {slot: i for i, slot in enumerate(first + second + kept)}
    table = jnp.array([order[k, q] for k in range(parts) for q in range(near)], jnp.int32)
    piece = jnp.arange(parts * near, dtype=jnp.int32)
    return jnp.concatenate([me[2:], table[piece ^ (me[0] * near + me[1])]])


def early_grads(me, n2, gate_up, inner, cotangent, context_t, mid, parts, near):
    rows = D // (2 * parts * near)
    shape = jax.ShapeDtypeStruct((parts * near, 11 * rows, LANES), BF16)
    operands = (n2, gate_up, inner, cotangent, context_t, mid)
    once = lambda a: pl.BlockSpec(a.shape, lambda i, at: (0,) * len(a.shape))
    return pl.pallas_call(
        early_grad_kernel,
        grid_spec=pltpu.PrefetchScalarGridSpec(
            num_scalar_prefetch=1,
            grid=(1,),
            in_specs=[once(a) for a in operands],
            out_specs=[once(shape), once(shape)],
        ),
        out_shape=[shape, shape],
        compiler_params=pltpu.CompilerParams(vmem_limit_bytes=28 << 20),
        cost_estimate=cost(2 * n2.shape[0] * 4224 * D, 14 << 20),
        name="early_grads",
    )(early_places(me, parts, near), *operands)


def late_grad_kernel(pieces, me_ref, *refs):
    grads = refs[:pieces]
    hn_ref, keep_ref, give_ref = refs[pieces:]
    parts = hn_ref.shape[0]
    near = keep_ref.shape[0]
    low = me_ref[2] == 0
    for j, ref in enumerate(grads):
        block = None
        for s in range(parts):
            term = dot(ref[s], hn_ref[s])
            block = term if block is None else block + term
        for part in range(3):
            head = block[part * HEAD_DIM : (part + 1) * HEAD_DIM]
            first, second = head[:HALF], head[HALF:]
            kept = jnp.where(low, first, second).astype(BF16)
            given = jnp.where(low, second, first).astype(BF16)
            for r in range(near):
                slot = me_ref[1] ^ r
                keep_ref[slot, 3 * j + part] = kept[8 * r : 8 * r + 8]
                give_ref[slot, 3 * j + part] = given[8 * r : 8 * r + 8]


def late_grads(me, grads, hn_row, near):
    pieces = len(grads)
    shape = jax.ShapeDtypeStruct((near, 3 * pieces, 8, D), BF16)
    vmem = pl.BlockSpec(memory_space=pltpu.VMEM)
    return pl.pallas_call(
        functools.partial(late_grad_kernel, pieces),
        in_specs=[pl.BlockSpec(memory_space=pltpu.SMEM)] + [vmem] * (pieces + 1),
        out_specs=[vmem, vmem],
        out_shape=[shape, shape],
        compiler_params=pltpu.CompilerParams(vmem_limit_bytes=12 << 20),
        cost_estimate=cost(2 * 2048 * 576 * D, 6 << 20),
        name="late_grads",
    )(me, *grads, hn_row)


def fold_lanes(wide):
    total = wide[:, :128]
    for i in range(1, wide.shape[1] // 128):
        total += wide[:, 128 * i : 128 * (i + 1)]
    return total


def early_kernel(
    me_ref, mine_ref, other_ref, w_ref, norm_ref, win_ref, wdown_ref, wout_ref, gain_ref, part_s
):
    near = mine_ref.shape[1]
    step = pl.program_id(0)
    steps = pl.num_programs(0)
    parts = steps // 2
    rows = D // (steps * near)

    def run(ref):
        for r in range(near):
            piece = ref[0, me_ref[1] ^ r].astype(F32)
            here = slice(r * rows, (r + 1) * rows)
            wide = jnp.concatenate([piece[rows * u : rows * (u + 1)] for u in range(6)], axis=1)
            win_ref[here, :] = wide
            at = pl.multiple_of((step * near + r) * rows, rows)
            part_s[pl.ds(at, rows), :] = fold_lanes(wide * w_ref[here, :].astype(F32))
            wdown_ref[3 * r * rows : 3 * (r + 1) * rows, :] = piece[6 * rows : 9 * rows]
            wout_ref[here, :LANES] = piece[9 * rows : 10 * rows]
            wout_ref[here, LANES:] = piece[10 * rows :]

    ours = (step // parts) == me_ref[2]
    pl.when(ours)(lambda: run(mine_ref))
    pl.when(jnp.logical_not(ours))(lambda: run(other_ref))

    @pl.when(step == steps - 1)
    def _():
        gain_ref[...] = jnp.sum(part_s[...].T, axis=0, keepdims=True) / norm_ref[...]


def assemble_early(me, mine, other, w_in, norm_two):
    parts, near = mine.shape[:2]
    steps = 2 * parts
    rows = D // steps

    def slot(own):
        def index(p, me):
            used = (p // parts == me[2]) == own
            return (jnp.where(used, me[0] ^ (p % parts), 0), 0, 0, 0)

        return pl.BlockSpec((1,) + mine.shape[1:], index)

    return pl.pallas_call(
        early_kernel,
        grid_spec=pltpu.PrefetchScalarGridSpec(
            num_scalar_prefetch=1,
            grid=(steps,),
            in_specs=[
                slot(True),
                slot(False),
                pl.BlockSpec((rows, 2 * FF), lambda p, me: (p, 0)),
                pl.BlockSpec((1, D), lambda p, me: (0, 0)),
            ],
            out_specs=[
                pl.BlockSpec((rows, 2 * FF), lambda p, me: (p, 0)),
                pl.BlockSpec((3 * rows, LANES), lambda p, me: (p % parts, p // parts)),
                pl.BlockSpec((rows, D), lambda p, me: (p, 0)),
                pl.BlockSpec((1, D), lambda p, me: (0, 0)),
            ],
            scratch_shapes=[pltpu.VMEM((D, 128), F32)],
        ),
        out_shape=[
            jax.ShapeDtypeStruct((D, 2 * FF), F32),
            jax.ShapeDtypeStruct((FF, D), F32),
            jax.ShapeDtypeStruct((D, D), F32),
            jax.ShapeDtypeStruct((1, D), F32),
        ],
        compiler_params=pltpu.CompilerParams(vmem_limit_bytes=12 << 20),
        cost_estimate=cost(1 << 20, 24 << 20),
        name="assemble_early",
    )(me, mine, other, w_in, norm_two[None, :])


def late_kernel(me_ref, *refs):
    mine, other = refs[:5], refs[5:10]
    w_ref, norm_ref, out_ref, gain_ref, rows_s = refs[10:]
    near = mine[0].shape[0]
    pieces = mine[0].shape[1] // 3
    width = rows_s.shape[1]
    lanes = pl.ds(pl.multiple_of(pl.program_id(0) * 128, 128), 128)
    total = None
    for block in range(3 * pieces):
        row = (block % pieces) * 3 + block // pieces
        for k in range(4):
            for q in range(near):
                which = k if k < 3 else 3 + q // (near // 2)
                place = q if k < 3 else q % (near // 2)
                at = (me_ref[0] ^ k) * HEAD_DIM + (me_ref[1] ^ q) * 8
                for ref, core in ((mine, me_ref[2]), (other, 1 - me_ref[2])):
                    here = pl.ds(pl.multiple_of(at + core * HALF, 8), 8)
                    rows_s[block, here, :] = ref[which][place, row, :, lanes].astype(F32)
        wide = rows_s[block].T
        cols = slice(block * width, (block + 1) * width)
        out_ref[:, cols] = wide
        part = fold_lanes(wide * w_ref[:, cols].astype(F32))
        total = part if total is None else total + part
    gain_ref[...] = jnp.sum(total.T, axis=0, keepdims=True) / norm_ref[...]


def assemble_late(me, mine, other, w_qkv, norm_one):
    blocks = mine[0].shape[1]
    sums = [pl.BlockSpec(v.shape, lambda b, me: (0, 0, 0, 0)) for v in mine]
    return pl.pallas_call(
        late_kernel,
        grid_spec=pltpu.PrefetchScalarGridSpec(
            num_scalar_prefetch=1,
            grid=(D // 128,),
            in_specs=sums
            + sums
            + [
                pl.BlockSpec((128, 3 * D), lambda b, me: (b, 0)),
                pl.BlockSpec((1, 128), lambda b, me: (0, b)),
            ],
            out_specs=[
                pl.BlockSpec((128, 3 * D), lambda b, me: (b, 0)),
                pl.BlockSpec((1, 128), lambda b, me: (0, b)),
            ],
            scratch_shapes=[pltpu.VMEM((blocks, 3 * D // blocks, 128), F32)],
        ),
        out_shape=[
            jax.ShapeDtypeStruct((D, 3 * D), F32),
            jax.ShapeDtypeStruct((1, D), F32),
        ],
        compiler_params=pltpu.CompilerParams(vmem_limit_bytes=60 << 20),
        cost_estimate=cost(1 << 20, 14 << 20),
        name="assemble_late",
    )(me, *mine, *other, w_qkv, norm_one[None, :])


def input_grad_kernel(parts, pieces, me_ref, *refs):
    pair, last = refs[:parts], refs[parts : 2 * parts]
    w_ref, tok_ref, norm_ref, mid_ref, out_ref, proj_s = refs[2 * parts :]
    span = proj_s.shape[1]
    for k in range(parts):
        group = me_ref[0] ^ k
        for j in range(pieces):
            if j < pieces - 1:
                piece = pair[k][...].reshape(pieces - 1, WIDE, span)[j]
            else:
                piece = last[k][...].reshape(WIDE, span)
            for part in range(3):
                at = part * D + (j * parts + group) * HEAD_DIM
                proj_s[pl.ds(pl.multiple_of(at, HEAD_DIM), HEAD_DIM), :] = piece[
                    part * HEAD_DIM : (part + 1) * HEAD_DIM
                ]
    upstream = dot(w_ref[...], proj_s[...]).T * norm_ref[...]
    values = tok_ref[...].astype(F32)
    centered = values - jnp.mean(values, axis=-1, keepdims=True)
    scale = lax.rsqrt(jnp.mean(centered * centered, axis=-1, keepdims=True) + EPSILON)
    unit = centered * scale
    flat = jnp.mean(upstream, axis=-1, keepdims=True)
    along = jnp.mean(upstream * unit, axis=-1, keepdims=True)
    out_ref[...] = mid_ref[...] + (upstream - flat - unit * along) * scale


def input_grad(me, pair, last, w_qkv, tokens, norm_one, grad_middle):
    parts = len(pair)
    span = tokens.shape[0]
    vmem = pl.BlockSpec(memory_space=pltpu.VMEM)
    return pl.pallas_call(
        functools.partial(input_grad_kernel, parts, 3),
        in_specs=[pl.BlockSpec(memory_space=pltpu.SMEM)] + [vmem] * (2 * parts + 4),
        out_specs=vmem,
        out_shape=jax.ShapeDtypeStruct((span, D), F32),
        scratch_shapes=[pltpu.VMEM((3 * D, span), BF16)],
        compiler_params=pltpu.CompilerParams(vmem_limit_bytes=20 << 20),
        cost_estimate=cost(2 * span * 3 * D * D, 10 << 20),
        name="input_grad",
    )(me, *pair, *last, w_qkv, tokens, norm_one[None, :], grad_middle)


def swap(values, axis, k):
    size = lax.axis_size(axis)
    return lax.ppermute(values, axis, [(i, i ^ k) for i in range(size)])


def add(*terms):
    total = terms[0].astype(F32)
    for term in terms[1:]:
        total += term.astype(F32)
    return total.astype(BF16)


def scatter_near(slots):
    return add(slots[0], *[swap(slots[k], "near", k) for k in range(1, len(slots))])


def gather_near(values):
    return jnp.stack([values] + [swap(values, "near", k) for k in range(1, lax.axis_size("near"))])


def tie(*values):
    return lax.optimization_barrier(values)


def on_device(tokens, doc_start, cotangent, norm_one, w_qkv, w_out, norm_two, w_in, w_down):
    parts = lax.axis_size("seq")
    near = lax.axis_size("near")
    far = lax.axis_size("far")
    span = tokens.shape[1]
    total = span * parts
    pieces = HEADS // parts
    bq = min(512, span)
    me_seq = lax.axis_index("seq").astype(jnp.int32)
    me = jnp.stack([lax.axis_index(a).astype(jnp.int32) for a in ("seq", "near", "core")])
    first_token = me_seq * span
    starts = doc_start[0]
    key_doc = starts[:, None]
    query_doc = starts[None, :]

    frequency = ROTARY_BASE ** (-(jnp.arange(HALF, dtype=F32) * 2.0 / HEAD_DIM))
    offset = (jnp.arange(total, dtype=jnp.int32) - starts).astype(F32)
    angles = frequency[:, None] * offset[None, :]
    cosine, sine = jnp.cos(angles), jnp.sin(angles)
    own_cosine = lax.dynamic_slice_in_dim(cosine, first_token, span, axis=1)
    own_sine = lax.dynamic_slice_in_dim(sine, first_token, span, axis=1)

    def sum_far(values):
        return lax.psum(values, "far") if far > 1 else values

    hn = first_norm(tokens[0], norm_one)
    qkv = []
    for j in range(pieces):
        sent = project(me, hn, w_qkv, own_cosine, own_sine, j, parts)
        qkv.append([sent] + [swap(sent[k], "seq", k) for k in range(1, parts)])
    contexts, lses = [], []
    for j in range(pieces):
        if j == pieces - 1:
            hn_late, qkv[j] = tie(hn, qkv[j])
            hn_near = [swap(hn_late, "seq", 1), swap(hn_late, "seq", 2)]
        context, lse = attend_forward(me, qkv[j], key_doc, query_doc, bq)
        contexts.append(context)
        lses.append(lse)
    arrived = [jnp.stack([c[k] for c in contexts]) for k in range(parts)]
    arrived[1:] = [swap(arrived[k], "seq", k) for k in range(1, parts)]
    arrived, hn_near = tie(arrived, hn_near)
    hn_far = [swap(hn_near[1][: span // 2], "seq", 1), swap(hn_near[0][span // 2 :], "seq", 2)]
    outs = middle_part(me, arrived, tokens[0], cotangent[0], w_out, norm_two, w_in, w_down)
    outs, hn_far = tie(outs, hn_far)
    context_t, normed_two, grad_gate_up, inner, grad_mid_low, grad_middle, result = outs[:7]
    hn_row = jnp.stack([hn, hn_near[0], hn_near[1], jnp.concatenate(hn_far)])
    upstream = [outs[7]] + [swap(outs[7 + k], "seq", k) for k in range(1, parts)]
    keep, give = early_grads(
        me, normed_two, grad_gate_up, inner, cotangent[0], context_t, grad_mid_low, parts, near
    )
    taken = swap(give, "core", 1)
    half = near // 2
    at = [2 * half, 4 * half, 5 * half, 6 * half, 7 * half, 8 * half]
    send_one = add(keep[: at[0]], taken[: at[0]])
    send_two = add(keep[at[0] : at[1]], taken[at[0] : at[1]])
    early = add(keep[at[1] :], taken[at[1] :])
    a_own, a_two, b_own, b_one = (early[i * half : (i + 1) * half] for i in range(4))
    send_one, send_two, early, upstream = tie(send_one, send_two, early, upstream)

    def backward(j, upstream):
        return attend_backward(
            me, qkv[j], key_doc, query_doc, upstream, j, contexts[j], lses[j], cosine, sine, bq,
            True,
        )

    from_one, from_two = swap(send_one, "seq", 1), swap(send_two, "seq", 2)
    grads = [backward(0, upstream)]
    grads[0], upstream, from_one, from_two = tie(grads[0], upstream, from_one, from_two)
    by_two = swap(add(a_two, from_one[half:]), "seq", 2)
    by_one = swap(add(b_one, from_two[half:]), "seq", 1)
    grads.append(backward(1, upstream))
    grads, upstream, by_two, by_one = tie(grads, upstream, by_two, by_one)
    own = jnp.stack(grads, axis=1)
    pair = [own[0]] + [swap(own[k], "seq", k) for k in range(1, parts)]
    early = [add(a_own[i], from_one[i], by_two[i]) for i in range(half)]
    early += [add(b_own[i], from_two[i], by_one[i]) for i in range(half)]
    early = scatter_near(early)
    grads.append(backward(2, upstream))

    grads, early, pair[1], pair[2] = tie(grads, early, pair[1], pair[2])
    early = sum_far(early)
    slots = [early] + [swap(early, "near", k) for k in range(1, near)]
    last = [grads[2][0]] + [swap(grads[2][k], "seq", k) for k in range(1, parts)]
    last, slots, grads, pair = tie(last, slots, grads, pair)
    early = jnp.stack(slots)
    one, two = swap(early, "seq", 1), swap(early, "seq", 2)
    kept, given = late_grads(me, grads, hn_row, near)
    late = add(kept, swap(given, "core", 1))
    late = sum_far(scatter_near(late))
    grad_input = input_grad(me, pair, last, w_qkv, tokens[0], norm_one, grad_middle)
    one, two, late, grad_input = tie(one, two, late, grad_input)
    far_one, far_two = swap(two[: near // 2], "seq", 1), swap(one[near // 2 :], "seq", 2)
    late = gather_near(late)
    far_one, far_two, late = tie(far_one, far_two, late)
    early = jnp.stack([early, one, two, jnp.concatenate([far_one, far_two])])
    early_other = swap(early, "core", 1)
    one, two = swap(late, "seq", 1), swap(late, "seq", 2)
    one, two, early_other = tie(one, two, early_other)
    far = [swap(two[: near // 2], "seq", 1), swap(one[near // 2 :], "seq", 2)]
    mine = [late, one, two]
    other = [swap(v, "core", 1) for v in mine]
    sum_w_in, sum_w_down, sum_w_out, sum_norm_two = assemble_early(
        me, early, early_other, w_in, norm_two
    )
    sum_w_in, far, other = tie(sum_w_in, far, other)
    mine += far
    other += [swap(v, "core", 1) for v in far]
    sum_w_qkv, sum_norm_one = assemble_late(me, mine, other, w_qkv, norm_one)
    return (
        result[None],
        grad_input[None],
        sum_norm_one[0],
        sum_w_qkv,
        sum_w_out,
        sum_norm_two[0],
        sum_w_in,
        sum_w_down,
    )


def solution(mesh):
    parts = mesh.shape["seq"]
    near = min(4, mesh.shape["dp"] // 2)
    split = Mesh(mesh.devices.reshape(parts, -1, near, 2), ("seq", "far", "near", "core"))
    rows = ("far", "near", "core")
    tokens_at = P(rows, "seq", None)
    return jax.shard_map(
        on_device,
        mesh=split,
        in_specs=(tokens_at, P(rows, None), tokens_at, P(), P(), P(), P(), P(), P()),
        out_specs=(tokens_at, tokens_at, P(), P(), P(), P(), P(), P()),
        check_vma=False,
    )
```

```python
import functools

import jax
import jax.numpy as jnp
from jax import lax
from jax.experimental import pallas as pl
from jax.experimental.pallas import tpu as pltpu
from jax.sharding import Mesh
from jax.sharding import PartitionSpec as P

D = 768
HEADS = 12
HEAD_DIM = 64
HALF = HEAD_DIM // 2
FF = 1152
WIDE = 3 * HEAD_DIM
LANES = D // 2

EPSILON = 1e-05
ROTARY_BASE = 160000.0
SCORE_SCALE = 0.125
SCORE_EXP2 = SCORE_SCALE * 1.4426950408889634
MASKED_SCORE = -1e30
KEY_CHUNK = 256
F32 = jnp.float32
BF16 = jnp.bfloat16

dot = functools.partial(jnp.dot, preferred_element_type=F32)


def cost(flops, moved, transcendentals=0):
    return pl.CostEstimate(
        flops=flops, bytes_accessed=moved, transcendentals=0
    )


def norm_kernel(tok_ref, norm_ref, out_ref):
    values = tok_ref[...].astype(F32)
    centered = values - jnp.mean(values, axis=-1, keepdims=True)
    variance = jnp.mean(centered * centered, axis=-1, keepdims=True)
    out_ref[...] = (centered * lax.rsqrt(variance + EPSILON) * norm_ref[...]).astype(BF16)


def first_norm(tokens, norm_one):
    rows = tokens.shape[0] // 2
    return pl.pallas_call(
        norm_kernel,
        grid=(2,),
        in_specs=[
            pl.BlockSpec((rows, D), lambda i: (i, 0)),
            pl.BlockSpec((1, D), lambda i: (0, 0)),
        ],
        out_specs=pl.BlockSpec((rows, D), lambda i: (i, 0)),
        out_shape=jax.ShapeDtypeStruct(tokens.shape, BF16),
        compiler_params=pltpu.CompilerParams(vmem_limit_bytes=6 << 20),
        cost_estimate=cost(1 << 20, 2 << 20),
        name="first_norm",
    )(tokens, norm_one[None, :])


def project_kernel(me_ref, hn_ref, w_ref, cos_ref, sin_ref, out_ref):
    part = pl.program_id(0)
    turned = dot(hn_ref[...], w_ref[...]).T
    cosine = jnp.where(part < 2, cos_ref[...], 1.0)
    sine = jnp.where(part < 2, sin_ref[...], 0.0)
    row = pl.multiple_of(part * HEAD_DIM, HEAD_DIM)
    for g in range(out_ref.shape[0]):
        slot = me_ref[0] ^ g
        first = turned[g * HEAD_DIM : g * HEAD_DIM + HALF]
        second = turned[g * HEAD_DIM + HALF : (g + 1) * HEAD_DIM]
        out_ref[slot, pl.ds(row, HALF), :] = (first * cosine - second * sine).astype(BF16)
        out_ref[slot, pl.ds(row + HALF, HALF), :] = (second * cosine + first * sine).astype(BF16)


def project(me, hn, w_qkv, cosine, sine, piece, groups):
    tokens = hn.shape[0]
    width = groups * HEAD_DIM
    pieces = D // width
    return pl.pallas_call(
        project_kernel,
        grid_spec=pltpu.PrefetchScalarGridSpec(
            num_scalar_prefetch=1,
            grid=(3,),
            in_specs=[
                pl.BlockSpec((tokens, D), lambda i, me: (0, 0)),
                pl.BlockSpec((D, width), lambda i, me: (0, i * pieces + piece)),
                pl.BlockSpec((HALF, tokens), lambda i, me: (0, 0)),
                pl.BlockSpec((HALF, tokens), lambda i, me: (0, 0)),
            ],
            out_specs=pl.BlockSpec((groups, WIDE, tokens), lambda i, me: (0, 0, 0)),
        ),
        out_shape=jax.ShapeDtypeStruct((groups, WIDE, tokens), BF16),
        compiler_params=pltpu.CompilerParams(vmem_limit_bytes=32 << 20),
        cost_estimate=cost(6 * tokens * D * width, 4 << 20),
        name="project",
    )(me, hn, w_qkv, cosine, sine)


def mask_scores(scores, chunk, chunks, edge, key_doc, query_doc, query_main):
    if chunk == 0 or chunk == chunks - 1:
        own = key_doc[: KEY_CHUNK, :] if chunk == 0 else key_doc[KEY_CHUNK :, :]
        return jnp.where(own == query_doc, scores, MASKED_SCORE)
    if edge:
        return jnp.where(query_main, scores, MASKED_SCORE)
    return scores


def put_edges(doc_ref, edge_s):
    total = doc_ref.shape[1]
    for i, at in enumerate((0, total - KEY_CHUNK)):
        tall = jnp.broadcast_to(doc_ref[:, at : at + KEY_CHUNK], (8, KEY_CHUNK)).T
        edge_s[i * KEY_CHUNK : (i + 1) * KEY_CHUNK, :] = tall[:, :1]


def put_in_order(me, slots, qkv_s, key_s, value_s=None):
    span = qkv_s.shape[2]
    for k, ref in enumerate(slots):
        at = me ^ k
        piece = ref[...].reshape(WIDE, span)
        qkv_s[at] = piece
        rows = pl.ds(pl.multiple_of(at * span, span), span)
        key_s[rows, :] = piece[HEAD_DIM : 2 * HEAD_DIM].astype(F32).T.astype(BF16)
        if value_s is not None:
            value_s[rows, :] = piece[2 * HEAD_DIM :].astype(F32).T.astype(BF16)


def slot_specs(slots):
    own = pl.BlockSpec((1,) + slots[0].shape[1:], lambda i, me: (0, 0, 0))
    rest = [pl.BlockSpec(s.shape, lambda i, me: (0, 0)) for s in slots[1:]]
    return [own] + rest


def forward_kernel(bq, parts, me_ref, *refs):
    slots = refs[:parts]
    doc_ref, out_ref, lse_ref, qkv_s, key_s, edge_s, score_s = refs[parts:]
    step = pl.program_id(0)
    steps = pl.num_programs(0)
    total = key_s.shape[0]
    chunks = total // KEY_CHUNK
    span = qkv_s.shape[2]
    ratio = span // bq

    @pl.when(step == 0)
    def _():
        put_in_order(me_ref[0], slots, qkv_s, key_s)
        put_edges(doc_ref, edge_s)

    def run(edge):
        lanes = pl.ds(pl.multiple_of((step % ratio) * bq, bq), bq)
        queries = qkv_s[step // ratio, 0:HEAD_DIM, lanes]
        query_doc = doc_ref[:, pl.ds(pl.multiple_of(step * bq, bq), bq)]
        query_main = query_doc == doc_ref[:, total // 2 : total // 2 + 1]
        top = None
        for c in range(chunks):
            rows = slice(c * KEY_CHUNK, (c + 1) * KEY_CHUNK)
            scores = dot(key_s[rows, :], queries)
            scores = mask_scores(scores, c, chunks, edge, edge_s, query_doc, query_main)
            score_s[rows, :] = scores
            peak = jnp.max(scores.reshape(KEY_CHUNK // 8, 8, bq), axis=0)
            top = peak if top is None else jnp.maximum(top, peak)
        top = jnp.max(top, axis=0, keepdims=True) * SCORE_EXP2
        mass, acc = None, None
        for c in range(chunks):
            rows = slice(c * KEY_CHUNK, (c + 1) * KEY_CHUNK)
            weight = jnp.exp2(score_s[rows, :] * SCORE_EXP2 - top)
            part = jnp.sum(weight.reshape(KEY_CHUNK // 8, 8, bq), axis=0)
            mass = part if mass is None else mass + part
            at = c * KEY_CHUNK % span
            values = qkv_s[c * KEY_CHUNK // span, 2 * HEAD_DIM :, at : at + KEY_CHUNK]
            term = dot(values, weight.astype(BF16))
            acc = term if acc is None else acc + term
        mass = jnp.sum(mass, axis=0, keepdims=True)
        out_ref[0] = (acc / mass).astype(BF16)
        lse_ref[...] = top + jnp.log2(mass)

    at_edge = (step == 0) | (step == steps - 1)
    pl.when(at_edge)(lambda: run(True))
    pl.when(jnp.logical_not(at_edge))(lambda: run(False))


def attend_forward(me, slots, docs, bq):
    parts, _, span = slots[0].shape
    total = parts * span
    ratio = span // bq
    return pl.pallas_call(
        functools.partial(forward_kernel, bq, parts),
        grid_spec=pltpu.PrefetchScalarGridSpec(
            num_scalar_prefetch=1,
            grid=(total // bq,),
            in_specs=slot_specs(slots)
            + [
                pl.BlockSpec((1, total), lambda i, me: (0, 0)),
            ],
            out_specs=[
                pl.BlockSpec((1, HEAD_DIM, bq), lambda i, me: (i // ratio ^ me[0], 0, i % ratio)),
                pl.BlockSpec((1, bq), lambda i, me: (0, i)),
            ],
            scratch_shapes=[
                pltpu.VMEM((parts, WIDE, span), BF16),
                pltpu.VMEM((total, HEAD_DIM), BF16),
                pltpu.VMEM((2 * KEY_CHUNK, 1), jnp.int32),
                pltpu.VMEM((total, bq), F32),
            ],
        ),
        out_shape=[
            jax.ShapeDtypeStruct((parts, HEAD_DIM, span), BF16),
            jax.ShapeDtypeStruct((1, total), F32),
        ],
        compiler_params=pltpu.CompilerParams(vmem_limit_bytes=40 << 20),
        cost_estimate=cost(16 * HEAD_DIM * total * total, 4 << 20, total * total),
        name="attend_forward",
    )(me, *slots, docs)


def backward_kernel(bq, parts, turn, me_ref, *refs):
    slots, ups = refs[:parts], refs[parts : 2 * parts]
    (doc_ref, o_ref, lse_ref, cos_ref, sin_ref, grad_ref,
     qkv_s, key_s, value_s, up_s, edge_s, dk_s, dv_s) = refs[2 * parts :]
    step = pl.program_id(0)
    steps = pl.num_programs(0)
    total = key_s.shape[0]
    chunks = total // KEY_CHUNK
    span = qkv_s.shape[2]
    ratio = span // bq

    @pl.when(step == 0)
    def _():
        put_in_order(me_ref[0], slots, qkv_s, key_s, value_s)
        put_edges(doc_ref, edge_s)
        for k, ref in enumerate(ups):
            up_s[me_ref[0] ^ k] = ref[...].reshape(HEAD_DIM, span)
        dk_s[...] = jnp.zeros_like(dk_s)
        dv_s[...] = jnp.zeros_like(dv_s)

    def turn_back(grad, cosine, sine):
        first, second = grad[:HALF], grad[HALF:]
        return first * cosine + second * sine, second * cosine - first * sine

    def run(edge):
        lanes = pl.ds(pl.multiple_of((step % ratio) * bq, bq), bq)
        here = pl.ds(pl.multiple_of(step * bq, bq), bq)
        queries = qkv_s[step // ratio, 0:HEAD_DIM, lanes]
        upstream = up_s[step // ratio, :, lanes]
        wide_up = upstream.astype(F32)
        centre = jnp.sum(wide_up * o_ref[0].astype(F32), axis=0, keepdims=True)
        query_rows = queries.astype(F32).T.astype(BF16)
        up_rows = wide_up.T.astype(BF16)
        query_doc = doc_ref[:, pl.ds(pl.multiple_of(step * bq, bq), bq)]
        query_main = query_doc == doc_ref[:, total // 2 : total // 2 + 1]
        lse = lse_ref[...]
        dq = None
        for c in range(chunks):
            rows = slice(c * KEY_CHUNK, (c + 1) * KEY_CHUNK)
            scores = dot(key_s[rows, :], queries)
            scores = mask_scores(scores, c, chunks, edge, edge_s, query_doc, query_main)
            probs = jnp.exp2(scores * SCORE_EXP2 - lse)
            grad_prob = dot(value_s[rows, :], upstream)
            grad_scores = (probs * (grad_prob - centre)).astype(BF16)
            dv_s[rows, :] += dot(probs.astype(BF16), up_rows)
            dk_s[rows, :] += dot(grad_scores, query_rows)
            at = c * KEY_CHUNK % span
            keys = qkv_s[c * KEY_CHUNK // span, HEAD_DIM : 2 * HEAD_DIM, at : at + KEY_CHUNK]
            term = dot(keys, grad_scores)
            dq = term if dq is None else dq + term
        one, two = turn_back(dq * SCORE_SCALE, cos_ref[:, here], sin_ref[:, here])
        slot = (me_ref[0] if turn else 0) ^ (step // ratio)
        grad_ref[slot, 0:HALF, lanes] = one.astype(BF16)
        grad_ref[slot, HALF:HEAD_DIM, lanes] = two.astype(BF16)

    at_edge = (step == 0) | (step == steps - 1)
    pl.when(at_edge)(lambda: run(True))
    pl.when(jnp.logical_not(at_edge))(lambda: run(False))

    @pl.when(step == steps - 1)
    def _():
        for s in range(parts):
            slot = (me_ref[0] if turn else 0) ^ s
            rows = slice(s * span, (s + 1) * span)
            one, two = turn_back(dk_s[rows, :].T * SCORE_SCALE, cos_ref[:, rows], sin_ref[:, rows])
            grad_ref[slot, HEAD_DIM : HEAD_DIM + HALF, :] = one.astype(BF16)
            grad_ref[slot, HEAD_DIM + HALF : 2 * HEAD_DIM, :] = two.astype(BF16)
            grad_ref[slot, 2 * HEAD_DIM :, :] = dv_s[rows, :].T.astype(BF16)


def attend_backward(
    me, slots, docs, upstream, piece, context, lse, cosine, sine, bq, turn
):
    parts, _, span = slots[0].shape
    total = parts * span
    ratio = span // bq
    return pl.pallas_call(
        functools.partial(backward_kernel, bq, parts, turn),
        grid_spec=pltpu.PrefetchScalarGridSpec(
            num_scalar_prefetch=1,
            grid=(total // bq,),
            in_specs=slot_specs(slots)
            + [pl.BlockSpec((1, HEAD_DIM, span), lambda i, me: (piece, 0, 0))] * parts
            + [
                pl.BlockSpec((1, total), lambda i, me: (0, 0)),
                pl.BlockSpec((1, HEAD_DIM, bq), lambda i, me: (i // ratio ^ me[0], 0, i % ratio)),
                pl.BlockSpec((1, bq), lambda i, me: (0, i)),
                pl.BlockSpec((HALF, total), lambda i, me: (0, 0)),
                pl.BlockSpec((HALF, total), lambda i, me: (0, 0)),
            ],
            out_specs=pl.BlockSpec((parts, WIDE, span), lambda i, me: (0, 0, 0)),
            scratch_shapes=[
                pltpu.VMEM((parts, WIDE, span), BF16),
                pltpu.VMEM((total, HEAD_DIM), BF16),
                pltpu.VMEM((total, HEAD_DIM), BF16),
                pltpu.VMEM((parts, HEAD_DIM, span), BF16),
                pltpu.VMEM((2 * KEY_CHUNK, 1), jnp.int32),
                pltpu.VMEM((total, HEAD_DIM), F32),
                pltpu.VMEM((total, HEAD_DIM), F32),
            ],
        ),
        out_shape=jax.ShapeDtypeStruct((parts, WIDE, span), BF16),
        compiler_params=pltpu.CompilerParams(vmem_limit_bytes=40 << 20),
        cost_estimate=cost(40 * HEAD_DIM * total * total, 6 << 20, total * total),
        name="attend_backward",
    )(me, *slots, *upstream, docs, context, lse, cosine, sine)


def dot_rows(a, b):
    return lax.dot_general(a, b, (((1,), (1,)), ((), ())), preferred_element_type=F32)


def middle_kernel(parts, me_ref, *refs):
    slots = refs[:parts]
    (tok_ref, cot_ref, wout_ref, norm_ref, win_ref, wdown_ref,
     ctx_ref, n2_ref, gu_ref, inner_ref, low_ref, mid_ref, result_ref) = refs[parts : parts + 13]
    outs, down_s = refs[parts + 13 : -1], refs[-1]
    pieces = slots[0].shape[0]

    def rows_of(j, k):
        at = (j * parts + (me_ref[0] ^ k)) * HEAD_DIM
        return pl.ds(pl.multiple_of(at, HEAD_DIM), HEAD_DIM)

    for k, ref in enumerate(slots):
        for j in range(pieces):
            ctx_ref[rows_of(j, k), :] = ref[j]
    context = ctx_ref[...].astype(F32).T.astype(BF16)
    middle = tok_ref[...].astype(F32) + dot(context, wout_ref[...])
    centered = middle - jnp.mean(middle, axis=-1, keepdims=True)
    scale = lax.rsqrt(jnp.mean(centered * centered, axis=-1, keepdims=True) + EPSILON)
    unit = centered * scale
    normed = (unit * norm_ref[...]).astype(BF16)
    n2_ref[...] = normed
    cotangent = cot_ref[...]
    for c in range(FF // LANES):
        cols = slice(c * LANES, (c + 1) * LANES)
        high = slice(FF + c * LANES, FF + (c + 1) * LANES)
        gate = dot(normed, win_ref[:, cols])
        up = dot(normed, win_ref[:, high])
        grad_inner = dot_rows(cotangent, wdown_ref[cols, :])
        share = 0.5 + 0.5 * lax.erf(gate * 0.7071067811865476)
        slope = share + gate * (0.3989422804014327 * jnp.exp(-0.5 * gate * gate))
        gelu = gate * share
        inner_ref[:, cols] = (gelu * up).astype(BF16)
        gu_ref[:, cols] = (slope * up * grad_inner).astype(BF16)
        gu_ref[:, high] = (gelu * grad_inner).astype(BF16)
    upstream = dot_rows(gu_ref[...], win_ref[...]) * norm_ref[...]
    flat = jnp.mean(upstream, axis=-1, keepdims=True)
    along = jnp.mean(upstream * unit, axis=-1, keepdims=True)
    grad_middle = cotangent.astype(F32) + (upstream - flat - unit * along) * scale
    mid_ref[...] = grad_middle
    low = grad_middle.astype(BF16)
    low_ref[...] = low
    down_s[...] = dot_rows(wout_ref[...], low).astype(BF16)
    for k, ref in enumerate(outs):
        for j in range(pieces):
            ref[j] = down_s[rows_of(j, k), :]
    result_ref[...] = (middle + dot(inner_ref[...], wdown_ref[...])).astype(BF16)


def middle_part(me, slots, tokens, cotangent, w_out, norm_two, w_in, w_down):
    parts, span = len(slots), tokens.shape[0]
    vmem = pl.BlockSpec(memory_space=pltpu.VMEM)
    like = lambda shape, kind=BF16: jax.ShapeDtypeStruct(shape, kind)
    out_shape = [
        like((D, span)),
        like((span, D)),
        like((span, 2 * FF)),
        like((span, FF)),
        like((span, D)),
        like((span, D), F32),
        like((span, D)),
    ] + [like(slots[0].shape)] * parts
    return pl.pallas_call(
        functools.partial(middle_kernel, parts),
        in_specs=[pl.BlockSpec(memory_space=pltpu.SMEM)] + [vmem] * (parts + 6),
        out_specs=[vmem] * len(out_shape),
        out_shape=out_shape,
        scratch_shapes=[pltpu.VMEM((D, span), BF16)],
        compiler_params=pltpu.CompilerParams(vmem_limit_bytes=18 << 20),
        cost_estimate=cost(2 * span * D * (2 * D + 5 * FF + 2 * FF), 20 << 20),
        name="middle_part",
    )(me, *slots, tokens, cotangent, w_out, norm_two[None, :], w_in, w_down)


def early_grad_kernel(at_ref, n2_ref, gu_ref, inner_ref, cot_ref, ctx_ref, mid_ref, keep_ref, give_ref):
    pieces = keep_ref.shape[0]
    rows = D // (2 * pieces)
    low = at_ref[0] == 0

    def put(first, second, count, at):
        kept = jnp.where(low, first, second).astype(BF16)
        given = jnp.where(low, second, first).astype(BF16)
        for p in range(pieces):
            here = slice(p * count, (p + 1) * count)
            place = at_ref[1 + p]
            keep_ref[place, at : at + count, :] = kept[here]
            give_ref[place, at : at + count, :] = given[here]

    n2_t = n2_ref[...].astype(F32).T.astype(BF16)
    for u in range(2 * FF // LANES):
        block = dot(n2_t, gu_ref[:, u * LANES : (u + 1) * LANES])
        put(block[: D // 2], block[D // 2 :], rows, u * rows)
    inner_t = inner_ref[...].astype(F32).T.astype(BF16)
    down = dot(inner_t, cot_ref[...])
    put(down[:, :LANES], down[:, LANES:], 3 * rows, 6 * rows)
    for u in range(2):
        block = dot(ctx_ref[...], mid_ref[:, u * LANES : (u + 1) * LANES])
        put(block[: D // 2], block[D // 2 :], rows, (9 + u) * rows)


def early_places(me, parts, near):
    half = near // 2
    first = [(k, q) for k in (1, 3) for q in range(half)]
    second = [(k, q) for k in (2, 3) for q in range(half, near)]
    kept = [(k, q) for k in (0, 2) for q in range(half)]
    kept += [(k, q) for k in (0, 1) for q in range(half, near)]
    order = {slot: i for i, slot in enumerate(first + second + kept)}
    table = jnp.array([order[k, q] for k in range(parts) for q in range(near)], jnp.int32)
    piece = jnp.arange(parts * near, dtype=jnp.int32)
    return jnp.concatenate([me[2:], table[piece ^ (me[0] * near + me[1])]])


def early_grads(me, n2, gate_up, inner, cotangent, context_t, mid, parts, near):
    rows = D // (2 * parts * near)
    shape = jax.ShapeDtypeStruct((parts * near, 11 * rows, LANES), BF16)
    operands = (n2, gate_up, inner, cotangent, context_t, mid)
    once = lambda a: pl.BlockSpec(a.shape, lambda i, at: (0,) * len(a.shape))
    return pl.pallas_call(
        early_grad_kernel,
        grid_spec=pltpu.PrefetchScalarGridSpec(
            num_scalar_prefetch=1,
            grid=(1,),
            in_specs=[once(a) for a in operands],
            out_specs=[once(shape), once(shape)],
        ),
        out_shape=[shape, shape],
        compiler_params=pltpu.CompilerParams(vmem_limit_bytes=28 << 20),
        cost_estimate=cost(2 * n2.shape[0] * 4224 * D, 14 << 20),
        name="early_grads",
    )(early_places(me, parts, near), *operands)


def late_grad_kernel(pieces, me_ref, *refs):
    grads = refs[:pieces]
    hn_ref, keep_ref, give_ref = refs[pieces:]
    parts = hn_ref.shape[0]
    near = keep_ref.shape[0]
    low = me_ref[2] == 0
    for j, ref in enumerate(grads):
        block = None
        for s in range(parts):
            term = dot(ref[s], hn_ref[s])
            block = term if block is None else block + term
        for part in range(3):
            head = block[part * HEAD_DIM : (part + 1) * HEAD_DIM]
            first, second = head[:HALF], head[HALF:]
            kept = jnp.where(low, first, second).astype(BF16)
            given = jnp.where(low, second, first).astype(BF16)
            for r in range(near):
                slot = me_ref[1] ^ r
                keep_ref[slot, 3 * j + part] = kept[8 * r : 8 * r + 8]
                give_ref[slot, 3 * j + part] = given[8 * r : 8 * r + 8]


def late_grads(me, grads, hn_row, near):
    pieces = len(grads)
    shape = jax.ShapeDtypeStruct((near, 3 * pieces, 8, D), BF16)
    vmem = pl.BlockSpec(memory_space=pltpu.VMEM)
    return pl.pallas_call(
        functools.partial(late_grad_kernel, pieces),
        in_specs=[pl.BlockSpec(memory_space=pltpu.SMEM)] + [vmem] * (pieces + 1),
        out_specs=[vmem, vmem],
        out_shape=[shape, shape],
        compiler_params=pltpu.CompilerParams(vmem_limit_bytes=12 << 20),
        cost_estimate=cost(2 * 2048 * 576 * D, 6 << 20),
        name="late_grads",
    )(me, *grads, hn_row)


def fold_lanes(wide):
    total = wide[:, :128]
    for i in range(1, wide.shape[1] // 128):
        total += wide[:, 128 * i : 128 * (i + 1)]
    return total


def early_kernel(
    me_ref, mine_ref, other_ref, w_ref, norm_ref, win_ref, wdown_ref, wout_ref, gain_ref, part_s
):
    near = mine_ref.shape[1]
    step = pl.program_id(0)
    steps = pl.num_programs(0)
    parts = steps // 2
    rows = D // (steps * near)

    def run(ref):
        for r in range(near):
            piece = ref[0, me_ref[1] ^ r].astype(F32)
            here = slice(r * rows, (r + 1) * rows)
            wide = jnp.concatenate([piece[rows * u : rows * (u + 1)] for u in range(6)], axis=1)
            win_ref[here, :] = wide
            at = pl.multiple_of((step * near + r) * rows, rows)
            part_s[pl.ds(at, rows), :] = fold_lanes(wide * w_ref[here, :].astype(F32))
            wdown_ref[3 * r * rows : 3 * (r + 1) * rows, :] = piece[6 * rows : 9 * rows]
            wout_ref[here, :LANES] = piece[9 * rows : 10 * rows]
            wout_ref[here, LANES:] = piece[10 * rows :]

    ours = (step // parts) == me_ref[2]
    pl.when(ours)(lambda: run(mine_ref))
    pl.when(jnp.logical_not(ours))(lambda: run(other_ref))

    @pl.when(step == steps - 1)
    def _():
        gain_ref[...] = jnp.sum(part_s[...].T, axis=0, keepdims=True) / norm_ref[...]


def assemble_early(me, mine, other, w_in, norm_two):
    parts, near = mine.shape[:2]
    steps = 2 * parts
    rows = D // steps

    def slot(own):
        def index(p, me):
            used = (p // parts == me[2]) == own
            return (jnp.where(used, me[0] ^ (p % parts), 0), 0, 0, 0)

        return pl.BlockSpec((1,) + mine.shape[1:], index)

    return pl.pallas_call(
        early_kernel,
        grid_spec=pltpu.PrefetchScalarGridSpec(
            num_scalar_prefetch=1,
            grid=(steps,),
            in_specs=[
                slot(True),
                slot(False),
                pl.BlockSpec((rows, 2 * FF), lambda p, me: (p, 0)),
                pl.BlockSpec((1, D), lambda p, me: (0, 0)),
            ],
            out_specs=[
                pl.BlockSpec((rows, 2 * FF), lambda p, me: (p, 0)),
                pl.BlockSpec((3 * rows, LANES), lambda p, me: (p % parts, p // parts)),
                pl.BlockSpec((rows, D), lambda p, me: (p, 0)),
                pl.BlockSpec((1, D), lambda p, me: (0, 0)),
            ],
            scratch_shapes=[pltpu.VMEM((D, 128), F32)],
        ),
        out_shape=[
            jax.ShapeDtypeStruct((D, 2 * FF), F32),
            jax.ShapeDtypeStruct((FF, D), F32),
            jax.ShapeDtypeStruct((D, D), F32),
            jax.ShapeDtypeStruct((1, D), F32),
        ],
        compiler_params=pltpu.CompilerParams(vmem_limit_bytes=12 << 20),
        cost_estimate=cost(1 << 20, 24 << 20),
        name="assemble_early",
    )(me, mine, other, w_in, norm_two[None, :])


def late_kernel(me_ref, *refs):
    mine, other = refs[:5], refs[5:10]
    w_ref, norm_ref, out_ref, gain_ref, rows_s = refs[10:]
    near = mine[0].shape[0]
    pieces = mine[0].shape[1] // 3
    width = rows_s.shape[1]
    lanes = pl.ds(pl.multiple_of(pl.program_id(0) * 128, 128), 128)
    total = None
    for block in range(3 * pieces):
        row = (block % pieces) * 3 + block // pieces
        for k in range(4):
            for q in range(near):
                which = k if k < 3 else 3 + q // (near // 2)
                place = q if k < 3 else q % (near // 2)
                at = (me_ref[0] ^ k) * HEAD_DIM + (me_ref[1] ^ q) * 8
                for ref, core in ((mine, me_ref[2]), (other, 1 - me_ref[2])):
                    here = pl.ds(pl.multiple_of(at + core * HALF, 8), 8)
                    rows_s[block, here, :] = ref[which][place, row, :, lanes].astype(F32)
        wide = rows_s[block].T
        cols = slice(block * width, (block + 1) * width)
        out_ref[:, cols] = wide
        part = fold_lanes(wide * w_ref[:, cols].astype(F32))
        total = part if total is None else total + part
    gain_ref[...] = jnp.sum(total.T, axis=0, keepdims=True) / norm_ref[...]


def assemble_late(me, mine, other, w_qkv, norm_one):
    blocks = mine[0].shape[1]
    sums = [pl.BlockSpec(v.shape, lambda b, me: (0, 0, 0, 0)) for v in mine]
    return pl.pallas_call(
        late_kernel,
        grid_spec=pltpu.PrefetchScalarGridSpec(
            num_scalar_prefetch=1,
            grid=(D // 128,),
            in_specs=sums
            + sums
            + [
                pl.BlockSpec((128, 3 * D), lambda b, me: (b, 0)),
                pl.BlockSpec((1, 128), lambda b, me: (0, b)),
            ],
            out_specs=[
                pl.BlockSpec((128, 3 * D), lambda b, me: (b, 0)),
                pl.BlockSpec((1, 128), lambda b, me: (0, b)),
            ],
            scratch_shapes=[pltpu.VMEM((blocks, 3 * D // blocks, 128), F32)],
        ),
        out_shape=[
            jax.ShapeDtypeStruct((D, 3 * D), F32),
            jax.ShapeDtypeStruct((1, D), F32),
        ],
        compiler_params=pltpu.CompilerParams(vmem_limit_bytes=60 << 20),
        cost_estimate=cost(1 << 20, 14 << 20),
        name="assemble_late",
    )(me, *mine, *other, w_qkv, norm_one[None, :])


def input_grad_kernel(parts, pieces, me_ref, *refs):
    pair, last = refs[:parts], refs[parts : 2 * parts]
    w_ref, tok_ref, norm_ref, mid_ref, out_ref, proj_s = refs[2 * parts :]
    span = proj_s.shape[1]
    for k in range(parts):
        group = me_ref[0] ^ k
        for j in range(pieces):
            if j < pieces - 1:
                piece = pair[k][...].reshape(pieces - 1, WIDE, span)[j]
            else:
                piece = last[k][...].reshape(WIDE, span)
            for part in range(3):
                at = part * D + (j * parts + group) * HEAD_DIM
                proj_s[pl.ds(pl.multiple_of(at, HEAD_DIM), HEAD_DIM), :] = piece[
                    part * HEAD_DIM : (part + 1) * HEAD_DIM
                ]
    upstream = dot(w_ref[...], proj_s[...]).T * norm_ref[...]
    values = tok_ref[...].astype(F32)
    centered = values - jnp.mean(values, axis=-1, keepdims=True)
    scale = lax.rsqrt(jnp.mean(centered * centered, axis=-1, keepdims=True) + EPSILON)
    unit = centered * scale
    flat = jnp.mean(upstream, axis=-1, keepdims=True)
    along = jnp.mean(upstream * unit, axis=-1, keepdims=True)
    out_ref[...] = mid_ref[...] + (upstream - flat - unit * along) * scale


def input_grad(me, pair, last, w_qkv, tokens, norm_one, grad_middle):
    parts = len(pair)
    span = tokens.shape[0]
    vmem = pl.BlockSpec(memory_space=pltpu.VMEM)
    return pl.pallas_call(
        functools.partial(input_grad_kernel, parts, 3),
        in_specs=[pl.BlockSpec(memory_space=pltpu.SMEM)] + [vmem] * (2 * parts + 4),
        out_specs=vmem,
        out_shape=jax.ShapeDtypeStruct((span, D), F32),
        scratch_shapes=[pltpu.VMEM((3 * D, span), BF16)],
        compiler_params=pltpu.CompilerParams(vmem_limit_bytes=20 << 20),
        cost_estimate=cost(2 * span * 3 * D * D, 10 << 20),
        name="input_grad",
    )(me, *pair, *last, w_qkv, tokens, norm_one[None, :], grad_middle)


def swap(values, axis, k):
    size = lax.axis_size(axis)
    return lax.ppermute(values, axis, [(i, i ^ k) for i in range(size)])


def add(*terms):
    total = terms[0].astype(F32)
    for term in terms[1:]:
        total += term.astype(F32)
    return total.astype(BF16)


def scatter_near(slots):
    return add(slots[0], *[swap(slots[k], "near", k) for k in range(1, len(slots))])


def gather_near(values):
    return jnp.stack([values] + [swap(values, "near", k) for k in range(1, lax.axis_size("near"))])


def tie(*values):
    return lax.optimization_barrier(values)


def on_device(tokens, doc_start, cotangent, norm_one, w_qkv, w_out, norm_two, w_in, w_down):
    parts = lax.axis_size("seq")
    near = lax.axis_size("near")
    far = lax.axis_size("far")
    span = tokens.shape[1]
    total = span * parts
    pieces = HEADS // parts
    bq = min(512, span)
    me_seq = lax.axis_index("seq").astype(jnp.int32)
    me = jnp.stack([lax.axis_index(a).astype(jnp.int32) for a in ("seq", "near", "core")])
    first_token = me_seq * span
    starts = doc_start[0]
    docs = doc_start

    frequency = ROTARY_BASE ** (-(jnp.arange(HALF, dtype=F32) * 2.0 / HEAD_DIM))
    offset = (jnp.arange(total, dtype=jnp.int32) - starts).astype(F32)
    angles = frequency[:, None] * offset[None, :]
    cosine, sine = jnp.cos(angles), jnp.sin(angles)
    own_cosine = lax.dynamic_slice_in_dim(cosine, first_token, span, axis=1)
    own_sine = lax.dynamic_slice_in_dim(sine, first_token, span, axis=1)

    def sum_far(values):
        return lax.psum(values, "far") if far > 1 else values

    hn = first_norm(tokens[0], norm_one)
    qkv = []
    for j in range(pieces):
        sent = project(me, hn, w_qkv, own_cosine, own_sine, j, parts)
        qkv.append([sent] + [swap(sent[k], "seq", k) for k in range(1, parts)])
    contexts, lses = [], []
    for j in range(pieces):
        if j == pieces - 1:
            hn_late, qkv[j] = tie(hn, qkv[j])
            hn_near = [swap(hn_late, "seq", 1), swap(hn_late, "seq", 2)]
        context, lse = attend_forward(me, qkv[j], docs, bq)
        contexts.append(context)
        lses.append(lse)
    arrived = [jnp.stack([c[k] for c in contexts]) for k in range(parts)]
    arrived[1:] = [swap(arrived[k], "seq", k) for k in range(1, parts)]
    arrived, hn_near = tie(arrived, hn_near)
    hn_far = [swap(hn_near[1][: span // 2], "seq", 1), swap(hn_near[0][span // 2 :], "seq", 2)]
    outs = middle_part(me, arrived, tokens[0], cotangent[0], w_out, norm_two, w_in, w_down)
    outs, hn_far = tie(outs, hn_far)
    context_t, normed_two, grad_gate_up, inner, grad_mid_low, grad_middle, result = outs[:7]
    hn_row = jnp.stack([hn, hn_near[0], hn_near[1], jnp.concatenate(hn_far)])
    upstream = [outs[7]] + [swap(outs[7 + k], "seq", k) for k in range(1, parts)]
    keep, give = early_grads(
        me, normed_two, grad_gate_up, inner, cotangent[0], context_t, grad_mid_low, parts, near
    )
    taken = swap(give, "core", 1)
    half = near // 2
    at = [2 * half, 4 * half, 5 * half, 6 * half, 7 * half, 8 * half]
    send_one = add(keep[: at[0]], taken[: at[0]])
    send_two = add(keep[at[0] : at[1]], taken[at[0] : at[1]])
    early = add(keep[at[1] :], taken[at[1] :])
    a_own, a_two, b_own, b_one = (early[i * half : (i + 1) * half] for i in range(4))
    send_one, send_two, early, upstream = tie(send_one, send_two, early, upstream)

    def backward(j, upstream):
        return attend_backward(
            me, qkv[j], docs, upstream, j, contexts[j], lses[j], cosine, sine, bq,
            True,
        )

    from_one, from_two = swap(send_one, "seq", 1), swap(send_two, "seq", 2)
    grads = [backward(0, upstream)]
    grads[0], upstream, from_one, from_two = tie(grads[0], upstream, from_one, from_two)
    by_two = swap(add(a_two, from_one[half:]), "seq", 2)
    by_one = swap(add(b_one, from_two[half:]), "seq", 1)
    grads.append(backward(1, upstream))
    grads, upstream, by_two, by_one = tie(grads, upstream, by_two, by_one)
    kept, given = late_grads(me, grads, hn_row, near)
    own = jnp.stack(grads, axis=1)
    pair = [own[0]] + [swap(own[k], "seq", k) for k in range(1, parts)]
    early = [add(a_own[i], from_one[i], by_two[i]) for i in range(half)]
    early += [add(b_own[i], from_two[i], by_one[i]) for i in range(half)]
    early = scatter_near(early)
    upstream, kept, given = tie(upstream, kept, given)
    grads.append(backward(2, upstream))

    grads, early, pair[1], pair[2] = tie(grads, early, pair[1], pair[2])
    early = sum_far(early)
    slots = [early] + [swap(early, "near", k) for k in range(1, near)]
    last = [grads[2][0]] + [swap(grads[2][k], "seq", k) for k in range(1, parts)]
    last, slots, grads[2], pair = tie(last, slots, grads[2], pair)
    early = jnp.stack(slots)
    one, two = swap(early, "seq", 1), swap(early, "seq", 2)
    kept_last, given_last = late_grads(me, grads[2:], hn_row, near)
    kept = jnp.concatenate([kept, kept_last], axis=1)
    given = jnp.concatenate([given, given_last], axis=1)
    late = add(kept, swap(given, "core", 1))
    late = sum_far(scatter_near(late))
    grad_input = input_grad(me, pair, last, w_qkv, tokens[0], norm_one, grad_middle)
    one, two, late, grad_input = tie(one, two, late, grad_input)
    far_one, far_two = swap(two[: near // 2], "seq", 1), swap(one[near // 2 :], "seq", 2)
    late = gather_near(late)
    far_one, far_two, late = tie(far_one, far_two, late)
    early = jnp.stack([early, one, two, jnp.concatenate([far_one, far_two])])
    early_other = swap(early, "core", 1)
    one, two = swap(late, "seq", 1), swap(late, "seq", 2)
    one, two, early_other = tie(one, two, early_other)
    far = [swap(two[: near // 2], "seq", 1), swap(one[near // 2 :], "seq", 2)]
    mine = [late, one, two]
    other = [swap(v, "core", 1) for v in mine]
    sum_w_in, sum_w_down, sum_w_out, sum_norm_two = assemble_early(
        me, early, early_other, w_in, norm_two
    )
    sum_w_in, far, other = tie(sum_w_in, far, other)
    mine += far
    other += [swap(v, "core", 1) for v in far]
    sum_w_qkv, sum_norm_one = assemble_late(me, mine, other, w_qkv, norm_one)
    return (
        result[None],
        grad_input[None],
        sum_norm_one[0],
        sum_w_qkv,
        sum_w_out,
        sum_norm_two[0],
        sum_w_in,
        sum_w_down,
    )


def solution(mesh):
    parts = mesh.shape["seq"]
    near = min(4, mesh.shape["dp"] // 2)
    split = Mesh(mesh.devices.reshape(parts, -1, near, 2), ("seq", "far", "near", "core"))
    rows = ("far", "near", "core")
    tokens_at = P(rows, "seq", None)
    return jax.shard_map(
        on_device,
        mesh=split,
        in_specs=(tokens_at, P(rows, None), tokens_at, P(), P(), P(), P(), P(), P()),
        out_specs=(tokens_at, tokens_at, P(), P(), P(), P(), P(), P()),
        check_vma=False,
    )
```

```python
import functools

import jax
import jax.numpy as jnp
from jax import lax
from jax.experimental import pallas as pl
from jax.experimental.pallas import tpu as pltpu
from jax.sharding import Mesh
from jax.sharding import PartitionSpec as P

D = 768
HEADS = 12
HEAD_DIM = 64
HALF = HEAD_DIM // 2
FF = 1152
WIDE = 3 * HEAD_DIM
LANES = D // 2

EPSILON = 1e-05
ROTARY_BASE = 160000.0
SCORE_SCALE = 0.125
SCORE_EXP2 = SCORE_SCALE * 1.4426950408889634
MASKED_SCORE = -1e30
KEY_CHUNK = 256
F32 = jnp.float32
BF16 = jnp.bfloat16

dot = functools.partial(jnp.dot, preferred_element_type=F32)


def cost(flops, moved, transcendentals=0):
    return pl.CostEstimate(
        flops=flops, bytes_accessed=moved, transcendentals=0
    )


def norm_kernel(tok_ref, norm_ref, out_ref):
    values = tok_ref[...].astype(F32)
    centered = values - jnp.mean(values, axis=-1, keepdims=True)
    variance = jnp.mean(centered * centered, axis=-1, keepdims=True)
    out_ref[...] = (centered * lax.rsqrt(variance + EPSILON) * norm_ref[...]).astype(BF16)


def first_norm(tokens, norm_one):
    rows = tokens.shape[0] // 2
    return pl.pallas_call(
        norm_kernel,
        grid=(2,),
        in_specs=[
            pl.BlockSpec((rows, D), lambda i: (i, 0)),
            pl.BlockSpec((1, D), lambda i: (0, 0)),
        ],
        out_specs=pl.BlockSpec((rows, D), lambda i: (i, 0)),
        out_shape=jax.ShapeDtypeStruct(tokens.shape, BF16),
        compiler_params=pltpu.CompilerParams(vmem_limit_bytes=6 << 20),
        cost_estimate=cost(1 << 20, 2 << 20),
        name="first_norm",
    )(tokens, norm_one[None, :])


def project_kernel(me_ref, hn_ref, w_ref, cos_ref, sin_ref, out_ref):
    part = pl.program_id(0)
    turned = dot(hn_ref[...], w_ref[...]).T
    cosine = jnp.where(part < 2, cos_ref[...], 1.0)
    sine = jnp.where(part < 2, sin_ref[...], 0.0)
    row = pl.multiple_of(part * HEAD_DIM, HEAD_DIM)
    for g in range(out_ref.shape[0]):
        slot = me_ref[0] ^ g
        first = turned[g * HEAD_DIM : g * HEAD_DIM + HALF]
        second = turned[g * HEAD_DIM + HALF : (g + 1) * HEAD_DIM]
        out_ref[slot, pl.ds(row, HALF), :] = (first * cosine - second * sine).astype(BF16)
        out_ref[slot, pl.ds(row + HALF, HALF), :] = (second * cosine + first * sine).astype(BF16)


def project(me, hn, w_qkv, cosine, sine, piece, groups):
    tokens = hn.shape[0]
    width = groups * HEAD_DIM
    pieces = D // width
    return pl.pallas_call(
        project_kernel,
        grid_spec=pltpu.PrefetchScalarGridSpec(
            num_scalar_prefetch=1,
            grid=(3,),
            in_specs=[
                pl.BlockSpec((tokens, D), lambda i, me: (0, 0)),
                pl.BlockSpec((D, width), lambda i, me: (0, i * pieces + piece)),
                pl.BlockSpec((HALF, tokens), lambda i, me: (0, 0)),
                pl.BlockSpec((HALF, tokens), lambda i, me: (0, 0)),
            ],
            out_specs=pl.BlockSpec((groups, WIDE, tokens), lambda i, me: (0, 0, 0)),
        ),
        out_shape=jax.ShapeDtypeStruct((groups, WIDE, tokens), BF16),
        compiler_params=pltpu.CompilerParams(vmem_limit_bytes=32 << 20),
        cost_estimate=cost(6 * tokens * D * width, 4 << 20),
        name="project",
    )(me, hn, w_qkv, cosine, sine)


def mask_scores(scores, chunk, chunks, edge, key_doc, query_doc, query_main):
    if chunk == 0 or chunk == chunks - 1:
        own = key_doc[: KEY_CHUNK, :] if chunk == 0 else key_doc[KEY_CHUNK :, :]
        return jnp.where(own == query_doc, scores, MASKED_SCORE)
    if edge:
        return jnp.where(query_main, scores, MASKED_SCORE)
    return scores


def put_edges(doc_ref, edge_s):
    total = doc_ref.shape[1]
    for i, at in enumerate((0, total - KEY_CHUNK)):
        tall = jnp.broadcast_to(doc_ref[:, at : at + KEY_CHUNK], (8, KEY_CHUNK)).T
        edge_s[i * KEY_CHUNK : (i + 1) * KEY_CHUNK, :] = tall[:, :1]


def put_in_order(me, slots, qkv_s, key_s, value_s=None):
    span = qkv_s.shape[2]
    for k, ref in enumerate(slots):
        at = me ^ k
        piece = ref[...].reshape(WIDE, span)
        qkv_s[at] = piece
        rows = pl.ds(pl.multiple_of(at * span, span), span)
        key_s[rows, :] = piece[HEAD_DIM : 2 * HEAD_DIM].astype(F32).T.astype(BF16)
        if value_s is not None:
            value_s[rows, :] = piece[2 * HEAD_DIM :].astype(F32).T.astype(BF16)


def slot_specs(slots):
    own = pl.BlockSpec((1,) + slots[0].shape[1:], lambda i, me: (0, 0, 0))
    rest = [pl.BlockSpec(s.shape, lambda i, me: (0, 0)) for s in slots[1:]]
    return [own] + rest


def forward_kernel(bq, parts, me_ref, *refs):
    slots = refs[:parts]
    doc_ref, out_ref, lse_ref, qkv_s, key_s, edge_s, score_s = refs[parts:]
    step = pl.program_id(0)
    steps = pl.num_programs(0)
    total = key_s.shape[0]
    chunks = total // KEY_CHUNK
    span = qkv_s.shape[2]
    ratio = span // bq

    @pl.when(step == 0)
    def _():
        put_in_order(me_ref[0], slots, qkv_s, key_s)
        put_edges(doc_ref, edge_s)

    def run(edge):
        lanes = pl.ds(pl.multiple_of((step % ratio) * bq, bq), bq)
        queries = qkv_s[step // ratio, 0:HEAD_DIM, lanes]
        query_doc = doc_ref[:, pl.ds(pl.multiple_of(step * bq, bq), bq)]
        query_main = query_doc == doc_ref[:, total // 2 : total // 2 + 1]
        top = None
        for c in range(chunks):
            rows = slice(c * KEY_CHUNK, (c + 1) * KEY_CHUNK)
            scores = dot(key_s[rows, :], queries)
            scores = mask_scores(scores, c, chunks, edge, edge_s, query_doc, query_main)
            score_s[rows, :] = scores
            peak = jnp.max(scores.reshape(KEY_CHUNK // 8, 8, bq), axis=0)
            top = peak if top is None else jnp.maximum(top, peak)
        top = jnp.max(top, axis=0, keepdims=True) * SCORE_EXP2
        mass, acc = None, None
        for c in range(chunks):
            rows = slice(c * KEY_CHUNK, (c + 1) * KEY_CHUNK)
            weight = jnp.exp2(score_s[rows, :] * SCORE_EXP2 - top)
            part = jnp.sum(weight.reshape(KEY_CHUNK // 8, 8, bq), axis=0)
            mass = part if mass is None else mass + part
            at = c * KEY_CHUNK % span
            values = qkv_s[c * KEY_CHUNK // span, 2 * HEAD_DIM :, at : at + KEY_CHUNK]
            term = dot(values, weight.astype(BF16))
            acc = term if acc is None else acc + term
        mass = jnp.sum(mass, axis=0, keepdims=True)
        out_ref[0] = (acc / mass).astype(BF16)
        lse_ref[...] = top + jnp.log2(mass)

    at_edge = (step == 0) | (step == steps - 1)
    pl.when(at_edge)(lambda: run(True))
    pl.when(jnp.logical_not(at_edge))(lambda: run(False))


def attend_forward(me, slots, docs, bq):
    parts, _, span = slots[0].shape
    total = parts * span
    ratio = span // bq
    return pl.pallas_call(
        functools.partial(forward_kernel, bq, parts),
        grid_spec=pltpu.PrefetchScalarGridSpec(
            num_scalar_prefetch=1,
            grid=(total // bq,),
            in_specs=slot_specs(slots)
            + [
                pl.BlockSpec((1, total), lambda i, me: (0, 0)),
            ],
            out_specs=[
                pl.BlockSpec((1, HEAD_DIM, bq), lambda i, me: (i // ratio ^ me[0], 0, i % ratio)),
                pl.BlockSpec((1, bq), lambda i, me: (0, i)),
            ],
            scratch_shapes=[
                pltpu.VMEM((parts, WIDE, span), BF16),
                pltpu.VMEM((total, HEAD_DIM), BF16),
                pltpu.VMEM((2 * KEY_CHUNK, 1), jnp.int32),
                pltpu.VMEM((total, bq), F32),
            ],
        ),
        out_shape=[
            jax.ShapeDtypeStruct((parts, HEAD_DIM, span), BF16),
            jax.ShapeDtypeStruct((1, total), F32),
        ],
        compiler_params=pltpu.CompilerParams(vmem_limit_bytes=40 << 20),
        cost_estimate=cost(16 * HEAD_DIM * total * total, 4 << 20, total * total),
        name="attend_forward",
    )(me, *slots, docs)


def backward_kernel(bq, parts, turn, me_ref, *refs):
    slots, ups = refs[:parts], refs[parts : 2 * parts]
    (doc_ref, o_ref, lse_ref, cos_ref, sin_ref, grad_ref,
     qkv_s, key_s, value_s, up_s, edge_s, dk_s, dv_s) = refs[2 * parts :]
    step = pl.program_id(0)
    steps = pl.num_programs(0)
    total = key_s.shape[0]
    chunks = total // KEY_CHUNK
    span = qkv_s.shape[2]
    ratio = span // bq

    @pl.when(step == 0)
    def _():
        put_in_order(me_ref[0], slots, qkv_s, key_s, value_s)
        put_edges(doc_ref, edge_s)
        for k, ref in enumerate(ups):
            up_s[me_ref[0] ^ k] = ref[...].reshape(HEAD_DIM, span)
        dk_s[...] = jnp.zeros_like(dk_s)
        dv_s[...] = jnp.zeros_like(dv_s)

    def turn_back(grad, cosine, sine):
        first, second = grad[:HALF], grad[HALF:]
        return first * cosine + second * sine, second * cosine - first * sine

    def run(edge):
        lanes = pl.ds(pl.multiple_of((step % ratio) * bq, bq), bq)
        here = pl.ds(pl.multiple_of(step * bq, bq), bq)
        queries = qkv_s[step // ratio, 0:HEAD_DIM, lanes]
        upstream = up_s[step // ratio, :, lanes]
        wide_up = upstream.astype(F32)
        centre = jnp.sum(wide_up * o_ref[0].astype(F32), axis=0, keepdims=True)
        query_rows = queries.astype(F32).T.astype(BF16)
        up_rows = wide_up.T.astype(BF16)
        query_doc = doc_ref[:, pl.ds(pl.multiple_of(step * bq, bq), bq)]
        query_main = query_doc == doc_ref[:, total // 2 : total // 2 + 1]
        lse = lse_ref[...]
        dq = None
        for c in range(chunks):
            rows = slice(c * KEY_CHUNK, (c + 1) * KEY_CHUNK)
            scores = dot(key_s[rows, :], queries)
            scores = mask_scores(scores, c, chunks, edge, edge_s, query_doc, query_main)
            probs = jnp.exp2(scores * SCORE_EXP2 - lse)
            grad_prob = dot(value_s[rows, :], upstream)
            grad_scores = (probs * (grad_prob - centre)).astype(BF16)
            dv_s[rows, :] += dot(probs.astype(BF16), up_rows)
            dk_s[rows, :] += dot(grad_scores, query_rows)
            at = c * KEY_CHUNK % span
            keys = qkv_s[c * KEY_CHUNK // span, HEAD_DIM : 2 * HEAD_DIM, at : at + KEY_CHUNK]
            term = dot(keys, grad_scores)
            dq = term if dq is None else dq + term
        one, two = turn_back(dq * SCORE_SCALE, cos_ref[:, here], sin_ref[:, here])
        slot = (me_ref[0] if turn else 0) ^ (step // ratio)
        grad_ref[slot, 0:HALF, lanes] = one.astype(BF16)
        grad_ref[slot, HALF:HEAD_DIM, lanes] = two.astype(BF16)

    at_edge = (step == 0) | (step == steps - 1)
    pl.when(at_edge)(lambda: run(True))
    pl.when(jnp.logical_not(at_edge))(lambda: run(False))

    @pl.when(step == steps - 1)
    def _():
        for s in range(parts):
            slot = (me_ref[0] if turn else 0) ^ s
            rows = slice(s * span, (s + 1) * span)
            one, two = turn_back(dk_s[rows, :].T * SCORE_SCALE, cos_ref[:, rows], sin_ref[:, rows])
            grad_ref[slot, HEAD_DIM : HEAD_DIM + HALF, :] = one.astype(BF16)
            grad_ref[slot, HEAD_DIM + HALF : 2 * HEAD_DIM, :] = two.astype(BF16)
            grad_ref[slot, 2 * HEAD_DIM :, :] = dv_s[rows, :].T.astype(BF16)


def attend_backward(
    me, slots, docs, upstream, piece, context, lse, cosine, sine, bq, turn
):
    parts, _, span = slots[0].shape
    total = parts * span
    ratio = span // bq
    return pl.pallas_call(
        functools.partial(backward_kernel, bq, parts, turn),
        grid_spec=pltpu.PrefetchScalarGridSpec(
            num_scalar_prefetch=1,
            grid=(total // bq,),
            in_specs=slot_specs(slots)
            + [pl.BlockSpec((1, HEAD_DIM, span), lambda i, me: (piece, 0, 0))] * parts
            + [
                pl.BlockSpec((1, total), lambda i, me: (0, 0)),
                pl.BlockSpec((1, HEAD_DIM, bq), lambda i, me: (i // ratio ^ me[0], 0, i % ratio)),
                pl.BlockSpec((1, bq), lambda i, me: (0, i)),
                pl.BlockSpec((HALF, total), lambda i, me: (0, 0)),
                pl.BlockSpec((HALF, total), lambda i, me: (0, 0)),
            ],
            out_specs=pl.BlockSpec((parts, WIDE, span), lambda i, me: (0, 0, 0)),
            scratch_shapes=[
                pltpu.VMEM((parts, WIDE, span), BF16),
                pltpu.VMEM((total, HEAD_DIM), BF16),
                pltpu.VMEM((total, HEAD_DIM), BF16),
                pltpu.VMEM((parts, HEAD_DIM, span), BF16),
                pltpu.VMEM((2 * KEY_CHUNK, 1), jnp.int32),
                pltpu.VMEM((total, HEAD_DIM), F32),
                pltpu.VMEM((total, HEAD_DIM), F32),
            ],
        ),
        out_shape=jax.ShapeDtypeStruct((parts, WIDE, span), BF16),
        compiler_params=pltpu.CompilerParams(vmem_limit_bytes=40 << 20),
        cost_estimate=cost(40 * HEAD_DIM * total * total, 6 << 20, total * total),
        name="attend_backward",
    )(me, *slots, *upstream, docs, context, lse, cosine, sine)


def dot_rows(a, b):
    return lax.dot_general(a, b, (((1,), (1,)), ((), ())), preferred_element_type=F32)


def middle_kernel(parts, me_ref, *refs):
    slots = refs[:parts]
    (tok_ref, cot_ref, wout_ref, norm_ref, win_ref, wdown_ref,
     ctx_ref, n2_ref, gu_ref, inner_ref, low_ref, mid_ref, result_ref) = refs[parts : parts + 13]
    outs, down_s = refs[parts + 13 : -1], refs[-1]
    pieces = slots[0].shape[0]

    def rows_of(j, k):
        at = (j * parts + (me_ref[0] ^ k)) * HEAD_DIM
        return pl.ds(pl.multiple_of(at, HEAD_DIM), HEAD_DIM)

    for k, ref in enumerate(slots):
        for j in range(pieces):
            ctx_ref[rows_of(j, k), :] = ref[j]
    context = ctx_ref[...].astype(F32).T.astype(BF16)
    middle = tok_ref[...].astype(F32) + dot(context, wout_ref[...])
    centered = middle - jnp.mean(middle, axis=-1, keepdims=True)
    scale = lax.rsqrt(jnp.mean(centered * centered, axis=-1, keepdims=True) + EPSILON)
    unit = centered * scale
    normed = (unit * norm_ref[...]).astype(BF16)
    n2_ref[...] = normed
    cotangent = cot_ref[...]
    for c in range(FF // LANES):
        cols = slice(c * LANES, (c + 1) * LANES)
        high = slice(FF + c * LANES, FF + (c + 1) * LANES)
        gate = dot(normed, win_ref[:, cols])
        up = dot(normed, win_ref[:, high])
        grad_inner = dot_rows(cotangent, wdown_ref[cols, :])
        share = 0.5 + 0.5 * lax.erf(gate * 0.7071067811865476)
        slope = share + gate * (0.3989422804014327 * jnp.exp(-0.5 * gate * gate))
        gelu = gate * share
        inner_ref[:, cols] = (gelu * up).astype(BF16)
        gu_ref[:, cols] = (slope * up * grad_inner).astype(BF16)
        gu_ref[:, high] = (gelu * grad_inner).astype(BF16)
    upstream = dot_rows(gu_ref[...], win_ref[...]) * norm_ref[...]
    flat = jnp.mean(upstream, axis=-1, keepdims=True)
    along = jnp.mean(upstream * unit, axis=-1, keepdims=True)
    grad_middle = cotangent.astype(F32) + (upstream - flat - unit * along) * scale
    mid_ref[...] = grad_middle
    low = grad_middle.astype(BF16)
    low_ref[...] = low
    down_s[...] = dot_rows(wout_ref[...], low).astype(BF16)
    for k, ref in enumerate(outs):
        for j in range(pieces):
            ref[j] = down_s[rows_of(j, k), :]
    result_ref[...] = (middle + dot(inner_ref[...], wdown_ref[...])).astype(BF16)


def middle_part(me, slots, tokens, cotangent, w_out, norm_two, w_in, w_down):
    parts, span = len(slots), tokens.shape[0]
    vmem = pl.BlockSpec(memory_space=pltpu.VMEM)
    like = lambda shape, kind=BF16: jax.ShapeDtypeStruct(shape, kind)
    out_shape = [
        like((D, span)),
        like((span, D)),
        like((span, 2 * FF)),
        like((span, FF)),
        like((span, D)),
        like((span, D), F32),
        like((span, D)),
    ] + [like(slots[0].shape)] * parts
    return pl.pallas_call(
        functools.partial(middle_kernel, parts),
        in_specs=[pl.BlockSpec(memory_space=pltpu.SMEM)] + [vmem] * (parts + 6),
        out_specs=[vmem] * len(out_shape),
        out_shape=out_shape,
        scratch_shapes=[pltpu.VMEM((D, span), BF16)],
        compiler_params=pltpu.CompilerParams(vmem_limit_bytes=18 << 20),
        cost_estimate=cost(2 * span * D * (2 * D + 5 * FF + 2 * FF), 20 << 20),
        name="middle_part",
    )(me, *slots, tokens, cotangent, w_out, norm_two[None, :], w_in, w_down)


def early_grad_kernel(at_ref, n2_ref, gu_ref, inner_ref, cot_ref, ctx_ref, mid_ref, keep_ref, give_ref):
    pieces = keep_ref.shape[0]
    rows = D // (2 * pieces)
    low = at_ref[0] == 0

    def put(first, second, count, at):
        kept = jnp.where(low, first, second).astype(BF16)
        given = jnp.where(low, second, first).astype(BF16)
        for p in range(pieces):
            here = slice(p * count, (p + 1) * count)
            place = at_ref[1 + p]
            keep_ref[place, at : at + count, :] = kept[here]
            give_ref[place, at : at + count, :] = given[here]

    n2_t = n2_ref[...].astype(F32).T.astype(BF16)
    for u in range(2 * FF // LANES):
        block = dot(n2_t, gu_ref[:, u * LANES : (u + 1) * LANES])
        put(block[: D // 2], block[D // 2 :], rows, u * rows)
    inner_t = inner_ref[...].astype(F32).T.astype(BF16)
    down = dot(inner_t, cot_ref[...])
    put(down[:, :LANES], down[:, LANES:], 3 * rows, 6 * rows)
    for u in range(2):
        block = dot(ctx_ref[...], mid_ref[:, u * LANES : (u + 1) * LANES])
        put(block[: D // 2], block[D // 2 :], rows, (9 + u) * rows)


def early_places(me, parts, near):
    half = near // 2
    first = [(k, q) for k in (1, 3) for q in range(half)]
    second = [(k, q) for k in (2, 3) for q in range(half, near)]
    kept = [(k, q) for k in (0, 2) for q in range(half)]
    kept += [(k, q) for k in (0, 1) for q in range(half, near)]
    order = {slot: i for i, slot in enumerate(first + second + kept)}
    table = jnp.array([order[k, q] for k in range(parts) for q in range(near)], jnp.int32)
    piece = jnp.arange(parts * near, dtype=jnp.int32)
    return jnp.concatenate([me[2:], table[piece ^ (me[0] * near + me[1])]])


def early_grads(me, n2, gate_up, inner, cotangent, context_t, mid, parts, near):
    rows = D // (2 * parts * near)
    shape = jax.ShapeDtypeStruct((parts * near, 11 * rows, LANES), BF16)
    operands = (n2, gate_up, inner, cotangent, context_t, mid)
    once = lambda a: pl.BlockSpec(a.shape, lambda i, at: (0,) * len(a.shape))
    return pl.pallas_call(
        early_grad_kernel,
        grid_spec=pltpu.PrefetchScalarGridSpec(
            num_scalar_prefetch=1,
            grid=(1,),
            in_specs=[once(a) for a in operands],
            out_specs=[once(shape), once(shape)],
        ),
        out_shape=[shape, shape],
        compiler_params=pltpu.CompilerParams(vmem_limit_bytes=28 << 20),
        cost_estimate=cost(2 * n2.shape[0] * 4224 * D, 14 << 20),
        name="early_grads",
    )(early_places(me, parts, near), *operands)


def late_grad_kernel(pieces, me_ref, *refs):
    grads = refs[:pieces]
    hn_ref, keep_ref, give_ref = refs[pieces:]
    parts = hn_ref.shape[0]
    near = keep_ref.shape[0]
    low = me_ref[2] == 0
    for j, ref in enumerate(grads):
        block = None
        for s in range(parts):
            term = dot(ref[s], hn_ref[s])
            block = term if block is None else block + term
        for part in range(3):
            head = block[part * HEAD_DIM : (part + 1) * HEAD_DIM]
            first, second = head[:HALF], head[HALF:]
            kept = jnp.where(low, first, second).astype(BF16)
            given = jnp.where(low, second, first).astype(BF16)
            for r in range(near):
                slot = me_ref[1] ^ r
                keep_ref[slot, 3 * j + part] = kept[8 * r : 8 * r + 8]
                give_ref[slot, 3 * j + part] = given[8 * r : 8 * r + 8]


def late_grads(me, grads, hn_row, near):
    pieces = len(grads)
    shape = jax.ShapeDtypeStruct((near, 3 * pieces, 8, D), BF16)
    vmem = pl.BlockSpec(memory_space=pltpu.VMEM)
    return pl.pallas_call(
        functools.partial(late_grad_kernel, pieces),
        in_specs=[pl.BlockSpec(memory_space=pltpu.SMEM)] + [vmem] * (pieces + 1),
        out_specs=[vmem, vmem],
        out_shape=[shape, shape],
        compiler_params=pltpu.CompilerParams(vmem_limit_bytes=12 << 20),
        cost_estimate=cost(2 * 2048 * 576 * D, 6 << 20),
        name="late_grads",
    )(me, *grads, hn_row)


def fold_lanes(wide):
    total = wide[:, :128]
    for i in range(1, wide.shape[1] // 128):
        total += wide[:, 128 * i : 128 * (i + 1)]
    return total


def early_kernel(
    me_ref, mine_ref, other_ref, w_ref, norm_ref, win_ref, wdown_ref, wout_ref, gain_ref, part_s
):
    near = mine_ref.shape[1]
    step = pl.program_id(0)
    steps = pl.num_programs(0)
    parts = steps // 2
    rows = D // (steps * near)

    def run(ref):
        for r in range(near):
            piece = ref[0, me_ref[1] ^ r].astype(F32)
            here = slice(r * rows, (r + 1) * rows)
            wide = jnp.concatenate([piece[rows * u : rows * (u + 1)] for u in range(6)], axis=1)
            win_ref[here, :] = wide
            at = pl.multiple_of((step * near + r) * rows, rows)
            part_s[pl.ds(at, rows), :] = fold_lanes(wide * w_ref[here, :].astype(F32))
            wdown_ref[3 * r * rows : 3 * (r + 1) * rows, :] = piece[6 * rows : 9 * rows]
            wout_ref[here, :LANES] = piece[9 * rows : 10 * rows]
            wout_ref[here, LANES:] = piece[10 * rows :]

    ours = (step // parts) == me_ref[2]
    pl.when(ours)(lambda: run(mine_ref))
    pl.when(jnp.logical_not(ours))(lambda: run(other_ref))

    @pl.when(step == steps - 1)
    def _():
        gain_ref[...] = jnp.sum(part_s[...].T, axis=0, keepdims=True) / norm_ref[...]


def assemble_early(me, mine, other, w_in, norm_two):
    parts, near = mine.shape[:2]
    steps = 2 * parts
    rows = D // steps

    def slot(own):
        def index(p, me):
            used = (p // parts == me[2]) == own
            return (jnp.where(used, me[0] ^ (p % parts), 0), 0, 0, 0)

        return pl.BlockSpec((1,) + mine.shape[1:], index)

    return pl.pallas_call(
        early_kernel,
        grid_spec=pltpu.PrefetchScalarGridSpec(
            num_scalar_prefetch=1,
            grid=(steps,),
            in_specs=[
                slot(True),
                slot(False),
                pl.BlockSpec((rows, 2 * FF), lambda p, me: (p, 0)),
                pl.BlockSpec((1, D), lambda p, me: (0, 0)),
            ],
            out_specs=[
                pl.BlockSpec((rows, 2 * FF), lambda p, me: (p, 0)),
                pl.BlockSpec((3 * rows, LANES), lambda p, me: (p % parts, p // parts)),
                pl.BlockSpec((rows, D), lambda p, me: (p, 0)),
                pl.BlockSpec((1, D), lambda p, me: (0, 0)),
            ],
            scratch_shapes=[pltpu.VMEM((D, 128), F32)],
        ),
        out_shape=[
            jax.ShapeDtypeStruct((D, 2 * FF), F32),
            jax.ShapeDtypeStruct((FF, D), F32),
            jax.ShapeDtypeStruct((D, D), F32),
            jax.ShapeDtypeStruct((1, D), F32),
        ],
        compiler_params=pltpu.CompilerParams(vmem_limit_bytes=12 << 20),
        cost_estimate=cost(1 << 20, 24 << 20),
        name="assemble_early",
    )(me, mine, other, w_in, norm_two[None, :])


def late_kernel(me_ref, *refs):
    mine, other = refs[:5], refs[5:10]
    w_ref, norm_ref, out_ref, gain_ref, rows_s = refs[10:]
    near = mine[0].shape[0]
    pieces = mine[0].shape[1] // 3
    width = rows_s.shape[1]
    lanes = pl.ds(pl.multiple_of(pl.program_id(0) * 128, 128), 128)
    total = None
    for block in range(3 * pieces):
        row = (block % pieces) * 3 + block // pieces
        for k in range(4):
            for q in range(near):
                which = k if k < 3 else 3 + q // (near // 2)
                place = q if k < 3 else q % (near // 2)
                at = (me_ref[0] ^ k) * HEAD_DIM + (me_ref[1] ^ q) * 8
                for ref, core in ((mine, me_ref[2]), (other, 1 - me_ref[2])):
                    here = pl.ds(pl.multiple_of(at + core * HALF, 8), 8)
                    rows_s[block, here, :] = ref[which][place, row, :, lanes].astype(F32)
        wide = rows_s[block].T
        cols = slice(block * width, (block + 1) * width)
        out_ref[:, cols] = wide
        part = fold_lanes(wide * w_ref[:, cols].astype(F32))
        total = part if total is None else total + part
    gain_ref[...] = jnp.sum(total.T, axis=0, keepdims=True) / norm_ref[...]


def assemble_late(me, mine, other, w_qkv, norm_one):
    blocks = mine[0].shape[1]
    sums = [pl.BlockSpec(v.shape, lambda b, me: (0, 0, 0, 0)) for v in mine]
    return pl.pallas_call(
        late_kernel,
        grid_spec=pltpu.PrefetchScalarGridSpec(
            num_scalar_prefetch=1,
            grid=(D // 128,),
            in_specs=sums
            + sums
            + [
                pl.BlockSpec((128, 3 * D), lambda b, me: (b, 0)),
                pl.BlockSpec((1, 128), lambda b, me: (0, b)),
            ],
            out_specs=[
                pl.BlockSpec((128, 3 * D), lambda b, me: (b, 0)),
                pl.BlockSpec((1, 128), lambda b, me: (0, b)),
            ],
            scratch_shapes=[pltpu.VMEM((blocks, 3 * D // blocks, 128), F32)],
        ),
        out_shape=[
            jax.ShapeDtypeStruct((D, 3 * D), F32),
            jax.ShapeDtypeStruct((1, D), F32),
        ],
        compiler_params=pltpu.CompilerParams(vmem_limit_bytes=60 << 20),
        cost_estimate=cost(1 << 20, 14 << 20),
        name="assemble_late",
    )(me, *mine, *other, w_qkv, norm_one[None, :])


def input_grad_kernel(parts, pieces, me_ref, *refs):
    pair, last = refs[:parts], refs[parts : 2 * parts]
    w_ref, tok_ref, norm_ref, mid_ref, out_ref, proj_s = refs[2 * parts :]
    span = proj_s.shape[1]
    for k in range(parts):
        group = me_ref[0] ^ k
        for j in range(pieces):
            if j < pieces - 1:
                piece = pair[k][...].reshape(pieces - 1, WIDE, span)[j]
            else:
                piece = last[k][...].reshape(WIDE, span)
            for part in range(3):
                at = part * D + (j * parts + group) * HEAD_DIM
                proj_s[pl.ds(pl.multiple_of(at, HEAD_DIM), HEAD_DIM), :] = piece[
                    part * HEAD_DIM : (part + 1) * HEAD_DIM
                ]
    upstream = dot(w_ref[...], proj_s[...]).T * norm_ref[...]
    values = tok_ref[...].astype(F32)
    centered = values - jnp.mean(values, axis=-1, keepdims=True)
    scale = lax.rsqrt(jnp.mean(centered * centered, axis=-1, keepdims=True) + EPSILON)
    unit = centered * scale
    flat = jnp.mean(upstream, axis=-1, keepdims=True)
    along = jnp.mean(upstream * unit, axis=-1, keepdims=True)
    out_ref[...] = mid_ref[...] + (upstream - flat - unit * along) * scale


def input_grad(me, pair, last, w_qkv, tokens, norm_one, grad_middle):
    parts = len(pair)
    span = tokens.shape[0]
    vmem = pl.BlockSpec(memory_space=pltpu.VMEM)
    return pl.pallas_call(
        functools.partial(input_grad_kernel, parts, 3),
        in_specs=[pl.BlockSpec(memory_space=pltpu.SMEM)] + [vmem] * (2 * parts + 4),
        out_specs=vmem,
        out_shape=jax.ShapeDtypeStruct((span, D), F32),
        scratch_shapes=[pltpu.VMEM((3 * D, span), BF16)],
        compiler_params=pltpu.CompilerParams(vmem_limit_bytes=20 << 20),
        cost_estimate=cost(2 * span * 3 * D * D, 10 << 20),
        name="input_grad",
    )(me, *pair, *last, w_qkv, tokens, norm_one[None, :], grad_middle)


def swap(values, axis, k):
    size = lax.axis_size(axis)
    return lax.ppermute(values, axis, [(i, i ^ k) for i in range(size)])


def add(*terms):
    total = terms[0].astype(F32)
    for term in terms[1:]:
        total += term.astype(F32)
    return total.astype(BF16)


def scatter_near(slots):
    return add(slots[0], *[swap(slots[k], "near", k) for k in range(1, len(slots))])


def gather_near(values):
    return jnp.stack([values] + [swap(values, "near", k) for k in range(1, lax.axis_size("near"))])


def tie(*values):
    return lax.optimization_barrier(values)


def on_device(tokens, doc_start, cotangent, norm_one, w_qkv, w_out, norm_two, w_in, w_down):
    parts = lax.axis_size("seq")
    near = lax.axis_size("near")
    far = lax.axis_size("far")
    span = tokens.shape[1]
    total = span * parts
    pieces = HEADS // parts
    bq = min(512, span)
    me_seq = lax.axis_index("seq").astype(jnp.int32)
    me = jnp.stack([lax.axis_index(a).astype(jnp.int32) for a in ("seq", "near", "core")])
    first_token = me_seq * span
    starts = doc_start[0]
    docs = doc_start

    frequency = ROTARY_BASE ** (-(jnp.arange(HALF, dtype=F32) * 2.0 / HEAD_DIM))
    offset = (jnp.arange(total, dtype=jnp.int32) - starts).astype(F32)
    angles = frequency[:, None] * offset[None, :]
    cosine, sine = jnp.cos(angles), jnp.sin(angles)
    own_cosine = lax.dynamic_slice_in_dim(cosine, first_token, span, axis=1)
    own_sine = lax.dynamic_slice_in_dim(sine, first_token, span, axis=1)

    def sum_far(values):
        return lax.psum(values, "far") if far > 1 else values

    hn = first_norm(tokens[0], norm_one)
    qkv = []
    for j in range(pieces):
        sent = project(me, hn, w_qkv, own_cosine, own_sine, j, parts)
        qkv.append([sent] + [swap(sent[k], "seq", k) for k in range(1, parts)])
    contexts, lses = [], []
    for j in range(pieces):
        if j == pieces - 1:
            hn_late, qkv[j] = tie(hn, qkv[j])
            hn_near = [swap(hn_late, "seq", 1), swap(hn_late, "seq", 2)]
        context, lse = attend_forward(me, qkv[j], docs, bq)
        contexts.append(context)
        lses.append(lse)
    arrived = [jnp.stack([c[k] for c in contexts]) for k in range(parts)]
    arrived[1:] = [swap(arrived[k], "seq", k) for k in range(1, parts)]
    arrived, hn_near = tie(arrived, hn_near)
    hn_far = [swap(hn_near[1][: span // 2], "seq", 1), swap(hn_near[0][span // 2 :], "seq", 2)]
    outs = middle_part(me, arrived, tokens[0], cotangent[0], w_out, norm_two, w_in, w_down)
    outs, hn_far = tie(outs, hn_far)
    context_t, normed_two, grad_gate_up, inner, grad_mid_low, grad_middle, result = outs[:7]
    hn_row = jnp.stack([hn, hn_near[0], hn_near[1], jnp.concatenate(hn_far)])
    upstream = [outs[7]] + [swap(outs[7 + k], "seq", k) for k in range(1, parts)]
    keep, give = early_grads(
        me, normed_two, grad_gate_up, inner, cotangent[0], context_t, grad_mid_low, parts, near
    )
    taken = swap(give, "core", 1)
    half = near // 2
    at = [2 * half, 4 * half, 5 * half, 6 * half, 7 * half, 8 * half]
    send_one = add(keep[: at[0]], taken[: at[0]])
    send_two = add(keep[at[0] : at[1]], taken[at[0] : at[1]])
    early = add(keep[at[1] :], taken[at[1] :])
    a_own, a_two, b_own, b_one = (early[i * half : (i + 1) * half] for i in range(4))
    send_one, send_two, early, upstream[1] = tie(send_one, send_two, early, upstream[1])

    def backward(j, upstream):
        return attend_backward(
            me, qkv[j], docs, upstream, j, contexts[j], lses[j], cosine, sine, bq,
            True,
        )

    from_one, from_two = swap(send_one, "seq", 1), swap(send_two, "seq", 2)
    grads = [backward(0, upstream)]
    grads[0], upstream, from_one, from_two = tie(grads[0], upstream, from_one, from_two)
    by_two = swap(add(a_two, from_one[half:]), "seq", 2)
    by_one = swap(add(b_one, from_two[half:]), "seq", 1)
    grads.append(backward(1, upstream))
    grads, upstream, by_two, by_one = tie(grads, upstream, by_two, by_one)
    kept, given = late_grads(me, grads, hn_row, near)
    own = jnp.stack(grads, axis=1)
    pair = [own[0]] + [swap(own[k], "seq", k) for k in range(1, parts)]
    early = [add(a_own[i], from_one[i], by_two[i]) for i in range(half)]
    early += [add(b_own[i], from_two[i], by_one[i]) for i in range(half)]
    early = scatter_near(early)
    grads.append(backward(2, upstream))

    grads, early, pair[1], pair[2] = tie(grads, early, pair[1], pair[2])
    early = sum_far(early)
    slots = [early] + [swap(early, "near", k) for k in range(1, near)]
    last = [grads[2][0]] + [swap(grads[2][k], "seq", k) for k in range(1, parts)]
    last, slots, grads[2], pair, kept, given = tie(last, slots, grads[2], pair, kept, given)
    early = jnp.stack(slots)
    one, two = swap(early, "seq", 1), swap(early, "seq", 2)
    kept_last, given_last = late_grads(me, grads[2:], hn_row, near)
    kept = jnp.concatenate([kept, kept_last], axis=1)
    given = jnp.concatenate([given, given_last], axis=1)
    late = add(kept, swap(given, "core", 1))
    late = sum_far(scatter_near(late))
    grad_input = input_grad(me, pair, last, w_qkv, tokens[0], norm_one, grad_middle)
    one, two, late, grad_input = tie(one, two, late, grad_input)
    far_one, far_two = swap(two[: near // 2], "seq", 1), swap(one[near // 2 :], "seq", 2)
    late = gather_near(late)
    far_one, far_two, late = tie(far_one, far_two, late)
    early = jnp.stack([early, one, two, jnp.concatenate([far_one, far_two])])
    early_other = swap(early, "core", 1)
    one, two = swap(late, "seq", 1), swap(late, "seq", 2)
    one, two, early_other = tie(one, two, early_other)
    far = [swap(two[: near // 2], "seq", 1), swap(one[near // 2 :], "seq", 2)]
    mine = [late, one, two]
    other = [swap(v, "core", 1) for v in mine]
    sum_w_in, sum_w_down, sum_w_out, sum_norm_two = assemble_early(
        me, early, early_other, w_in, norm_two
    )
    sum_w_in, far, other = tie(sum_w_in, far, other)
    mine += far
    other += [swap(v, "core", 1) for v in far]
    sum_w_qkv, sum_norm_one = assemble_late(me, mine, other, w_qkv, norm_one)
    return (
        result[None],
        grad_input[None],
        sum_norm_one[0],
        sum_w_qkv,
        sum_w_out,
        sum_norm_two[0],
        sum_w_in,
        sum_w_down,
    )


def solution(mesh):
    parts = mesh.shape["seq"]
    near = min(4, mesh.shape["dp"] // 2)
    split = Mesh(mesh.devices.reshape(parts, -1, near, 2), ("seq", "far", "near", "core"))
    rows = ("far", "near", "core")
    tokens_at = P(rows, "seq", None)
    return jax.shard_map(
        on_device,
        mesh=split,
        in_specs=(tokens_at, P(rows, None), tokens_at, P(), P(), P(), P(), P(), P()),
        out_specs=(tokens_at, tokens_at, P(), P(), P(), P(), P(), P()),
        check_vma=False,
    )
```

```python
import functools

import jax
import jax.numpy as jnp
from jax import lax
from jax.experimental import pallas as pl
from jax.experimental.pallas import tpu as pltpu
from jax.sharding import Mesh
from jax.sharding import PartitionSpec as P

D = 768
HEADS = 12
HEAD_DIM = 64
HALF = HEAD_DIM // 2
FF = 1152
WIDE = 3 * HEAD_DIM
LANES = D // 2

EPSILON = 1e-05
ROTARY_BASE = 160000.0
SCORE_SCALE = 0.125
SCORE_EXP2 = SCORE_SCALE * 1.4426950408889634
MASKED_SCORE = -1e30
KEY_CHUNK = 256
F32 = jnp.float32
BF16 = jnp.bfloat16

dot = functools.partial(jnp.dot, preferred_element_type=F32)


def cost(flops, moved, transcendentals=0):
    return pl.CostEstimate(
        flops=flops, bytes_accessed=moved, transcendentals=0
    )


def norm_kernel(tok_ref, norm_ref, out_ref):
    values = tok_ref[...].astype(F32)
    centered = values - jnp.mean(values, axis=-1, keepdims=True)
    variance = jnp.mean(centered * centered, axis=-1, keepdims=True)
    out_ref[...] = (centered * lax.rsqrt(variance + EPSILON) * norm_ref[...]).astype(BF16)


def first_norm(tokens, norm_one):
    rows = tokens.shape[0] // 2
    return pl.pallas_call(
        norm_kernel,
        grid=(2,),
        in_specs=[
            pl.BlockSpec((rows, D), lambda i: (i, 0)),
            pl.BlockSpec((1, D), lambda i: (0, 0)),
        ],
        out_specs=pl.BlockSpec((rows, D), lambda i: (i, 0)),
        out_shape=jax.ShapeDtypeStruct(tokens.shape, BF16),
        compiler_params=pltpu.CompilerParams(vmem_limit_bytes=6 << 20),
        cost_estimate=cost(1 << 20, 2 << 20),
        name="first_norm",
    )(tokens, norm_one[None, :])


def project_kernel(me_ref, hn_ref, w_ref, cos_ref, sin_ref, out_ref):
    part = pl.program_id(0)
    turned = dot(hn_ref[...], w_ref[...]).T
    cosine = jnp.where(part < 2, cos_ref[...], 1.0)
    sine = jnp.where(part < 2, sin_ref[...], 0.0)
    row = pl.multiple_of(part * HEAD_DIM, HEAD_DIM)
    for g in range(out_ref.shape[0]):
        slot = me_ref[0] ^ g
        first = turned[g * HEAD_DIM : g * HEAD_DIM + HALF]
        second = turned[g * HEAD_DIM + HALF : (g + 1) * HEAD_DIM]
        out_ref[slot, pl.ds(row, HALF), :] = (first * cosine - second * sine).astype(BF16)
        out_ref[slot, pl.ds(row + HALF, HALF), :] = (second * cosine + first * sine).astype(BF16)


def project(me, hn, w_qkv, cosine, sine, piece, groups):
    tokens = hn.shape[0]
    width = groups * HEAD_DIM
    pieces = D // width
    return pl.pallas_call(
        project_kernel,
        grid_spec=pltpu.PrefetchScalarGridSpec(
            num_scalar_prefetch=1,
            grid=(3,),
            in_specs=[
                pl.BlockSpec((tokens, D), lambda i, me: (0, 0)),
                pl.BlockSpec((D, width), lambda i, me: (0, i * pieces + piece)),
                pl.BlockSpec((HALF, tokens), lambda i, me: (0, 0)),
                pl.BlockSpec((HALF, tokens), lambda i, me: (0, 0)),
            ],
            out_specs=pl.BlockSpec((groups, WIDE, tokens), lambda i, me: (0, 0, 0)),
        ),
        out_shape=jax.ShapeDtypeStruct((groups, WIDE, tokens), BF16),
        compiler_params=pltpu.CompilerParams(vmem_limit_bytes=32 << 20),
        cost_estimate=cost(6 * tokens * D * width, 4 << 20),
        name="project",
    )(me, hn, w_qkv, cosine, sine)


def mask_scores(scores, chunk, chunks, edge, key_doc, query_doc, query_main):
    if chunk == 0 or chunk == chunks - 1:
        own = key_doc[: KEY_CHUNK, :] if chunk == 0 else key_doc[KEY_CHUNK :, :]
        return jnp.where(own == query_doc, scores, MASKED_SCORE)
    if edge:
        return jnp.where(query_main, scores, MASKED_SCORE)
    return scores


def put_edges(doc_ref, edge_s):
    total = doc_ref.shape[1]
    for i, at in enumerate((0, total - KEY_CHUNK)):
        tall = jnp.broadcast_to(doc_ref[:, at : at + KEY_CHUNK], (8, KEY_CHUNK)).T
        edge_s[i * KEY_CHUNK : (i + 1) * KEY_CHUNK, :] = tall[:, :1]


def put_in_order(me, slots, qkv_s, key_s, value_s=None):
    span = qkv_s.shape[2]
    for k, ref in enumerate(slots):
        at = me ^ k
        piece = ref[...].reshape(WIDE, span)
        qkv_s[at] = piece
        rows = pl.ds(pl.multiple_of(at * span, span), span)
        key_s[rows, :] = piece[HEAD_DIM : 2 * HEAD_DIM].astype(F32).T.astype(BF16)
        if value_s is not None:
            value_s[rows, :] = piece[2 * HEAD_DIM :].astype(F32).T.astype(BF16)


def slot_specs(slots):
    own = pl.BlockSpec((1,) + slots[0].shape[1:], lambda i, me: (0, 0, 0))
    rest = [pl.BlockSpec(s.shape, lambda i, me: (0, 0)) for s in slots[1:]]
    return [own] + rest


def forward_kernel(bq, parts, me_ref, *refs):
    slots = refs[:parts]
    doc_ref, out_ref, lse_ref, qkv_s, key_s, edge_s, score_s = refs[parts:]
    step = pl.program_id(0)
    steps = pl.num_programs(0)
    total = key_s.shape[0]
    chunks = total // KEY_CHUNK
    span = qkv_s.shape[2]
    ratio = span // bq

    @pl.when(step == 0)
    def _():
        put_in_order(me_ref[0], slots, qkv_s, key_s)
        put_edges(doc_ref, edge_s)

    def run(edge):
        lanes = pl.ds(pl.multiple_of((step % ratio) * bq, bq), bq)
        queries = qkv_s[step // ratio, 0:HEAD_DIM, lanes]
        query_doc = doc_ref[:, pl.ds(pl.multiple_of(step * bq, bq), bq)]
        query_main = query_doc == doc_ref[:, total // 2 : total // 2 + 1]
        top = None
        for c in range(chunks):
            rows = slice(c * KEY_CHUNK, (c + 1) * KEY_CHUNK)
            scores = dot(key_s[rows, :], queries)
            scores = mask_scores(scores, c, chunks, edge, edge_s, query_doc, query_main)
            score_s[rows, :] = scores
            peak = jnp.max(scores.reshape(KEY_CHUNK // 8, 8, bq), axis=0)
            top = peak if top is None else jnp.maximum(top, peak)
        top = jnp.max(top, axis=0, keepdims=True) * SCORE_EXP2
        mass, acc = None, None
        for c in range(chunks):
            rows = slice(c * KEY_CHUNK, (c + 1) * KEY_CHUNK)
            weight = jnp.exp2(score_s[rows, :] * SCORE_EXP2 - top)
            part = jnp.sum(weight.reshape(KEY_CHUNK // 8, 8, bq), axis=0)
            mass = part if mass is None else mass + part
            at = c * KEY_CHUNK % span
            values = qkv_s[c * KEY_CHUNK // span, 2 * HEAD_DIM :, at : at + KEY_CHUNK]
            term = dot(values, weight.astype(BF16))
            acc = term if acc is None else acc + term
        mass = jnp.sum(mass, axis=0, keepdims=True)
        out_ref[0] = (acc / mass).astype(BF16)
        lse_ref[...] = top + jnp.log2(mass)

    at_edge = (step == 0) | (step == steps - 1)
    pl.when(at_edge)(lambda: run(True))
    pl.when(jnp.logical_not(at_edge))(lambda: run(False))


def attend_forward(me, slots, docs, bq):
    parts, _, span = slots[0].shape
    total = parts * span
    ratio = span // bq
    return pl.pallas_call(
        functools.partial(forward_kernel, bq, parts),
        grid_spec=pltpu.PrefetchScalarGridSpec(
            num_scalar_prefetch=1,
            grid=(total // bq,),
            in_specs=slot_specs(slots)
            + [
                pl.BlockSpec((1, total), lambda i, me: (0, 0)),
            ],
            out_specs=[
                pl.BlockSpec((1, HEAD_DIM, bq), lambda i, me: (i // ratio ^ me[0], 0, i % ratio)),
                pl.BlockSpec((1, bq), lambda i, me: (0, i)),
            ],
            scratch_shapes=[
                pltpu.VMEM((parts, WIDE, span), BF16),
                pltpu.VMEM((total, HEAD_DIM), BF16),
                pltpu.VMEM((2 * KEY_CHUNK, 1), jnp.int32),
                pltpu.VMEM((total, bq), F32),
            ],
        ),
        out_shape=[
            jax.ShapeDtypeStruct((parts, HEAD_DIM, span), BF16),
            jax.ShapeDtypeStruct((1, total), F32),
        ],
        compiler_params=pltpu.CompilerParams(vmem_limit_bytes=40 << 20),
        cost_estimate=cost(16 * HEAD_DIM * total * total, 4 << 20, total * total),
        name="attend_forward",
    )(me, *slots, docs)


def backward_kernel(bq, parts, turn, me_ref, *refs):
    slots, ups = refs[:parts], refs[parts : 2 * parts]
    (doc_ref, o_ref, lse_ref, cos_ref, sin_ref, grad_ref,
     qkv_s, key_s, value_s, up_s, edge_s, dk_s, dv_s) = refs[2 * parts :]
    step = pl.program_id(0)
    steps = pl.num_programs(0)
    total = key_s.shape[0]
    chunks = total // KEY_CHUNK
    span = qkv_s.shape[2]
    ratio = span // bq

    @pl.when(step == 0)
    def _():
        put_in_order(me_ref[0], slots, qkv_s, key_s, value_s)
        put_edges(doc_ref, edge_s)
        for k, ref in enumerate(ups):
            up_s[me_ref[0] ^ k] = ref[...].reshape(HEAD_DIM, span)
        dk_s[...] = jnp.zeros_like(dk_s)
        dv_s[...] = jnp.zeros_like(dv_s)

    def turn_back(grad, cosine, sine):
        first, second = grad[:HALF], grad[HALF:]
        return first * cosine + second * sine, second * cosine - first * sine

    def run(edge):
        lanes = pl.ds(pl.multiple_of((step % ratio) * bq, bq), bq)
        here = pl.ds(pl.multiple_of(step * bq, bq), bq)
        queries = qkv_s[step // ratio, 0:HEAD_DIM, lanes]
        upstream = up_s[step // ratio, :, lanes]
        wide_up = upstream.astype(F32)
        centre = jnp.sum(wide_up * o_ref[0].astype(F32), axis=0, keepdims=True)
        query_rows = queries.astype(F32).T.astype(BF16)
        up_rows = wide_up.T.astype(BF16)
        query_doc = doc_ref[:, pl.ds(pl.multiple_of(step * bq, bq), bq)]
        query_main = query_doc == doc_ref[:, total // 2 : total // 2 + 1]
        lse = lse_ref[...]
        dq = None
        for c in range(chunks):
            rows = slice(c * KEY_CHUNK, (c + 1) * KEY_CHUNK)
            scores = dot(key_s[rows, :], queries)
            scores = mask_scores(scores, c, chunks, edge, edge_s, query_doc, query_main)
            probs = jnp.exp2(scores * SCORE_EXP2 - lse)
            grad_prob = dot(value_s[rows, :], upstream)
            grad_scores = (probs * (grad_prob - centre)).astype(BF16)
            dv_s[rows, :] += dot(probs.astype(BF16), up_rows)
            dk_s[rows, :] += dot(grad_scores, query_rows)
            at = c * KEY_CHUNK % span
            keys = qkv_s[c * KEY_CHUNK // span, HEAD_DIM : 2 * HEAD_DIM, at : at + KEY_CHUNK]
            term = dot(keys, grad_scores)
            dq = term if dq is None else dq + term
        one, two = turn_back(dq * SCORE_SCALE, cos_ref[:, here], sin_ref[:, here])
        slot = (me_ref[0] if turn else 0) ^ (step // ratio)
        grad_ref[slot, 0:HALF, lanes] = one.astype(BF16)
        grad_ref[slot, HALF:HEAD_DIM, lanes] = two.astype(BF16)

    at_edge = (step == 0) | (step == steps - 1)
    pl.when(at_edge)(lambda: run(True))
    pl.when(jnp.logical_not(at_edge))(lambda: run(False))

    @pl.when(step == steps - 1)
    def _():
        for s in range(parts):
            slot = (me_ref[0] if turn else 0) ^ s
            rows = slice(s * span, (s + 1) * span)
            one, two = turn_back(dk_s[rows, :].T * SCORE_SCALE, cos_ref[:, rows], sin_ref[:, rows])
            grad_ref[slot, HEAD_DIM : HEAD_DIM + HALF, :] = one.astype(BF16)
            grad_ref[slot, HEAD_DIM + HALF : 2 * HEAD_DIM, :] = two.astype(BF16)
            grad_ref[slot, 2 * HEAD_DIM :, :] = dv_s[rows, :].T.astype(BF16)


def attend_backward(
    me, slots, docs, upstream, piece, context, lse, cosine, sine, bq, turn
):
    parts, _, span = slots[0].shape
    total = parts * span
    ratio = span // bq
    return pl.pallas_call(
        functools.partial(backward_kernel, bq, parts, turn),
        grid_spec=pltpu.PrefetchScalarGridSpec(
            num_scalar_prefetch=1,
            grid=(total // bq,),
            in_specs=slot_specs(slots)
            + [pl.BlockSpec((1, HEAD_DIM, span), lambda i, me: (piece, 0, 0))] * parts
            + [
                pl.BlockSpec((1, total), lambda i, me: (0, 0)),
                pl.BlockSpec((1, HEAD_DIM, bq), lambda i, me: (i // ratio ^ me[0], 0, i % ratio)),
                pl.BlockSpec((1, bq), lambda i, me: (0, i)),
                pl.BlockSpec((HALF, total), lambda i, me: (0, 0)),
                pl.BlockSpec((HALF, total), lambda i, me: (0, 0)),
            ],
            out_specs=pl.BlockSpec((parts, WIDE, span), lambda i, me: (0, 0, 0)),
            scratch_shapes=[
                pltpu.VMEM((parts, WIDE, span), BF16),
                pltpu.VMEM((total, HEAD_DIM), BF16),
                pltpu.VMEM((total, HEAD_DIM), BF16),
                pltpu.VMEM((parts, HEAD_DIM, span), BF16),
                pltpu.VMEM((2 * KEY_CHUNK, 1), jnp.int32),
                pltpu.VMEM((total, HEAD_DIM), F32),
                pltpu.VMEM((total, HEAD_DIM), F32),
            ],
        ),
        out_shape=jax.ShapeDtypeStruct((parts, WIDE, span), BF16),
        compiler_params=pltpu.CompilerParams(vmem_limit_bytes=40 << 20),
        cost_estimate=cost(40 * HEAD_DIM * total * total, 6 << 20, total * total),
        name="attend_backward",
    )(me, *slots, *upstream, docs, context, lse, cosine, sine)


def dot_rows(a, b):
    return lax.dot_general(a, b, (((1,), (1,)), ((), ())), preferred_element_type=F32)


def middle_kernel(parts, me_ref, *refs):
    slots = refs[:parts]
    (tok_ref, cot_ref, wout_ref, norm_ref, win_ref, wdown_ref,
     ctx_ref, n2_ref, gu_ref, inner_ref, low_ref, mid_ref, result_ref) = refs[parts : parts + 13]
    outs, down_s = refs[parts + 13 : -1], refs[-1]
    pieces = slots[0].shape[0]

    def rows_of(j, k):
        at = (j * parts + (me_ref[0] ^ k)) * HEAD_DIM
        return pl.ds(pl.multiple_of(at, HEAD_DIM), HEAD_DIM)

    for k, ref in enumerate(slots):
        for j in range(pieces):
            ctx_ref[rows_of(j, k), :] = ref[j]
    context = ctx_ref[...].astype(F32).T.astype(BF16)
    middle = tok_ref[...].astype(F32) + dot(context, wout_ref[...])
    centered = middle - jnp.mean(middle, axis=-1, keepdims=True)
    scale = lax.rsqrt(jnp.mean(centered * centered, axis=-1, keepdims=True) + EPSILON)
    unit = centered * scale
    normed = (unit * norm_ref[...]).astype(BF16)
    n2_ref[...] = normed
    cotangent = cot_ref[...]
    for c in range(FF // LANES):
        cols = slice(c * LANES, (c + 1) * LANES)
        high = slice(FF + c * LANES, FF + (c + 1) * LANES)
        gate = dot(normed, win_ref[:, cols])
        up = dot(normed, win_ref[:, high])
        grad_inner = dot_rows(cotangent, wdown_ref[cols, :])
        share = 0.5 + 0.5 * lax.erf(gate * 0.7071067811865476)
        slope = share + gate * (0.3989422804014327 * jnp.exp(-0.5 * gate * gate))
        gelu = gate * share
        inner_ref[:, cols] = (gelu * up).astype(BF16)
        gu_ref[:, cols] = (slope * up * grad_inner).astype(BF16)
        gu_ref[:, high] = (gelu * grad_inner).astype(BF16)
    upstream = dot_rows(gu_ref[...], win_ref[...]) * norm_ref[...]
    flat = jnp.mean(upstream, axis=-1, keepdims=True)
    along = jnp.mean(upstream * unit, axis=-1, keepdims=True)
    grad_middle = cotangent.astype(F32) + (upstream - flat - unit * along) * scale
    mid_ref[...] = grad_middle
    low = grad_middle.astype(BF16)
    low_ref[...] = low
    down_s[...] = dot_rows(wout_ref[...], low).astype(BF16)
    for k, ref in enumerate(outs):
        for j in range(pieces):
            ref[j] = down_s[rows_of(j, k), :]
    result_ref[...] = (middle + dot(inner_ref[...], wdown_ref[...])).astype(BF16)


def middle_part(me, slots, tokens, cotangent, w_out, norm_two, w_in, w_down):
    parts, span = len(slots), tokens.shape[0]
    vmem = pl.BlockSpec(memory_space=pltpu.VMEM)
    like = lambda shape, kind=BF16: jax.ShapeDtypeStruct(shape, kind)
    out_shape = [
        like((D, span)),
        like((span, D)),
        like((span, 2 * FF)),
        like((span, FF)),
        like((span, D)),
        like((span, D), F32),
        like((span, D)),
    ] + [like(slots[0].shape)] * parts
    return pl.pallas_call(
        functools.partial(middle_kernel, parts),
        in_specs=[pl.BlockSpec(memory_space=pltpu.SMEM)] + [vmem] * (parts + 6),
        out_specs=[vmem] * len(out_shape),
        out_shape=out_shape,
        scratch_shapes=[pltpu.VMEM((D, span), BF16)],
        compiler_params=pltpu.CompilerParams(vmem_limit_bytes=18 << 20),
        cost_estimate=cost(2 * span * D * (2 * D + 5 * FF + 2 * FF), 20 << 20),
        name="middle_part",
    )(me, *slots, tokens, cotangent, w_out, norm_two[None, :], w_in, w_down)


def early_grad_kernel(at_ref, n2_ref, gu_ref, inner_ref, cot_ref, ctx_ref, mid_ref, keep_ref, give_ref):
    pieces = keep_ref.shape[0]
    rows = D // (2 * pieces)
    low = at_ref[0] == 0

    def put(first, second, count, at):
        kept = jnp.where(low, first, second).astype(BF16)
        given = jnp.where(low, second, first).astype(BF16)
        for p in range(pieces):
            here = slice(p * count, (p + 1) * count)
            place = at_ref[1 + p]
            keep_ref[place, at : at + count, :] = kept[here]
            give_ref[place, at : at + count, :] = given[here]

    n2_t = n2_ref[...].astype(F32).T.astype(BF16)
    for u in range(2 * FF // LANES):
        block = dot(n2_t, gu_ref[:, u * LANES : (u + 1) * LANES])
        put(block[: D // 2], block[D // 2 :], rows, u * rows)
    inner_t = inner_ref[...].astype(F32).T.astype(BF16)
    down = dot(inner_t, cot_ref[...])
    put(down[:, :LANES], down[:, LANES:], 3 * rows, 6 * rows)
    for u in range(2):
        block = dot(ctx_ref[...], mid_ref[:, u * LANES : (u + 1) * LANES])
        put(block[: D // 2], block[D // 2 :], rows, (9 + u) * rows)


def early_places(me, parts, near):
    half = near // 2
    first = [(k, q) for k in (1, 3) for q in range(half)]
    second = [(k, q) for k in (2, 3) for q in range(half, near)]
    kept = [(k, q) for k in (0, 2) for q in range(half)]
    kept += [(k, q) for k in (0, 1) for q in range(half, near)]
    order = {slot: i for i, slot in enumerate(first + second + kept)}
    table = jnp.array([order[k, q] for k in range(parts) for q in range(near)], jnp.int32)
    piece = jnp.arange(parts * near, dtype=jnp.int32)
    return jnp.concatenate([me[2:], table[piece ^ (me[0] * near + me[1])]])


def early_grads(me, n2, gate_up, inner, cotangent, context_t, mid, parts, near):
    rows = D // (2 * parts * near)
    shape = jax.ShapeDtypeStruct((parts * near, 11 * rows, LANES), BF16)
    operands = (n2, gate_up, inner, cotangent, context_t, mid)
    once = lambda a: pl.BlockSpec(a.shape, lambda i, at: (0,) * len(a.shape))
    return pl.pallas_call(
        early_grad_kernel,
        grid_spec=pltpu.PrefetchScalarGridSpec(
            num_scalar_prefetch=1,
            grid=(1,),
            in_specs=[once(a) for a in operands],
            out_specs=[once(shape), once(shape)],
        ),
        out_shape=[shape, shape],
        compiler_params=pltpu.CompilerParams(vmem_limit_bytes=28 << 20),
        cost_estimate=cost(2 * n2.shape[0] * 4224 * D, 14 << 20),
        name="early_grads",
    )(early_places(me, parts, near), *operands)


def late_grad_kernel(pieces, me_ref, *refs):
    grads = refs[:pieces]
    hn_ref, keep_ref, give_ref = refs[pieces:]
    parts = hn_ref.shape[0]
    near = keep_ref.shape[0]
    low = me_ref[2] == 0
    for j, ref in enumerate(grads):
        block = None
        for s in range(parts):
            term = dot(ref[s], hn_ref[s])
            block = term if block is None else block + term
        for part in range(3):
            head = block[part * HEAD_DIM : (part + 1) * HEAD_DIM]
            first, second = head[:HALF], head[HALF:]
            kept = jnp.where(low, first, second).astype(BF16)
            given = jnp.where(low, second, first).astype(BF16)
            for r in range(near):
                slot = me_ref[1] ^ r
                keep_ref[slot, 3 * j + part] = kept[8 * r : 8 * r + 8]
                give_ref[slot, 3 * j + part] = given[8 * r : 8 * r + 8]


def late_grads(me, grads, hn_row, near):
    pieces = len(grads)
    shape = jax.ShapeDtypeStruct((near, 3 * pieces, 8, D), BF16)
    vmem = pl.BlockSpec(memory_space=pltpu.VMEM)
    return pl.pallas_call(
        functools.partial(late_grad_kernel, pieces),
        in_specs=[pl.BlockSpec(memory_space=pltpu.SMEM)] + [vmem] * (pieces + 1),
        out_specs=[vmem, vmem],
        out_shape=[shape, shape],
        compiler_params=pltpu.CompilerParams(vmem_limit_bytes=12 << 20),
        cost_estimate=cost(2 * 2048 * 576 * D, 6 << 20),
        name="late_grads",
    )(me, *grads, hn_row)


def fold_lanes(wide):
    total = wide[:, :128]
    for i in range(1, wide.shape[1] // 128):
        total += wide[:, 128 * i : 128 * (i + 1)]
    return total


def early_kernel(
    me_ref, mine_ref, other_ref, w_ref, norm_ref, win_ref, wdown_ref, wout_ref, gain_ref, part_s
):
    near = mine_ref.shape[1]
    step = pl.program_id(0)
    steps = pl.num_programs(0)
    parts = steps // 2
    rows = D // (steps * near)

    def run(ref):
        for r in range(near):
            piece = ref[0, me_ref[1] ^ r].astype(F32)
            here = slice(r * rows, (r + 1) * rows)
            wide = jnp.concatenate([piece[rows * u : rows * (u + 1)] for u in range(6)], axis=1)
            win_ref[here, :] = wide
            at = pl.multiple_of((step * near + r) * rows, rows)
            part_s[pl.ds(at, rows), :] = fold_lanes(wide * w_ref[here, :].astype(F32))
            wdown_ref[3 * r * rows : 3 * (r + 1) * rows, :] = piece[6 * rows : 9 * rows]
            wout_ref[here, :LANES] = piece[9 * rows : 10 * rows]
            wout_ref[here, LANES:] = piece[10 * rows :]

    ours = (step // parts) == me_ref[2]
    pl.when(ours)(lambda: run(mine_ref))
    pl.when(jnp.logical_not(ours))(lambda: run(other_ref))

    @pl.when(step == steps - 1)
    def _():
        gain_ref[...] = jnp.sum(part_s[...].T, axis=0, keepdims=True) / norm_ref[...]


def assemble_early(me, mine, other, w_in, norm_two):
    parts, near = mine.shape[:2]
    steps = 2 * parts
    rows = D // steps

    def slot(own):
        def index(p, me):
            used = (p // parts == me[2]) == own
            return (jnp.where(used, me[0] ^ (p % parts), 0), 0, 0, 0)

        return pl.BlockSpec((1,) + mine.shape[1:], index)

    return pl.pallas_call(
        early_kernel,
        grid_spec=pltpu.PrefetchScalarGridSpec(
            num_scalar_prefetch=1,
            grid=(steps,),
            in_specs=[
                slot(True),
                slot(False),
                pl.BlockSpec((rows, 2 * FF), lambda p, me: (p, 0)),
                pl.BlockSpec((1, D), lambda p, me: (0, 0)),
            ],
            out_specs=[
                pl.BlockSpec((rows, 2 * FF), lambda p, me: (p, 0)),
                pl.BlockSpec((3 * rows, LANES), lambda p, me: (p % parts, p // parts)),
                pl.BlockSpec((rows, D), lambda p, me: (p, 0)),
                pl.BlockSpec((1, D), lambda p, me: (0, 0)),
            ],
            scratch_shapes=[pltpu.VMEM((D, 128), F32)],
        ),
        out_shape=[
            jax.ShapeDtypeStruct((D, 2 * FF), F32),
            jax.ShapeDtypeStruct((FF, D), F32),
            jax.ShapeDtypeStruct((D, D), F32),
            jax.ShapeDtypeStruct((1, D), F32),
        ],
        compiler_params=pltpu.CompilerParams(vmem_limit_bytes=12 << 20),
        cost_estimate=cost(1 << 20, 24 << 20),
        name="assemble_early",
    )(me, mine, other, w_in, norm_two[None, :])


def late_kernel(me_ref, *refs):
    mine, other = refs[:5], refs[5:10]
    w_ref, norm_ref, out_ref, gain_ref, rows_s, gain_s = refs[10:]
    near = mine[0].shape[0]
    pieces = mine[0].shape[1] // 3
    width = rows_s.shape[1]
    lanes = pl.ds(pl.multiple_of(pl.program_id(0) * 128, 128), 128)
    total = None
    for block in range(3 * pieces):
        row = (block % pieces) * 3 + block // pieces
        for k in range(4):
            for q in range(near):
                which = k if k < 3 else 3 + q // (near // 2)
                place = q if k < 3 else q % (near // 2)
                at = (me_ref[0] ^ k) * HEAD_DIM + (me_ref[1] ^ q) * 8
                for ref, core in ((mine, me_ref[2]), (other, 1 - me_ref[2])):
                    here = pl.ds(pl.multiple_of(at + core * HALF, 8), 8)
                    rows_s[block, here, :] = ref[which][place, row, :, lanes].astype(F32)
        wide = rows_s[block].T
        cols = slice(block * width, (block + 1) * width)
        out_ref[:, cols] = wide
        part = fold_lanes(wide * w_ref[:, cols].astype(F32))
        total = part if total is None else total + part
    gain_s[:, lanes] = jnp.sum(total.T, axis=0, keepdims=True) / norm_ref[...]

    @pl.when(pl.program_id(0) == pl.num_programs(0) - 1)
    def _():
        gain_ref[...] = gain_s[0]


def assemble_late(me, mine, other, w_qkv, norm_one):
    blocks = mine[0].shape[1]
    sums = [pl.BlockSpec(v.shape, lambda b, me: (0, 0, 0, 0)) for v in mine]
    return pl.pallas_call(
        late_kernel,
        grid_spec=pltpu.PrefetchScalarGridSpec(
            num_scalar_prefetch=1,
            grid=(D // 128,),
            in_specs=sums
            + sums
            + [
                pl.BlockSpec((128, 3 * D), lambda b, me: (b, 0)),
                pl.BlockSpec((1, 128), lambda b, me: (0, b)),
            ],
            out_specs=[
                pl.BlockSpec((128, 3 * D), lambda b, me: (b, 0)),
                pl.BlockSpec((D,), lambda b, me: (0,)),
            ],
            scratch_shapes=[
                pltpu.VMEM((blocks, 3 * D // blocks, 128), F32),
                pltpu.VMEM((1, D), F32),
            ],
        ),
        out_shape=[
            jax.ShapeDtypeStruct((D, 3 * D), F32),
            jax.ShapeDtypeStruct((D,), F32),
        ],
        compiler_params=pltpu.CompilerParams(vmem_limit_bytes=60 << 20),
        cost_estimate=cost(1 << 20, 14 << 20),
        name="assemble_late",
    )(me, *mine, *other, w_qkv, norm_one[None, :])


def input_grad_kernel(parts, pieces, me_ref, *refs):
    pair, last = refs[:parts], refs[parts : 2 * parts]
    w_ref, tok_ref, norm_ref, mid_ref, out_ref, proj_s = refs[2 * parts :]
    span = proj_s.shape[1]
    for k in range(parts):
        group = me_ref[0] ^ k
        for j in range(pieces):
            if j < pieces - 1:
                piece = pair[k][...].reshape(pieces - 1, WIDE, span)[j]
            else:
                piece = last[k][...].reshape(WIDE, span)
            for part in range(3):
                at = part * D + (j * parts + group) * HEAD_DIM
                proj_s[pl.ds(pl.multiple_of(at, HEAD_DIM), HEAD_DIM), :] = piece[
                    part * HEAD_DIM : (part + 1) * HEAD_DIM
                ]
    upstream = dot(w_ref[...], proj_s[...]).T * norm_ref[...]
    values = tok_ref[...].astype(F32)
    centered = values - jnp.mean(values, axis=-1, keepdims=True)
    scale = lax.rsqrt(jnp.mean(centered * centered, axis=-1, keepdims=True) + EPSILON)
    unit = centered * scale
    flat = jnp.mean(upstream, axis=-1, keepdims=True)
    along = jnp.mean(upstream * unit, axis=-1, keepdims=True)
    out_ref[...] = mid_ref[...] + (upstream - flat - unit * along) * scale


def input_grad(me, pair, last, w_qkv, tokens, norm_one, grad_middle):
    parts = len(pair)
    span = tokens.shape[0]
    vmem = pl.BlockSpec(memory_space=pltpu.VMEM)
    return pl.pallas_call(
        functools.partial(input_grad_kernel, parts, 3),
        in_specs=[pl.BlockSpec(memory_space=pltpu.SMEM)] + [vmem] * (2 * parts + 4),
        out_specs=vmem,
        out_shape=jax.ShapeDtypeStruct((span, D), F32),
        scratch_shapes=[pltpu.VMEM((3 * D, span), BF16)],
        compiler_params=pltpu.CompilerParams(vmem_limit_bytes=20 << 20),
        cost_estimate=cost(2 * span * 3 * D * D, 10 << 20),
        name="input_grad",
    )(me, *pair, *last, w_qkv, tokens, norm_one[None, :], grad_middle)


def swap(values, axis, k):
    size = lax.axis_size(axis)
    return lax.ppermute(values, axis, [(i, i ^ k) for i in range(size)])


def add(*terms):
    total = terms[0].astype(F32)
    for term in terms[1:]:
        total += term.astype(F32)
    return total.astype(BF16)


def scatter_near(slots):
    return add(slots[0], *[swap(slots[k], "near", k) for k in range(1, len(slots))])


def gather_near(values):
    return jnp.stack([values] + [swap(values, "near", k) for k in range(1, lax.axis_size("near"))])


def tie(*values):
    return lax.optimization_barrier(values)


def on_device(tokens, doc_start, cotangent, norm_one, w_qkv, w_out, norm_two, w_in, w_down):
    parts = lax.axis_size("seq")
    near = lax.axis_size("near")
    far = lax.axis_size("far")
    span = tokens.shape[1]
    total = span * parts
    pieces = HEADS // parts
    bq = min(512, span)
    me_seq = lax.axis_index("seq").astype(jnp.int32)
    me = jnp.stack([lax.axis_index(a).astype(jnp.int32) for a in ("seq", "near", "core")])
    first_token = me_seq * span
    starts = doc_start[0]
    docs = doc_start

    frequency = ROTARY_BASE ** (-(jnp.arange(HALF, dtype=F32) * 2.0 / HEAD_DIM))
    offset = (jnp.arange(total, dtype=jnp.int32) - starts).astype(F32)
    angles = frequency[:, None] * offset[None, :]
    cosine, sine = jnp.cos(angles), jnp.sin(angles)
    own_cosine = lax.dynamic_slice_in_dim(cosine, first_token, span, axis=1)
    own_sine = lax.dynamic_slice_in_dim(sine, first_token, span, axis=1)

    def sum_far(values):
        return lax.psum(values, "far") if far > 1 else values

    hn = first_norm(tokens[0], norm_one)
    qkv = []
    for j in range(pieces):
        sent = project(me, hn, w_qkv, own_cosine, own_sine, j, parts)
        qkv.append([sent] + [swap(sent[k], "seq", k) for k in range(1, parts)])
    contexts, lses = [], []
    for j in range(pieces):
        if j == pieces - 1:
            hn_late, qkv[j] = tie(hn, qkv[j])
            hn_near = [swap(hn_late, "seq", 1), swap(hn_late, "seq", 2)]
        context, lse = attend_forward(me, qkv[j], docs, bq)
        contexts.append(context)
        lses.append(lse)
    arrived = [jnp.stack([c[k] for c in contexts]) for k in range(parts)]
    arrived[1:] = [swap(arrived[k], "seq", k) for k in range(1, parts)]
    arrived, hn_near = tie(arrived, hn_near)
    hn_far = [swap(hn_near[1][: span // 2], "seq", 1), swap(hn_near[0][span // 2 :], "seq", 2)]
    outs = middle_part(me, arrived, tokens[0], cotangent[0], w_out, norm_two, w_in, w_down)
    outs, hn_far = tie(outs, hn_far)
    context_t, normed_two, grad_gate_up, inner, grad_mid_low, grad_middle, result = outs[:7]
    hn_row = jnp.stack([hn, hn_near[0], hn_near[1], jnp.concatenate(hn_far)])
    upstream = [outs[7]] + [swap(outs[7 + k], "seq", k) for k in range(1, parts)]
    keep, give = early_grads(
        me, normed_two, grad_gate_up, inner, cotangent[0], context_t, grad_mid_low, parts, near
    )
    taken = swap(give, "core", 1)
    half = near // 2
    at = [2 * half, 4 * half, 5 * half, 6 * half, 7 * half, 8 * half]
    send_one = add(keep[: at[0]], taken[: at[0]])
    send_two = add(keep[at[0] : at[1]], taken[at[0] : at[1]])
    early = add(keep[at[1] :], taken[at[1] :])
    a_own, a_two, b_own, b_one = (early[i * half : (i + 1) * half] for i in range(4))
    send_one, send_two, early, upstream[1] = tie(send_one, send_two, early, upstream[1])

    def backward(j, upstream):
        return attend_backward(
            me, qkv[j], docs, upstream, j, contexts[j], lses[j], cosine, sine, bq,
            True,
        )

    from_one, from_two = swap(send_one, "seq", 1), swap(send_two, "seq", 2)
    grads = [backward(0, upstream)]
    grads[0], upstream, from_one, from_two = tie(grads[0], upstream, from_one, from_two)
    by_two = swap(add(a_two, from_one[half:]), "seq", 2)
    by_one = swap(add(b_one, from_two[half:]), "seq", 1)
    grads.append(backward(1, upstream))
    grads, upstream, by_two, by_one = tie(grads, upstream, by_two, by_one)
    kept, given = late_grads(me, grads, hn_row, near)
    own = jnp.stack(grads, axis=1)
    pair = [own[0]] + [swap(own[k], "seq", k) for k in range(1, parts)]
    early = [add(a_own[i], from_one[i], by_two[i]) for i in range(half)]
    early += [add(b_own[i], from_two[i], by_one[i]) for i in range(half)]
    early = scatter_near(early)
    grads.append(backward(2, upstream))

    grads, early, pair[1], pair[2] = tie(grads, early, pair[1], pair[2])
    early = sum_far(early)
    slots = [early] + [swap(early, "near", k) for k in range(1, near)]
    last = [grads[2][0]] + [swap(grads[2][k], "seq", k) for k in range(1, parts)]
    last, slots, grads[2], pair, kept, given = tie(last, slots, grads[2], pair, kept, given)
    early = jnp.stack(slots)
    one, two = swap(early, "seq", 1), swap(early, "seq", 2)
    kept_last, given_last = late_grads(me, grads[2:], hn_row, near)
    kept = jnp.concatenate([kept, kept_last], axis=1)
    given = jnp.concatenate([given, given_last], axis=1)
    late = add(kept, swap(given, "core", 1))
    late = sum_far(scatter_near(late))
    grad_input = input_grad(me, pair, last, w_qkv, tokens[0], norm_one, grad_middle)
    one, two, late, grad_input = tie(one, two, late, grad_input)
    far_one, far_two = swap(two[: near // 2], "seq", 1), swap(one[near // 2 :], "seq", 2)
    late = gather_near(late)
    far_one, far_two, late = tie(far_one, far_two, late)
    early = jnp.stack([early, one, two, jnp.concatenate([far_one, far_two])])
    early_other = swap(early, "core", 1)
    one, two = swap(late, "seq", 1), swap(late, "seq", 2)
    one, two, early_other = tie(one, two, early_other)
    far = [swap(two[: near // 2], "seq", 1), swap(one[near // 2 :], "seq", 2)]
    mine = [late, one, two]
    other = [swap(v, "core", 1) for v in mine]
    sum_w_in, sum_w_down, sum_w_out, sum_norm_two = assemble_early(
        me, early, early_other, w_in, norm_two
    )
    sum_w_in, far, other = tie(sum_w_in, far, other)
    mine += far
    other += [swap(v, "core", 1) for v in far]
    sum_w_qkv, sum_norm_one = assemble_late(me, mine, other, w_qkv, norm_one)
    return (
        result[None],
        grad_input[None],
        sum_norm_one,
        sum_w_qkv,
        sum_w_out,
        sum_norm_two[0],
        sum_w_in,
        sum_w_down,
    )


def solution(mesh):
    parts = mesh.shape["seq"]
    near = min(4, mesh.shape["dp"] // 2)
    split = Mesh(mesh.devices.reshape(parts, -1, near, 2), ("seq", "far", "near", "core"))
    rows = ("far", "near", "core")
    tokens_at = P(rows, "seq", None)
    return jax.shard_map(
        on_device,
        mesh=split,
        in_specs=(tokens_at, P(rows, None), tokens_at, P(), P(), P(), P(), P(), P()),
        out_specs=(tokens_at, tokens_at, P(), P(), P(), P(), P(), P()),
        check_vma=False,
    )
```
